128 devices in a mesh: section: 8 (over z, core), tensor: 16 (over x, y).
Axes of the slice: x: 4, y: 4, z: 4, core: 2. Of those that a mesh axis runs over, the one named last changes fastest.
Arguments:
- dy_top: bfloat16 [2, 64, 8192], replicated, may hold values from -6 to 6
- loss_mask: int32 [2, 64], replicated, may hold values 0 or 1
- counts: int32 [2], replicated, may hold values from 8 to 64, as said below
- layer_in: bfloat16 [8, 2, 64, 8192], P('section'), may hold values from -60 to 60
- conv_in: bfloat16 [8, 2, 64, 10240], P('section', None, None, 'tensor'), may hold values from -6 to 6
- norm_gain: float32 [8, 8192], P('section'), may hold values from 0.3 to 3
- conv_weight: float32 [8, 4, 10240], P('section', None, 'tensor'), may hold values from -2.5 to 2.5
- in_proj: bfloat16 [8, 8192, 10240], P('section', None, 'tensor'), may hold values from -1 to 1
- out_proj: bfloat16 [8, 10240, 8192], P('section', 'tensor'), may hold values from -0.0625 to 0.0625
Outputs:
- section_grads: bfloat16 [8, 2, 64, 8192], P('section')
- gain_grads: float32 [8, 8192], P('section')
- conv_grads: float32 [8, 4, 10240], P('section', None, 'tensor')
The draws below stay inside these ranges and needn't reach their ends.
Inputs may be any that keep to these rules, and one draw needn't show every extreme that they name: `counts`: one micro-batch holds all 64 positions; the other holds 8 to 32 tokens.
All inputs are finite; a program needn't handle non-finite values.
Results may differ from the reference program's by a relative error of at most 0.033.
Values may be sent and summed in bfloat16 or wider, within the bound.
A program may use at most 128 MiB of HBM per device.

```python
import math
import jax
import jax.numpy as jnp
from jax import lax

D = 8192
CH = 10240
KW = 4
MB = 2
SEQ = 64
N_SECTION = 8
N_TENSOR = 16


def draw_counts(key, part):
    key_short, key_full = jax.random.split(jax.random.fold_in(key, 11))
    short_len = jax.random.randint(key_short, (), SEQ // 8, SEQ // 2 + 1)
    full_slot = jax.random.randint(key_full, (), 0, MB)
    return jnp.where(jnp.arange(MB) == full_slot, SEQ, short_len).astype(jnp.int32)


def draw_layer_in(key, part):
    key_rows, key_cols, key_base, key_common = jax.random.split(jax.random.fold_in(key, 23), 4)
    row_scale = jnp.exp(jax.random.uniform(key_rows, (N_SECTION, MB, SEQ, 1), minval=math.log(0.1), maxval=0.0))
    col_scale = jnp.exp(jax.random.uniform(key_cols, (N_SECTION, 1, 1, D), minval=0.0, maxval=math.log(10.0)))
    base_vals = jnp.clip(jax.random.normal(key_base, (N_SECTION, MB, SEQ, D)), -4.0, 4.0)
    base_vals = base_vals + jnp.clip(jax.random.normal(key_common, (N_SECTION, MB, SEQ, 1)), -2.0, 2.0)
    return (base_vals * row_scale * col_scale).astype(jnp.bfloat16)


def draw_in_proj(key, part):
    key_base, key_offset = jax.random.split(jax.random.fold_in(key, 37))
    weight_scale = 1.0 / math.sqrt(D)
    base_vals = jnp.clip(jax.random.normal(key_base, (N_SECTION, D, CH)), -4.0, 4.0)
    offset_vals = 0.7 * jnp.clip(jax.random.normal(key_offset, (N_SECTION, 1, CH)), -3.0, 3.0)
    return ((base_vals + offset_vals) * weight_scale).astype(jnp.bfloat16)


def place_ends(entries, key, least, high):
    shape = entries.shape
    place = [jax.random.randint(jax.random.fold_in(key, axis), (), 0, shape[axis]) for axis in range(len(shape))]
    entries = entries.at[tuple(place)].set(least)
    longest = shape.index(max(shape))
    place[longest] = (place[longest] + 1) % shape[longest]
    return entries.at[tuple(place)].set(high)


def block_scale(own_key, shape, cuts, smallest, largest):
    def one(dim, shards_of):
        heights = jax.random.uniform(jax.random.fold_in(jax.random.fold_in(own_key, 6), dim), (shards_of,), jnp.float32, smallest / len(cuts), largest / len(cuts))
        return jnp.repeat(jnp.exp(heights), shape[dim] // shards_of).reshape((-1,) + (1,) * (len(shape) - dim - 1))

    level = one(*cuts[0])
    for cut in cuts[1:]:
        level = level * one(*cut)
    return level


def gaussian(key, extent, width, most, cuts=(), held_as=jnp.bfloat16):
    result = jax.random.normal(key, extent, jnp.float32) * width
    if len(cuts) > 0:
        result = block_scale(key, extent, cuts, -0.22, 0.18) * result
    return jnp.clip(result, min=-most, max=most).astype(held_as)


def setup_inputs(seed: int = 0) -> dict:
    splits = jax.random.split(jax.random.key(seed), 10)
    dy_top = gaussian(splits[0], (MB, SEQ, D), 1.0, 6.0)
    loss_mask = place_ends((jax.random.randint(splits[1], (MB, SEQ), 0, 4) < 3).astype(jnp.int32), jax.random.fold_in(splits[1], 1), 0, 1)
    counts = draw_counts(jax.random.fold_in(splits[9], 71), 0)
    layer_in = draw_layer_in(jax.random.fold_in(splits[9], 71), 0)
    conv_in = gaussian(splits[4], (N_SECTION, MB, SEQ, CH), 1.0, 6.0, ((0, 8), (3, 16)))
    norm_gain = jnp.clip(jnp.exp(math.log(3.0) - 2.3025851 * jax.random.uniform(splits[5], (N_SECTION, D), jnp.float32) ** block_scale(splits[5], (N_SECTION, D), ((0, 8),), -0.2, 0.2)), 0.3, 3.0)
    conv_weight = gaussian(splits[6], (N_SECTION, KW, CH), 0.5, 2.5, ((0, 8), (2, 16)), jnp.float32)
    in_proj = draw_in_proj(jax.random.fold_in(splits[9], 71), 0)
    out_proj = gaussian(splits[8], (N_SECTION, CH, D), CH ** -0.5, 0.0625, ((0, 8), (1, 16)))
    return {"dy_top": dy_top, "loss_mask": loss_mask, "counts": counts, "layer_in": layer_in, "conv_in": conv_in, "norm_gain": norm_gain, "conv_weight": conv_weight, "in_proj": in_proj, "out_proj": out_proj}


EPSILON = 1e-05

def conv_backward(weights, values, d_act):
    kernel_width = weights.shape[0]
    length = values.shape[0]
    padded = jnp.pad(values, ((kernel_width - 1, 0), (0, 0)))
    pre_act = jnp.zeros_like(values)
    for lag_idx in range(kernel_width):
        pre_act = pre_act + weights[lag_idx] * padded[kernel_width - 1 - lag_idx:kernel_width - 1 - lag_idx + length]
    gate_sig = jax.nn.sigmoid(pre_act)
    d_pre = d_act * gate_sig * (1.0 + pre_act * (1.0 - gate_sig))
    padded_back = jnp.pad(d_pre, ((0, kernel_width - 1), (0, 0)))
    d_vals = jnp.zeros_like(d_pre)
    for lag_idx in range(kernel_width):
        d_vals = d_vals + weights[lag_idx] * padded_back[lag_idx:lag_idx + length]
    lag_grads = jnp.stack([lax.optimization_barrier(jnp.sum(d_pre * padded[kernel_width - 1 - lag_idx:kernel_width - 1 - lag_idx + length], axis=0)) for lag_idx in range(kernel_width)])
    return (d_vals.astype(jnp.bfloat16), lag_grads)

def norm_backward(d_norm, saved_now, upstream, gain_vec):
    values = saved_now.astype(jnp.float32)
    inv_rms = lax.rsqrt(lax.optimization_barrier(jnp.mean(values * values, axis=-1, keepdims=True)) + EPSILON)
    normed = values * inv_rms
    d_hat = d_norm * gain_vec
    d_in = inv_rms * (d_hat - normed * lax.optimization_barrier(jnp.mean(d_hat * normed, axis=-1, keepdims=True)))
    return (upstream.astype(jnp.float32) + d_in, lax.optimization_barrier(jnp.sum(d_norm * normed, axis=0)))

def reference(dy_top, loss_mask, counts, layer_in, conv_in, norm_gain, conv_weight, in_proj, out_proj):
    positions = jnp.arange(SEQ, dtype=jnp.int32)
    keep_mask = (loss_mask == 1) & (positions[None, :] < counts[:, None])
    grad_now = jnp.where(keep_mask[:, :, None], dy_top, jnp.zeros_like(dy_top))
    block_size = CH // N_TENSOR
    section_list = []
    gain_list = []
    conv_list = []
    for section_idx in reversed(range(N_SECTION)):
        d_act = jnp.einsum('msd,cd->msc', grad_now.astype(jnp.float32), out_proj[section_idx].astype(jnp.float32))
        d_vals, lag_grads = jax.vmap(conv_backward, in_axes=(None, 0, 0))(conv_weight[section_idx], conv_in[section_idx].astype(jnp.float32), d_act)
        conv_grad = lax.optimization_barrier(jnp.sum(lag_grads, axis=0))
        d_norm = jnp.zeros((MB, SEQ, D), jnp.float32)
        for part_idx in range(N_TENSOR):
            first = part_idx * block_size
            term = jnp.einsum('msc,dc->msd', d_vals[:, :, first:first + block_size].astype(jnp.float32), in_proj[section_idx][:, first:first + block_size].astype(jnp.float32))
            rounded = lax.optimization_barrier(term.astype(jnp.bfloat16))
            d_norm = d_norm + rounded.astype(jnp.float32)
        grad_next, gain_grad = norm_backward(d_norm.reshape(MB * SEQ, D), layer_in[section_idx].reshape(MB * SEQ, D), grad_now.reshape(MB * SEQ, D), norm_gain[section_idx])
        grad_now = grad_next.astype(jnp.bfloat16).reshape(MB, SEQ, D)
        section_list.append(grad_now)
        gain_list.append(gain_grad)
        conv_list.append(conv_grad)
    section_list = section_list[::-1]
    gain_list = gain_list[::-1]
    conv_list = conv_list[::-1]
    return (jnp.stack(section_list), jnp.stack(gain_list), jnp.stack(conv_list))
```

```python
import jax
import jax.numpy as jnp
from jax import lax
from jax.sharding import PartitionSpec as P

EPSILON = 1e-05
CHUNKS_PER_BATCH = 2


def sent_to_all(x, axis):
    copies = jnp.broadcast_to(x, (lax.axis_size(axis), *x.shape))
    return lax.all_to_all(copies, axis, split_axis=0, concat_axis=0, tiled=True)


def summed_on_arrival(x, axis):
    devices = lax.axis_size(axis)
    parts = x.reshape(devices, x.shape[0] // devices, x.shape[1])
    arrived = lax.all_to_all(parts, axis, split_axis=0, concat_axis=0, tiled=True)
    return arrived.astype(jnp.float32).sum(axis=0)


def of_everyone(x, axis):
    return sent_to_all(x, axis).astype(jnp.float32).sum(axis=0)


def conv_block(weights, ext_vals, tail_rows, d_act):
    kernel_width = weights.shape[0]
    length = d_act.shape[0]
    pre_act = jnp.zeros_like(d_act)
    for lag_idx in range(kernel_width):
        start = kernel_width - 1 - lag_idx
        pre_act = pre_act + weights[lag_idx] * ext_vals[start : start + length]
    gate_sig = jax.nn.sigmoid(pre_act)
    d_pre = d_act * gate_sig * (1.0 + pre_act * (1.0 - gate_sig))
    padded_back = jnp.concatenate([d_pre, tail_rows], axis=0)
    d_vals = jnp.zeros_like(d_pre)
    for lag_idx in range(kernel_width):
        d_vals = d_vals + weights[lag_idx] * padded_back[lag_idx : lag_idx + length]
    lag_grads = jnp.stack(
        [
            jnp.sum(
                d_pre * ext_vals[kernel_width - 1 - lag_idx : kernel_width - 1 - lag_idx + length],
                axis=0,
            )
            for lag_idx in range(kernel_width)
        ]
    )
    return (d_vals.astype(jnp.bfloat16), lag_grads, d_pre[: kernel_width - 1])


def norm_backward(d_norm, saved_now, upstream, gain_vec):
    values = saved_now.astype(jnp.float32)
    inv_rms = lax.rsqrt(jnp.mean(values * values, axis=-1, keepdims=True) + EPSILON)
    normed = values * inv_rms
    d_hat = d_norm * gain_vec
    d_in = inv_rms * (d_hat - normed * jnp.mean(d_hat * normed, axis=-1, keepdims=True))
    return (upstream.astype(jnp.float32) + d_in, jnp.sum(d_norm * normed, axis=0))


def local(dy_top, loss_mask, counts, layer_in, conv_in, norm_gain, conv_weight, in_proj, out_proj):
    sections = lax.axis_size("section")
    tensors = lax.axis_size("tensor")
    section_idx = lax.axis_index("section")
    tensor_idx = lax.axis_index("tensor")
    batches, seq_len, model_width = dy_top.shape
    saved_rows = layer_in[0]
    gain_vec = norm_gain[0]
    weights = conv_weight[0]
    kernel_width = weights.shape[0]
    local_channels = weights.shape[1]
    w_in = in_proj[0]
    w_out = out_proj[0]
    conv_padded = jnp.pad(conv_in[0], ((0, 0), (kernel_width - 1, 0), (0, 0)))
    positions = jnp.arange(seq_len, dtype=jnp.int32)
    keep_mask = (loss_mask == 1) & (positions[None, :] < counts[:, None])
    top_grads = jnp.where(keep_mask[:, :, None], dy_top, jnp.zeros_like(dy_top))
    is_last = section_idx == sections - 1
    contract = (((1,), (1,)), ((), ()))

    halves = CHUNKS_PER_BATCH
    chunk_len = seq_len // halves
    local_rows = chunk_len // tensors
    order = [(b, h) for b in range(batches) for h in reversed(range(halves))]
    block_slot = jnp.array([b for b, _ in order], jnp.int32)
    block_half = jnp.array([h for _, h in order], jnp.int32)
    block_join = jnp.array([h < halves - 1 for _, h in order], jnp.bool_)
    n_chunks = len(order)
    total_steps = sections + n_chunks - 1

    def pick_block(step_idx):
        block_raw = step_idx - (sections - 1 - section_idx)
        active = (block_raw >= 0) & (block_raw < n_chunks)
        block_now = jnp.clip(block_raw, 0, n_chunks - 1)
        return (block_slot[block_now], block_half[block_now], block_join[block_now], active)

    def rows_of(array, batch_slot, first_row, row_count):
        return lax.dynamic_slice(array, (batch_slot, first_row, 0), (1, row_count, array.shape[2]))[0]

    tail_init = jnp.zeros((kernel_width - 1, local_channels), jnp.float32)

    def step_rows(step_idx, loop_state):
        incoming, results, gain_acc, conv_acc, tail_carry = loop_state
        batch_slot, half_now, join_now, active = pick_block(step_idx)
        row_start = half_now * chunk_len
        own_start = row_start + tensor_idx * local_rows
        upstream = jnp.where(is_last, rows_of(top_grads, batch_slot, own_start, local_rows), incoming)
        gathered = sent_to_all(incoming, "tensor").reshape(chunk_len, model_width)
        full_chunk = jnp.where(is_last, rows_of(top_grads, batch_slot, row_start, chunk_len), gathered)
        d_act = lax.dot_general(full_chunk, w_out, contract, preferred_element_type=jnp.float32)
        d_act = lax.optimization_barrier(d_act)
        ext_vals = lax.dynamic_slice(
            conv_padded, (batch_slot, row_start, 0), (1, chunk_len + kernel_width - 1, local_channels)
        )[0].astype(jnp.float32)
        tail_rows = jnp.where(join_now, tail_carry, 0.0)
        d_vals, conv_part, new_tail = conv_block(weights, ext_vals, tail_rows, d_act)
        partial = lax.dot_general(d_vals, w_in, contract, preferred_element_type=jnp.float32)
        d_norm = summed_on_arrival(partial.astype(jnp.bfloat16), "tensor")
        saved_now = rows_of(saved_rows, batch_slot, own_start, local_rows)
        grad_in, gain_part = norm_backward(d_norm, saved_now, upstream, gain_vec)
        grad_out = grad_in.astype(jnp.bfloat16)
        previous = lax.dynamic_slice(results, (batch_slot, half_now, 0, 0), (1, 1, local_rows, model_width))
        updated = jnp.where(active, grad_out[None, None], previous)
        results = lax.dynamic_update_slice(results, updated, (batch_slot, half_now, 0, 0))
        gain_acc = gain_acc + jnp.where(active, gain_part, 0.0)
        conv_acc = conv_acc + jnp.where(active, conv_part, 0.0)
        tail_carry = jnp.where(active, new_tail, tail_carry)
        incoming = lax.ppermute(grad_out, "section", [(i, i - 1) for i in range(1, sections)])
        return (incoming, results, gain_acc, conv_acc, tail_carry)

    initial = (
        jnp.zeros((local_rows, model_width), jnp.bfloat16),
        jnp.zeros((batches, halves, local_rows, model_width), jnp.bfloat16),
        jnp.zeros(gain_vec.shape, jnp.float32),
        jnp.zeros(weights.shape, jnp.float32),
        tail_init,
    )
    last_state = lax.fori_loop(0, total_steps, step_rows, initial)
    gathered = sent_to_all(last_state[1], "tensor")
    results = jnp.transpose(gathered, (1, 2, 0, 3, 4)).reshape(batches, seq_len, model_width)
    conv_acc = last_state[3]
    gain_total = of_everyone(last_state[2].astype(jnp.bfloat16), "tensor")
    return (results[None], gain_total[None], conv_acc[None])


def solution(mesh):
    placed = (
        P(),
        P(),
        P(),
        P("section", None, None, None),
        P("section", None, None, "tensor"),
        P("section", None),
        P("section", None, "tensor"),
        P("section", None, "tensor"),
        P("section", "tensor", None),
    )
    return jax.shard_map(
        local,
        mesh=mesh,
        in_specs=placed,
        out_specs=(
            P("section", None, None, None),
            P("section", None),
            P("section", None, "tensor"),
        ),
        check_vma=False,
    )
```

```python
import functools

import jax
import jax.numpy as jnp
from jax import lax
from jax.experimental import pallas as pl
from jax.experimental.pallas import tpu as pltpu
from jax.sharding import PartitionSpec as P

EPSILON = 1e-05
MESH = pl.DeviceIdType.MESH
CHUNKS_PER_BATCH = 2


def sent_to_all(x, axis):
    copies = jnp.broadcast_to(x, (lax.axis_size(axis), *x.shape))
    return lax.all_to_all(copies, axis, split_axis=0, concat_axis=0, tiled=True)


def scatter_sum_kernel(n, width, x_ref, s_ref, out_ref, sum_ref, recv, srecv, send_sem, recv_sem, ssend_sem, srecv_sem):
    me = lax.axis_index("tensor")
    sec = lax.axis_index("section")
    barrier = pltpu.get_barrier_semaphore()
    for k in range(1, n):
        pl.semaphore_signal(barrier, inc=1, device_id=(sec, lax.rem(me + k, n)), device_id_type=MESH)
    pl.semaphore_wait(barrier, n - 1)
    copies = []
    for k in range(1, n):
        peer = lax.rem(me + k, n)
        cols = pl.ds(pl.multiple_of(peer * width, 128), width)
        block = pltpu.make_async_remote_copy(
            src_ref=x_ref.at[:, cols],
            dst_ref=recv.at[me],
            send_sem=send_sem.at[k],
            recv_sem=recv_sem.at[k],
            device_id=(sec, peer),
            device_id_type=MESH,
        )
        block.start()
        stat = pltpu.make_async_remote_copy(
            src_ref=s_ref,
            dst_ref=srecv.at[me],
            send_sem=ssend_sem.at[k],
            recv_sem=srecv_sem.at[k],
            device_id=(sec, peer),
            device_id_type=MESH,
        )
        stat.start()
        copies.append((block, stat))
    for block, stat in copies:
        block.wait()
        stat.wait()
    mine = pl.ds(pl.multiple_of(me * width, 128), width)
    total = x_ref[:, mine].astype(jnp.float32)
    stat_total = s_ref[...]
    for k in range(1, n):
        src = lax.rem(me + n - k, n)
        total = total + recv[src].astype(jnp.float32)
        stat_total = stat_total + srecv[src]
    out_ref[...] = total
    sum_ref[...] = stat_total


def scatter_sum(x, stats, n, width):
    rows = x.shape[0]
    return pl.pallas_call(
        functools.partial(scatter_sum_kernel, n, width),
        out_shape=(
            jax.ShapeDtypeStruct((rows, width), jnp.float32),
            jax.ShapeDtypeStruct(stats.shape, jnp.float32),
        ),
        in_specs=[pl.BlockSpec(memory_space=pltpu.VMEM)] * 2,
        out_specs=(pl.BlockSpec(memory_space=pltpu.VMEM), pl.BlockSpec(memory_space=pltpu.VMEM)),
        scratch_shapes=[
            pltpu.VMEM((n, rows, width), x.dtype),
            pltpu.VMEM((n, *stats.shape), jnp.float32),
            pltpu.SemaphoreType.DMA((n,)),
            pltpu.SemaphoreType.DMA((n,)),
            pltpu.SemaphoreType.DMA((n,)),
            pltpu.SemaphoreType.DMA((n,)),
        ],
        compiler_params=pltpu.CompilerParams(collective_id=0, has_side_effects=True),
    )(x, stats)


def handed_down_kernel(n, n_sec, width, g_ref, out_ref, recv, send_sem, recv_sem):
    me = lax.axis_index("tensor")
    sec = lax.axis_index("section")
    barrier = pltpu.get_barrier_semaphore()
    mine = pl.ds(pl.multiple_of(me * width, 128), width)

    @pl.when(sec < n_sec - 1)
    def _():
        for t in range(n):
            pl.semaphore_signal(barrier, inc=1, device_id=(sec + 1, t), device_id_type=MESH)

    @pl.when(sec > 0)
    def _():
        pl.semaphore_wait(barrier, n)
        copies = []
        for t in range(n):
            copy = pltpu.make_async_remote_copy(
                src_ref=g_ref,
                dst_ref=recv.at[:, mine],
                send_sem=send_sem.at[t],
                recv_sem=recv_sem.at[me],
                device_id=(sec - 1, t),
                device_id_type=MESH,
            )
            copy.start()
            copies.append(copy)
        for copy in copies:
            copy.wait_send()

    @pl.when(sec < n_sec - 1)
    def _():
        for src in range(n):
            pltpu.make_async_remote_copy(
                src_ref=g_ref,
                dst_ref=recv.at[:, pl.ds(src * width, width)],
                send_sem=send_sem.at[src],
                recv_sem=recv_sem.at[src],
                device_id=(sec + 1, src),
                device_id_type=MESH,
            ).wait_recv()
        out_ref[...] = recv[...]

    @pl.when(sec == n_sec - 1)
    def _():
        out_ref[...] = jnp.zeros_like(out_ref)


def handed_down(g_block, n, n_sec, width):
    rows = g_block.shape[0]
    return pl.pallas_call(
        functools.partial(handed_down_kernel, n, n_sec, width),
        out_shape=jax.ShapeDtypeStruct((rows, n * width), g_block.dtype),
        in_specs=[pl.BlockSpec(memory_space=pltpu.VMEM)],
        out_specs=pl.BlockSpec(memory_space=pltpu.VMEM),
        scratch_shapes=[
            pltpu.VMEM((rows, n * width), g_block.dtype),
            pltpu.SemaphoreType.DMA((n,)),
            pltpu.SemaphoreType.DMA((n,)),
        ],
        compiler_params=pltpu.CompilerParams(collective_id=1, has_side_effects=True),
    )(g_block)


def conv_block(weights, ext_vals, tail_rows, d_act):
    kernel_width = weights.shape[0]
    length = d_act.shape[0]
    pre_act = jnp.zeros_like(d_act)
    for lag_idx in range(kernel_width):
        start = kernel_width - 1 - lag_idx
        pre_act = pre_act + weights[lag_idx] * ext_vals[start : start + length]
    gate_sig = jax.nn.sigmoid(pre_act)
    d_pre = d_act * gate_sig * (1.0 + pre_act * (1.0 - gate_sig))
    padded_back = jnp.concatenate([d_pre, tail_rows], axis=0)
    d_vals = jnp.zeros_like(d_pre)
    for lag_idx in range(kernel_width):
        d_vals = d_vals + weights[lag_idx] * padded_back[lag_idx : lag_idx + length]
    lag_grads = jnp.stack(
        [
            jnp.sum(
                d_pre * ext_vals[kernel_width - 1 - lag_idx : kernel_width - 1 - lag_idx + length],
                axis=0,
            )
            for lag_idx in range(kernel_width)
        ]
    )
    return (d_vals.astype(jnp.bfloat16), lag_grads, d_pre[: kernel_width - 1])


def local(dy_top, loss_mask, counts, layer_in, conv_in, norm_gain, conv_weight, in_proj, out_proj):
    sections = lax.axis_size("section")
    tensors = lax.axis_size("tensor")
    section_idx = lax.axis_index("section")
    tensor_idx = lax.axis_index("tensor")
    batches, seq_len, model_width = dy_top.shape
    width = model_width // tensors
    gain_vec = norm_gain[0]
    weights = conv_weight[0]
    kernel_width = weights.shape[0]
    local_channels = weights.shape[1]
    w_in = in_proj[0]
    w_out = out_proj[0]
    conv_padded = jnp.pad(conv_in[0], ((0, 0), (kernel_width - 1, 0), (0, 0)))
    positions = jnp.arange(seq_len, dtype=jnp.int32)
    keep_mask = (loss_mask == 1) & (positions[None, :] < counts[:, None])
    top_grads = jnp.where(keep_mask[:, :, None], dy_top, jnp.zeros_like(dy_top))
    is_last = section_idx == sections - 1
    contract = (((1,), (1,)), ((), ()))

    values = layer_in[0].astype(jnp.float32)
    inv_rms_all = lax.rsqrt(jnp.mean(values * values, axis=-1, keepdims=True) + EPSILON)
    normed_all = values * inv_rms_all
    gain_own = lax.dynamic_slice(gain_vec, (tensor_idx * width,), (width,))

    halves = CHUNKS_PER_BATCH
    chunk_len = seq_len // halves
    order = [(b, h) for b in range(batches) for h in reversed(range(halves))]
    block_slot = jnp.array([b for b, _ in order], jnp.int32)
    block_half = jnp.array([h for _, h in order], jnp.int32)
    block_join = jnp.array([h < halves - 1 for _, h in order], jnp.bool_)
    n_chunks = len(order)
    total_steps = sections + n_chunks - 1

    def pick_block(step_idx):
        block_raw = step_idx - (sections - 1 - section_idx)
        active = (block_raw >= 0) & (block_raw < n_chunks)
        block_now = jnp.clip(block_raw, 0, n_chunks - 1)
        return (block_slot[block_now], block_half[block_now], block_join[block_now], active)

    def rows_of(array, batch_slot, first_row, row_count):
        return lax.dynamic_slice(array, (batch_slot, first_row, 0), (1, row_count, array.shape[2]))[0]

    tail_init = jnp.zeros((kernel_width - 1, local_channels), jnp.float32)

    def step_rows(step_idx, loop_state):
        incoming, results, gain_acc, conv_acc, tail_carry = loop_state
        batch_slot, half_now, join_now, active = pick_block(step_idx)
        row_start = half_now * chunk_len
        full_chunk = jnp.where(is_last, rows_of(top_grads, batch_slot, row_start, chunk_len), incoming)
        d_act = lax.dot_general(full_chunk, w_out, contract, preferred_element_type=jnp.float32)
        d_act = lax.optimization_barrier(d_act)
        ext_vals = lax.dynamic_slice(
            conv_padded, (batch_slot, row_start, 0), (1, chunk_len + kernel_width - 1, local_channels)
        )[0].astype(jnp.float32)
        tail_rows = jnp.where(join_now, tail_carry, 0.0)
        d_vals, conv_part, new_tail = conv_block(weights, ext_vals, tail_rows, d_act)
        partial = lax.dot_general(d_vals, w_in, contract, preferred_element_type=jnp.float32).astype(jnp.bfloat16)
        normed = rows_of(normed_all, batch_slot, row_start, chunk_len)
        inv_rms = rows_of(inv_rms_all, batch_slot, row_start, chunk_len)
        row_part = jnp.sum(partial.astype(jnp.float32) * gain_vec * normed, axis=-1)
        stats = jnp.zeros((8, 128), jnp.float32).at[0, :chunk_len].set(row_part)
        d_norm, stats_total = scatter_sum(partial, stats, tensors, width)
        row_mean = stats_total[0, :chunk_len][:, None] / model_width
        normed_own = lax.dynamic_slice(normed, (0, tensor_idx * width), (chunk_len, width))
        upstream_own = lax.dynamic_slice(full_chunk, (0, tensor_idx * width), (chunk_len, width))
        d_in = inv_rms * (d_norm * gain_own - normed_own * row_mean)
        grad_out = (upstream_own.astype(jnp.float32) + d_in).astype(jnp.bfloat16)
        gain_part = jnp.sum(d_norm * normed_own, axis=0)
        previous = lax.dynamic_slice(results, (batch_slot, half_now, 0, 0), (1, 1, chunk_len, width))
        updated = jnp.where(active, grad_out[None, None], previous)
        results = lax.dynamic_update_slice(results, updated, (batch_slot, half_now, 0, 0))
        gain_acc = gain_acc + jnp.where(active, gain_part, 0.0)
        conv_acc = conv_acc + jnp.where(active, conv_part, 0.0)
        tail_carry = jnp.where(active, new_tail, tail_carry)
        incoming = handed_down(grad_out, tensors, sections, width)
        return (incoming, results, gain_acc, conv_acc, tail_carry)

    initial = (
        jnp.zeros((chunk_len, model_width), jnp.bfloat16),
        jnp.zeros((batches, halves, chunk_len, width), jnp.bfloat16),
        jnp.zeros((width,), jnp.float32),
        jnp.zeros(weights.shape, jnp.float32),
        tail_init,
    )
    last_state = lax.fori_loop(0, total_steps, step_rows, initial)
    gathered = sent_to_all(last_state[1], "tensor")
    results = jnp.transpose(gathered, (1, 2, 3, 0, 4)).reshape(batches, seq_len, model_width)
    conv_acc = last_state[3]
    gain_total = sent_to_all(last_state[2], "tensor").reshape(model_width)
    return (results[None], gain_total[None], conv_acc[None])


def solution(mesh):
    placed = (
        P(),
        P(),
        P(),
        P("section", None, None, None),
        P("section", None, None, "tensor"),
        P("section", None),
        P("section", None, "tensor"),
        P("section", None, "tensor"),
        P("section", "tensor", None),
    )
    return jax.shard_map(
        local,
        mesh=mesh,
        in_specs=placed,
        out_specs=(
            P("section", None, None, None),
            P("section", None),
            P("section", None, "tensor"),
        ),
        check_vma=False,
    )
```

```python
import functools

import jax
import jax.numpy as jnp
from jax import lax
from jax.experimental import pallas as pl
from jax.experimental.pallas import tpu as pltpu
from jax.sharding import PartitionSpec as P

EPSILON = 1e-05
MESH = pl.DeviceIdType.MESH
CHUNKS_PER_BATCH = 2


def sent_to_all(x, axis):
    copies = jnp.broadcast_to(x, (lax.axis_size(axis), *x.shape))
    return lax.all_to_all(copies, axis, split_axis=0, concat_axis=0, tiled=True)


def scatter_sum_kernel(n, width, x_ref, out_ref, recv, send_sem, recv_sem):
    me = lax.axis_index("tensor")
    sec = lax.axis_index("section")
    barrier = pltpu.get_barrier_semaphore()
    for k in range(1, n):
        pl.semaphore_signal(barrier, inc=1, device_id=(sec, lax.rem(me + k, n)), device_id_type=MESH)
    pl.semaphore_wait(barrier, n - 1)
    copies = []
    for k in range(1, n):
        peer = lax.rem(me + k, n)
        cols = pl.ds(pl.multiple_of(peer * width, 128), width)
        block = pltpu.make_async_remote_copy(
            src_ref=x_ref.at[:, cols],
            dst_ref=recv.at[me],
            send_sem=send_sem.at[k],
            recv_sem=recv_sem.at[k],
            device_id=(sec, peer),
            device_id_type=MESH,
        )
        block.start()
        copies.append(block)
    for block in copies:
        block.wait()
    mine = pl.ds(pl.multiple_of(me * width, 128), width)
    total = x_ref[:, mine].astype(jnp.float32)
    for k in range(1, n):
        src = lax.rem(me + n - k, n)
        total = total + recv[src].astype(jnp.float32)
    out_ref[...] = total


def scatter_sum(x, n, width):
    rows = x.shape[0]
    return pl.pallas_call(
        functools.partial(scatter_sum_kernel, n, width),
        out_shape=jax.ShapeDtypeStruct((rows, width), jnp.float32),
        in_specs=[pl.BlockSpec(memory_space=pltpu.VMEM)],
        out_specs=pl.BlockSpec(memory_space=pltpu.VMEM),
        scratch_shapes=[
            pltpu.VMEM((n, rows, width), x.dtype),
            pltpu.SemaphoreType.DMA((n,)),
            pltpu.SemaphoreType.DMA((n,)),
        ],
        compiler_params=pltpu.CompilerParams(collective_id=0, has_side_effects=True),
    )(x)


def handed_down_kernel(n, n_sec, width, g_ref, out_ref, recv, send_sem, recv_sem):
    me = lax.axis_index("tensor")
    sec = lax.axis_index("section")
    barrier = pltpu.get_barrier_semaphore()
    mine = pl.ds(pl.multiple_of(me * width, 128), width)

    @pl.when(sec < n_sec - 1)
    def _():
        for t in range(n):
            pl.semaphore_signal(barrier, inc=1, device_id=(sec + 1, t), device_id_type=MESH)

    @pl.when(sec > 0)
    def _():
        pl.semaphore_wait(barrier, n)
        copies = []
        for t in range(n):
            copy = pltpu.make_async_remote_copy(
                src_ref=g_ref,
                dst_ref=recv.at[:, mine],
                send_sem=send_sem.at[t],
                recv_sem=recv_sem.at[me],
                device_id=(sec - 1, t),
                device_id_type=MESH,
            )
            copy.start()
            copies.append(copy)
        for copy in copies:
            copy.wait_send()

    @pl.when(sec < n_sec - 1)
    def _():
        for src in range(n):
            pltpu.make_async_remote_copy(
                src_ref=g_ref,
                dst_ref=recv.at[:, pl.ds(src * width, width)],
                send_sem=send_sem.at[src],
                recv_sem=recv_sem.at[src],
                device_id=(sec + 1, src),
                device_id_type=MESH,
            ).wait_recv()
        out_ref[...] = recv[...]

    @pl.when(sec == n_sec - 1)
    def _():
        out_ref[...] = jnp.zeros_like(out_ref)


def handed_down(g_block, n, n_sec, width):
    rows = g_block.shape[0]
    return pl.pallas_call(
        functools.partial(handed_down_kernel, n, n_sec, width),
        out_shape=jax.ShapeDtypeStruct((rows, n * width), g_block.dtype),
        in_specs=[pl.BlockSpec(memory_space=pltpu.VMEM)],
        out_specs=pl.BlockSpec(memory_space=pltpu.VMEM),
        scratch_shapes=[
            pltpu.VMEM((rows, n * width), g_block.dtype),
            pltpu.SemaphoreType.DMA((n,)),
            pltpu.SemaphoreType.DMA((n,)),
        ],
        compiler_params=pltpu.CompilerParams(collective_id=1, has_side_effects=True),
    )(g_block)


def conv_block(weights, ext_vals, tail_rows, d_act):
    kernel_width = weights.shape[0]
    length = d_act.shape[0]
    pre_act = jnp.zeros_like(d_act)
    for lag_idx in range(kernel_width):
        start = kernel_width - 1 - lag_idx
        pre_act = pre_act + weights[lag_idx] * ext_vals[start : start + length]
    gate_sig = jax.nn.sigmoid(pre_act)
    d_pre = d_act * gate_sig * (1.0 + pre_act * (1.0 - gate_sig))
    padded_back = jnp.concatenate([d_pre, tail_rows], axis=0)
    d_vals = jnp.zeros_like(d_pre)
    for lag_idx in range(kernel_width):
        d_vals = d_vals + weights[lag_idx] * padded_back[lag_idx : lag_idx + length]
    lag_grads = jnp.stack(
        [
            jnp.sum(
                d_pre * ext_vals[kernel_width - 1 - lag_idx : kernel_width - 1 - lag_idx + length],
                axis=0,
            )
            for lag_idx in range(kernel_width)
        ]
    )
    return (d_vals.astype(jnp.bfloat16), lag_grads, d_pre[: kernel_width - 1])


def local(dy_top, loss_mask, counts, layer_in, conv_in, norm_gain, conv_weight, in_proj, out_proj):
    sections = lax.axis_size("section")
    tensors = lax.axis_size("tensor")
    section_idx = lax.axis_index("section")
    tensor_idx = lax.axis_index("tensor")
    batches, seq_len, model_width = dy_top.shape
    width = model_width // tensors
    gain_vec = norm_gain[0]
    weights = conv_weight[0]
    kernel_width = weights.shape[0]
    local_channels = weights.shape[1]
    w_in = in_proj[0]
    w_out_t = jnp.transpose(out_proj[0])
    conv_padded = jnp.pad(conv_in[0], ((0, 0), (kernel_width - 1, 0), (0, 0)))
    positions = jnp.arange(seq_len, dtype=jnp.int32)
    keep_mask = (loss_mask == 1) & (positions[None, :] < counts[:, None])
    top_grads = jnp.where(keep_mask[:, :, None], dy_top, jnp.zeros_like(dy_top))
    is_last = section_idx == sections - 1
    contract = (((1,), (1,)), ((), ()))

    values = layer_in[0].astype(jnp.float32)
    inv_rms_all = lax.rsqrt(jnp.mean(values * values, axis=-1, keepdims=True) + EPSILON)
    normed_all = values * inv_rms_all
    gain_own = lax.dynamic_slice(gain_vec, (tensor_idx * width,), (width,))

    stat_rows_n = 16
    halves = CHUNKS_PER_BATCH
    chunk_len = seq_len // halves
    order = [(b, h) for b in range(batches) for h in reversed(range(halves))]
    block_slot = jnp.array([b for b, _ in order], jnp.int32)
    block_half = jnp.array([h for _, h in order], jnp.int32)
    block_join = jnp.array([h < halves - 1 for _, h in order], jnp.bool_)
    n_chunks = len(order)
    total_steps = sections + n_chunks - 1

    def pick_block(step_idx):
        block_raw = step_idx - (sections - 1 - section_idx)
        active = (block_raw >= 0) & (block_raw < n_chunks)
        block_now = jnp.clip(block_raw, 0, n_chunks - 1)
        return (block_slot[block_now], block_half[block_now], block_join[block_now], active)

    def rows_of(array, batch_slot, first_row, row_count):
        return lax.dynamic_slice(array, (batch_slot, first_row, 0), (1, row_count, array.shape[2]))[0]

    tail_init = jnp.zeros((kernel_width - 1, local_channels), jnp.float32)

    def step_rows(step_idx, loop_state):
        incoming, results, gain_acc, conv_acc, tail_carry = loop_state
        batch_slot, half_now, join_now, active = pick_block(step_idx)
        row_start = half_now * chunk_len
        full_chunk = jnp.where(is_last, rows_of(top_grads, batch_slot, row_start, chunk_len), incoming)
        d_act = jnp.dot(full_chunk, w_out_t, preferred_element_type=jnp.float32)
        d_act = lax.optimization_barrier(d_act)
        ext_vals = lax.dynamic_slice(
            conv_padded, (batch_slot, row_start, 0), (1, chunk_len + kernel_width - 1, local_channels)
        )[0].astype(jnp.float32)
        tail_rows = jnp.where(join_now, tail_carry, 0.0)
        d_vals, conv_part, new_tail = conv_block(weights, ext_vals, tail_rows, d_act)
        partial = lax.dot_general(d_vals, w_in, contract, preferred_element_type=jnp.float32).astype(jnp.bfloat16)
        normed = rows_of(normed_all, batch_slot, row_start, chunk_len)
        inv_rms = rows_of(inv_rms_all, batch_slot, row_start, chunk_len)
        row_part = jnp.sum(partial.astype(jnp.float32) * gain_vec * normed, axis=-1)
        part_hi = row_part.astype(jnp.bfloat16)
        part_lo = (row_part - part_hi.astype(jnp.float32)).astype(jnp.bfloat16)
        stat_rows = jnp.zeros((stat_rows_n, width), jnp.bfloat16)
        stat_rows = stat_rows.at[0, :chunk_len].set(part_hi).at[1, :chunk_len].set(part_lo)
        sent = jnp.concatenate([partial, jnp.tile(stat_rows, (1, tensors))], axis=0)
        summed = scatter_sum(sent, tensors, width)
        d_norm = summed[:chunk_len]
        row_mean = (summed[chunk_len, :chunk_len] + summed[chunk_len + 1, :chunk_len])[:, None] / model_width
        normed_own = lax.dynamic_slice(normed, (0, tensor_idx * width), (chunk_len, width))
        upstream_own = lax.dynamic_slice(full_chunk, (0, tensor_idx * width), (chunk_len, width))
        d_in = inv_rms * (d_norm * gain_own - normed_own * row_mean)
        grad_out = (upstream_own.astype(jnp.float32) + d_in).astype(jnp.bfloat16)
        gain_part = jnp.sum(d_norm * normed_own, axis=0)
        previous = lax.dynamic_slice(results, (batch_slot, half_now, 0, 0), (1, 1, chunk_len, width))
        updated = jnp.where(active, grad_out[None, None], previous)
        results = lax.dynamic_update_slice(results, updated, (batch_slot, half_now, 0, 0))
        gain_acc = gain_acc + jnp.where(active, gain_part, 0.0)
        conv_acc = conv_acc + jnp.where(active, conv_part, 0.0)
        tail_carry = jnp.where(active, new_tail, tail_carry)
        incoming = handed_down(grad_out, tensors, sections, width)
        return (incoming, results, gain_acc, conv_acc, tail_carry)

    initial = (
        jnp.zeros((chunk_len, model_width), jnp.bfloat16),
        jnp.zeros((batches, halves, chunk_len, width), jnp.bfloat16),
        jnp.zeros((width,), jnp.float32),
        jnp.zeros(weights.shape, jnp.float32),
        tail_init,
    )
    last_state = lax.fori_loop(0, total_steps, step_rows, initial)
    gathered = sent_to_all(last_state[1], "tensor")
    results = jnp.transpose(gathered, (1, 2, 3, 0, 4)).reshape(batches, seq_len, model_width)
    conv_acc = last_state[3]
    gain_total = sent_to_all(last_state[2], "tensor").reshape(model_width)
    return (results[None], gain_total[None], conv_acc[None])


def solution(mesh):
    placed = (
        P(),
        P(),
        P(),
        P("section", None, None, None),
        P("section", None, None, "tensor"),
        P("section", None),
        P("section", None, "tensor"),
        P("section", None, "tensor"),
        P("section", "tensor", None),
    )
    return jax.shard_map(
        local,
        mesh=mesh,
        in_specs=placed,
        out_specs=(
            P("section", None, None, None),
            P("section", None),
            P("section", None, "tensor"),
        ),
        check_vma=False,
    )
```

```python
import functools

import jax
import jax.numpy as jnp
from jax import lax
from jax.experimental import pallas as pl
from jax.experimental.pallas import tpu as pltpu
from jax.sharding import PartitionSpec as P

EPSILON = 1e-05
MESH = pl.DeviceIdType.MESH
CHUNKS_PER_BATCH = 2


def sent_to_all(x, axis):
    copies = jnp.broadcast_to(x, (lax.axis_size(axis), *x.shape))
    return lax.all_to_all(copies, axis, split_axis=0, concat_axis=0, tiled=True)


def scatter_sum_kernel(n, width, x_ref, s_ref, out_ref, sum_ref, recv, srecv, send_sem, recv_sem, ssend_sem, srecv_sem):
    me = lax.axis_index("tensor")
    sec = lax.axis_index("section")
    barrier = pltpu.get_barrier_semaphore()
    for k in range(1, n):
        pl.semaphore_signal(barrier, inc=1, device_id=(sec, lax.rem(me + k, n)), device_id_type=MESH)
    pl.semaphore_wait(barrier, n - 1)
    copies = []
    for k in range(1, n):
        peer = lax.rem(me + k, n)
        cols = pl.ds(pl.multiple_of(peer * width, 128), width)
        block = pltpu.make_async_remote_copy(
            src_ref=x_ref.at[:, cols],
            dst_ref=recv.at[me],
            send_sem=send_sem.at[k],
            recv_sem=recv_sem.at[k],
            device_id=(sec, peer),
            device_id_type=MESH,
        )
        block.start()
        stat = pltpu.make_async_remote_copy(
            src_ref=s_ref,
            dst_ref=srecv.at[me],
            send_sem=ssend_sem.at[k],
            recv_sem=srecv_sem.at[k],
            device_id=(sec, peer),
            device_id_type=MESH,
        )
        stat.start()
        copies.append((block, stat))
    for block, stat in copies:
        block.wait()
        stat.wait()
    mine = pl.ds(pl.multiple_of(me * width, 128), width)
    total = x_ref[:, mine].astype(jnp.float32)
    stat_total = s_ref[...]
    for k in range(1, n):
        src = lax.rem(me + n - k, n)
        total = total + recv[src].astype(jnp.float32)
        stat_total = stat_total + srecv[src]
    out_ref[...] = total
    sum_ref[...] = stat_total


def scatter_sum(x, stats, n, width):
    rows = x.shape[0]
    return pl.pallas_call(
        functools.partial(scatter_sum_kernel, n, width),
        out_shape=(
            jax.ShapeDtypeStruct((rows, width), jnp.float32),
            jax.ShapeDtypeStruct(stats.shape, jnp.float32),
        ),
        in_specs=[pl.BlockSpec(memory_space=pltpu.VMEM)] * 2,
        out_specs=(pl.BlockSpec(memory_space=pltpu.VMEM), pl.BlockSpec(memory_space=pltpu.VMEM)),
        scratch_shapes=[
            pltpu.VMEM((n, rows, width), x.dtype),
            pltpu.VMEM((n, *stats.shape), jnp.float32),
            pltpu.SemaphoreType.DMA((n,)),
            pltpu.SemaphoreType.DMA((n,)),
            pltpu.SemaphoreType.DMA((n,)),
            pltpu.SemaphoreType.DMA((n,)),
        ],
        compiler_params=pltpu.CompilerParams(collective_id=0, has_side_effects=True),
    )(x, stats)


def handed_down_kernel(n, n_sec, width, g_ref, out_ref, recv, send_sem, recv_sem):
    me = lax.axis_index("tensor")
    sec = lax.axis_index("section")
    barrier = pltpu.get_barrier_semaphore()
    mine = pl.ds(pl.multiple_of(me * width, 128), width)

    @pl.when(sec < n_sec - 1)
    def _():
        for t in range(n):
            pl.semaphore_signal(barrier, inc=1, device_id=(sec + 1, t), device_id_type=MESH)

    @pl.when(sec > 0)
    def _():
        pl.semaphore_wait(barrier, n)
        copies = []
        for t in range(n):
            copy = pltpu.make_async_remote_copy(
                src_ref=g_ref,
                dst_ref=recv.at[:, mine],
                send_sem=send_sem.at[t],
                recv_sem=recv_sem.at[me],
                device_id=(sec - 1, t),
                device_id_type=MESH,
            )
            copy.start()
            copies.append(copy)
        for copy in copies:
            copy.wait_send()

    @pl.when(sec < n_sec - 1)
    def _():
        for src in range(n):
            pltpu.make_async_remote_copy(
                src_ref=g_ref,
                dst_ref=recv.at[:, pl.ds(src * width, width)],
                send_sem=send_sem.at[src],
                recv_sem=recv_sem.at[src],
                device_id=(sec + 1, src),
                device_id_type=MESH,
            ).wait_recv()
        out_ref[...] = recv[...]

    @pl.when(sec == n_sec - 1)
    def _():
        out_ref[...] = jnp.zeros_like(out_ref)


def handed_down(g_block, n, n_sec, width):
    rows = g_block.shape[0]
    return pl.pallas_call(
        functools.partial(handed_down_kernel, n, n_sec, width),
        out_shape=jax.ShapeDtypeStruct((rows, n * width), g_block.dtype),
        in_specs=[pl.BlockSpec(memory_space=pltpu.VMEM)],
        out_specs=pl.BlockSpec(memory_space=pltpu.VMEM),
        scratch_shapes=[
            pltpu.VMEM((rows, n * width), g_block.dtype),
            pltpu.SemaphoreType.DMA((n,)),
            pltpu.SemaphoreType.DMA((n,)),
        ],
        compiler_params=pltpu.CompilerParams(collective_id=1, has_side_effects=True),
    )(g_block)


def conv_block(weights, ext_vals, tail_rows, d_act):
    kernel_width = weights.shape[0]
    length = d_act.shape[0]
    pre_act = jnp.zeros_like(d_act)
    for lag_idx in range(kernel_width):
        start = kernel_width - 1 - lag_idx
        pre_act = pre_act + weights[lag_idx] * ext_vals[start : start + length]
    gate_sig = jax.nn.sigmoid(pre_act)
    d_pre = d_act * gate_sig * (1.0 + pre_act * (1.0 - gate_sig))
    padded_back = jnp.concatenate([d_pre, tail_rows], axis=0)
    d_vals = jnp.zeros_like(d_pre)
    for lag_idx in range(kernel_width):
        d_vals = d_vals + weights[lag_idx] * padded_back[lag_idx : lag_idx + length]
    lag_grads = jnp.stack(
        [
            jnp.sum(
                d_pre * ext_vals[kernel_width - 1 - lag_idx : kernel_width - 1 - lag_idx + length],
                axis=0,
            )
            for lag_idx in range(kernel_width)
        ]
    )
    return (d_vals.astype(jnp.bfloat16), lag_grads, d_pre[: kernel_width - 1])


def local(dy_top, loss_mask, counts, layer_in, conv_in, norm_gain, conv_weight, in_proj, out_proj):
    sections = lax.axis_size("section")
    tensors = lax.axis_size("tensor")
    section_idx = lax.axis_index("section")
    tensor_idx = lax.axis_index("tensor")
    batches, seq_len, model_width = dy_top.shape
    width = model_width // tensors
    gain_vec = norm_gain[0]
    weights = conv_weight[0]
    kernel_width = weights.shape[0]
    local_channels = weights.shape[1]
    w_in = in_proj[0]
    w_out = out_proj[0]
    conv_padded = jnp.pad(conv_in[0], ((0, 0), (kernel_width - 1, 0), (0, 0)))
    positions = jnp.arange(seq_len, dtype=jnp.int32)
    keep_mask = (loss_mask == 1) & (positions[None, :] < counts[:, None])
    top_grads = jnp.where(keep_mask[:, :, None], dy_top, jnp.zeros_like(dy_top))
    is_last = section_idx == sections - 1
    contract = (((1,), (1,)), ((), ()))

    values = layer_in[0].astype(jnp.float32)
    inv_rms_all = lax.rsqrt(jnp.mean(values * values, axis=-1, keepdims=True) + EPSILON)
    normed_all = values * inv_rms_all
    gain_own = lax.dynamic_slice(gain_vec, (tensor_idx * width,), (width,))

    halves = CHUNKS_PER_BATCH
    chunk_len = seq_len // halves
    n_chunks = batches * halves
    total_steps = sections + n_chunks - 1

    def pick_block(step_idx):
        block_raw = step_idx - (sections - 1 - section_idx)
        active = (block_raw >= 0) & (block_raw < n_chunks)
        block_now = jnp.clip(block_raw, 0, n_chunks - 1)
        within = lax.rem(block_now, halves)
        return (block_now // halves, halves - 1 - within, within > 0, active)

    def rows_of(array, batch_slot, first_row, row_count):
        return lax.dynamic_slice(array, (batch_slot, first_row, 0), (1, row_count, array.shape[2]))[0]

    tail_init = jnp.zeros((kernel_width - 1, local_channels), jnp.float32)

    def step_rows(step_idx, loop_state):
        incoming, results, gain_acc, conv_acc, tail_carry = loop_state
        batch_slot, half_now, join_now, active = pick_block(step_idx)
        row_start = half_now * chunk_len
        full_chunk = jnp.where(is_last, rows_of(top_grads, batch_slot, row_start, chunk_len), incoming)
        d_act = lax.dot_general(full_chunk, w_out, contract, preferred_element_type=jnp.float32)
        d_act = lax.optimization_barrier(d_act)
        ext_vals = lax.dynamic_slice(
            conv_padded, (batch_slot, row_start, 0), (1, chunk_len + kernel_width - 1, local_channels)
        )[0].astype(jnp.float32)
        tail_rows = jnp.where(join_now, tail_carry, 0.0)
        d_vals, conv_part, new_tail = conv_block(weights, ext_vals, tail_rows, d_act)
        partial = lax.dot_general(d_vals, w_in, contract, preferred_element_type=jnp.float32).astype(jnp.bfloat16)
        normed = rows_of(normed_all, batch_slot, row_start, chunk_len)
        inv_rms = rows_of(inv_rms_all, batch_slot, row_start, chunk_len)
        row_part = jnp.sum(partial.astype(jnp.float32) * gain_vec * normed, axis=-1)
        stats = jnp.zeros((8, 128), jnp.float32).at[0, :chunk_len].set(row_part)
        d_norm, stats_total = scatter_sum(partial, stats, tensors, width)
        row_mean = stats_total[0, :chunk_len][:, None] / model_width
        normed_own = lax.dynamic_slice(normed, (0, tensor_idx * width), (chunk_len, width))
        upstream_own = lax.dynamic_slice(full_chunk, (0, tensor_idx * width), (chunk_len, width))
        d_in = inv_rms * (d_norm * gain_own - normed_own * row_mean)
        grad_out = (upstream_own.astype(jnp.float32) + d_in).astype(jnp.bfloat16)
        gain_part = jnp.sum(d_norm * normed_own, axis=0)
        previous = lax.dynamic_slice(results, (batch_slot, half_now, 0, 0), (1, 1, chunk_len, width))
        updated = jnp.where(active, grad_out[None, None], previous)
        results = lax.dynamic_update_slice(results, updated, (batch_slot, half_now, 0, 0))
        gain_acc = gain_acc + jnp.where(active, gain_part, 0.0)
        conv_acc = conv_acc + jnp.where(active, conv_part, 0.0)
        tail_carry = jnp.where(active, new_tail, tail_carry)
        incoming = handed_down(grad_out, tensors, sections, width)
        return (incoming, results, gain_acc, conv_acc, tail_carry)

    initial = (
        jnp.zeros((chunk_len, model_width), jnp.bfloat16),
        jnp.zeros((batches, halves, chunk_len, width), jnp.bfloat16),
        jnp.zeros((width,), jnp.float32),
        jnp.zeros(weights.shape, jnp.float32),
        tail_init,
    )
    last_state = lax.fori_loop(0, total_steps, step_rows, initial)
    gathered = sent_to_all(last_state[1], "tensor")
    results = jnp.transpose(gathered, (1, 2, 3, 0, 4)).reshape(batches, seq_len, model_width)
    conv_acc = last_state[3]
    gain_total = sent_to_all(last_state[2], "tensor").reshape(model_width)
    return (results[None], gain_total[None], conv_acc[None])


def solution(mesh):
    placed = (
        P(),
        P(),
        P(),
        P("section", None, None, None),
        P("section", None, None, "tensor"),
        P("section", None),
        P("section", None, "tensor"),
        P("section", None, "tensor"),
        P("section", "tensor", None),
    )
    return jax.shard_map(
        local,
        mesh=mesh,
        in_specs=placed,
        out_specs=(
            P("section", None, None, None),
            P("section", None),
            P("section", None, "tensor"),
        ),
        check_vma=False,
    )
```

```python
import functools

import jax
import jax.numpy as jnp
from jax import lax
from jax.experimental import pallas as pl
from jax.experimental.pallas import tpu as pltpu
from jax.sharding import PartitionSpec as P

EPSILON = 1e-05
MESH = pl.DeviceIdType.MESH
CHUNKS_PER_BATCH = 2


def sent_to_all(x, axis):
    copies = jnp.broadcast_to(x, (lax.axis_size(axis), *x.shape))
    return lax.all_to_all(copies, axis, split_axis=0, concat_axis=0, tiled=True)


def scatter_sum_kernel(n, width, x_ref, s_ref, out_ref, sum_ref, recv, srecv, send_sem, recv_sem, ssend_sem, srecv_sem):
    me = lax.axis_index("tensor")
    sec = lax.axis_index("section")
    barrier = pltpu.get_barrier_semaphore()
    for k in range(1, n):
        pl.semaphore_signal(barrier, inc=1, device_id=(sec, lax.rem(me + k, n)), device_id_type=MESH)
    pl.semaphore_wait(barrier, n - 1)
    copies = []
    for k in range(1, n):
        peer = lax.rem(me + k, n)
        cols = pl.ds(pl.multiple_of(peer * width, 128), width)
        block = pltpu.make_async_remote_copy(
            src_ref=x_ref.at[:, cols],
            dst_ref=recv.at[me],
            send_sem=send_sem.at[k],
            recv_sem=recv_sem.at[k],
            device_id=(sec, peer),
            device_id_type=MESH,
        )
        block.start()
        stat = pltpu.make_async_remote_copy(
            src_ref=s_ref,
            dst_ref=srecv.at[me],
            send_sem=ssend_sem.at[k],
            recv_sem=srecv_sem.at[k],
            device_id=(sec, peer),
            device_id_type=MESH,
        )
        stat.start()
        copies.append((block, stat))
    for block, stat in copies:
        block.wait()
        stat.wait()
    mine = pl.ds(pl.multiple_of(me * width, 128), width)
    total = x_ref[:, mine].astype(jnp.float32)
    stat_total = s_ref[...]
    for k in range(1, n):
        src = lax.rem(me + n - k, n)
        total = total + recv[src].astype(jnp.float32)
        stat_total = stat_total + srecv[src]
    out_ref[...] = total
    sum_ref[...] = stat_total


def scatter_sum(x, stats, n, width):
    rows = x.shape[0]
    return pl.pallas_call(
        functools.partial(scatter_sum_kernel, n, width),
        out_shape=(
            jax.ShapeDtypeStruct((rows, width), jnp.float32),
            jax.ShapeDtypeStruct(stats.shape, jnp.float32),
        ),
        in_specs=[pl.BlockSpec(memory_space=pltpu.VMEM)] * 2,
        out_specs=(pl.BlockSpec(memory_space=pltpu.VMEM), pl.BlockSpec(memory_space=pltpu.VMEM)),
        scratch_shapes=[
            pltpu.VMEM((n, rows, width), x.dtype),
            pltpu.VMEM((n, *stats.shape), jnp.float32),
            pltpu.SemaphoreType.DMA((n,)),
            pltpu.SemaphoreType.DMA((n,)),
            pltpu.SemaphoreType.DMA((n,)),
            pltpu.SemaphoreType.DMA((n,)),
        ],
        compiler_params=pltpu.CompilerParams(collective_id=0, has_side_effects=True),
    )(x, stats)


def handed_down_kernel(n, n_sec, width, g_ref, out_ref, recv, send_sem, recv_sem):
    me = lax.axis_index("tensor")
    sec = lax.axis_index("section")
    barrier = pltpu.get_barrier_semaphore()
    mine = pl.ds(pl.multiple_of(me * width, 128), width)

    @pl.when(sec < n_sec - 1)
    def _():
        for t in range(n):
            pl.semaphore_signal(barrier, inc=1, device_id=(sec + 1, t), device_id_type=MESH)

    @pl.when(sec > 0)
    def _():
        pl.semaphore_wait(barrier, n)
        copies = []
        for t in range(n):
            copy = pltpu.make_async_remote_copy(
                src_ref=g_ref,
                dst_ref=recv.at[:, mine],
                send_sem=send_sem.at[t],
                recv_sem=recv_sem.at[me],
                device_id=(sec - 1, t),
                device_id_type=MESH,
            )
            copy.start()
            copies.append(copy)
        for copy in copies:
            copy.wait_send()

    @pl.when(sec < n_sec - 1)
    def _():
        for src in range(n):
            pltpu.make_async_remote_copy(
                src_ref=g_ref,
                dst_ref=recv.at[:, pl.ds(src * width, width)],
                send_sem=send_sem.at[src],
                recv_sem=recv_sem.at[src],
                device_id=(sec + 1, src),
                device_id_type=MESH,
            ).wait_recv()
        out_ref[...] = recv[...]

    @pl.when(sec == n_sec - 1)
    def _():
        out_ref[...] = jnp.zeros_like(out_ref)


def handed_down(g_block, n, n_sec, width):
    rows = g_block.shape[0]
    return pl.pallas_call(
        functools.partial(handed_down_kernel, n, n_sec, width),
        out_shape=jax.ShapeDtypeStruct((rows, n * width), g_block.dtype),
        in_specs=[pl.BlockSpec(memory_space=pltpu.VMEM)],
        out_specs=pl.BlockSpec(memory_space=pltpu.VMEM),
        scratch_shapes=[
            pltpu.VMEM((rows, n * width), g_block.dtype),
            pltpu.SemaphoreType.DMA((n,)),
            pltpu.SemaphoreType.DMA((n,)),
        ],
        compiler_params=pltpu.CompilerParams(collective_id=1, has_side_effects=True),
    )(g_block)


def matmul_nt_kernel(x_ref, w_ref, out_ref):
    product = lax.dot_general(
        x_ref[...], w_ref[...], (((1,), (1,)), ((), ())), preferred_element_type=jnp.float32
    )

    @pl.when(pl.program_id(1) == 0)
    def _():
        out_ref[...] = product.astype(out_ref.dtype)

    @pl.when(pl.program_id(1) > 0)
    def _():
        out_ref[...] += product.astype(out_ref.dtype)


def matmul_nt(x, w, block_n, block_k, out_dtype):
    rows, depth = x.shape
    cols = w.shape[0]
    grid = (cols // block_n, depth // block_k)
    return pl.pallas_call(
        matmul_nt_kernel,
        out_shape=jax.ShapeDtypeStruct((rows, cols), out_dtype),
        grid=grid,
        in_specs=[
            pl.BlockSpec((rows, block_k), lambda n, k: (0, k)),
            pl.BlockSpec((block_n, block_k), lambda n, k: (n, k)),
        ],
        out_specs=pl.BlockSpec((rows, block_n), lambda n, k: (0, n)),
        compiler_params=pltpu.CompilerParams(
            dimension_semantics=("arbitrary", "arbitrary"), vmem_limit_bytes=48 * 1024 * 1024
        ),
        cost_estimate=pl.CostEstimate(
            flops=2 * rows * cols * depth,
            bytes_accessed=2 * (rows * depth + cols * depth) + rows * cols * jnp.dtype(out_dtype).itemsize,
            transcendentals=0,
        ),
    )(x, w)


def conv_block(weights, ext_vals, tail_rows, d_act):
    kernel_width = weights.shape[0]
    length = d_act.shape[0]
    pre_act = jnp.zeros_like(d_act)
    for lag_idx in range(kernel_width):
        start = kernel_width - 1 - lag_idx
        pre_act = pre_act + weights[lag_idx] * ext_vals[start : start + length]
    gate_sig = jax.nn.sigmoid(pre_act)
    d_pre = d_act * gate_sig * (1.0 + pre_act * (1.0 - gate_sig))
    padded_back = jnp.concatenate([d_pre, tail_rows], axis=0)
    d_vals = jnp.zeros_like(d_pre)
    for lag_idx in range(kernel_width):
        d_vals = d_vals + weights[lag_idx] * padded_back[lag_idx : lag_idx + length]
    lag_grads = jnp.stack(
        [
            jnp.sum(
                d_pre * ext_vals[kernel_width - 1 - lag_idx : kernel_width - 1 - lag_idx + length],
                axis=0,
            )
            for lag_idx in range(kernel_width)
        ]
    )
    return (d_vals.astype(jnp.bfloat16), lag_grads, d_pre[: kernel_width - 1])


def local(dy_top, loss_mask, counts, layer_in, conv_in, norm_gain, conv_weight, in_proj, out_proj):
    sections = lax.axis_size("section")
    tensors = lax.axis_size("tensor")
    section_idx = lax.axis_index("section")
    tensor_idx = lax.axis_index("tensor")
    batches, seq_len, model_width = dy_top.shape
    width = model_width // tensors
    gain_vec = norm_gain[0]
    weights = conv_weight[0]
    kernel_width = weights.shape[0]
    local_channels = weights.shape[1]
    w_in = in_proj[0]
    w_out = out_proj[0]
    conv_padded = jnp.pad(conv_in[0], ((0, 0), (kernel_width - 1, 0), (0, 0)))
    positions = jnp.arange(seq_len, dtype=jnp.int32)
    keep_mask = (loss_mask == 1) & (positions[None, :] < counts[:, None])
    top_grads = jnp.where(keep_mask[:, :, None], dy_top, jnp.zeros_like(dy_top))
    is_last = section_idx == sections - 1
    contract = (((1,), (1,)), ((), ()))

    values = layer_in[0].astype(jnp.float32)
    inv_rms_all = lax.rsqrt(jnp.mean(values * values, axis=-1, keepdims=True) + EPSILON)
    normed_all = values * inv_rms_all
    gain_own = lax.dynamic_slice(gain_vec, (tensor_idx * width,), (width,))

    halves = CHUNKS_PER_BATCH
    chunk_len = seq_len // halves
    n_chunks = batches * halves
    total_steps = sections + n_chunks - 1

    def pick_block(step_idx):
        block_raw = step_idx - (sections - 1 - section_idx)
        active = (block_raw >= 0) & (block_raw < n_chunks)
        block_now = jnp.clip(block_raw, 0, n_chunks - 1)
        within = lax.rem(block_now, halves)
        return (block_now // halves, halves - 1 - within, within > 0, active)

    def rows_of(array, batch_slot, first_row, row_count):
        return lax.dynamic_slice(array, (batch_slot, first_row, 0), (1, row_count, array.shape[2]))[0]

    tail_init = jnp.zeros((kernel_width - 1, local_channels), jnp.float32)

    def step_rows(step_idx, loop_state):
        incoming, results, gain_acc, conv_acc, tail_carry = loop_state
        batch_slot, half_now, join_now, active = pick_block(step_idx)
        row_start = half_now * chunk_len
        full_chunk = jnp.where(is_last, rows_of(top_grads, batch_slot, row_start, chunk_len), incoming)
        d_act = matmul_nt(full_chunk, w_out, w_out.shape[0], 2048, jnp.float32)
        ext_vals = lax.dynamic_slice(
            conv_padded, (batch_slot, row_start, 0), (1, chunk_len + kernel_width - 1, local_channels)
        )[0].astype(jnp.float32)
        tail_rows = jnp.where(join_now, tail_carry, 0.0)
        d_vals, conv_part, new_tail = conv_block(weights, ext_vals, tail_rows, d_act)
        partial = lax.dot_general(d_vals, w_in, contract, preferred_element_type=jnp.float32).astype(jnp.bfloat16)
        normed = rows_of(normed_all, batch_slot, row_start, chunk_len)
        inv_rms = rows_of(inv_rms_all, batch_slot, row_start, chunk_len)
        row_part = jnp.sum(partial.astype(jnp.float32) * gain_vec * normed, axis=-1)
        stats = jnp.zeros((8, 128), jnp.float32).at[0, :chunk_len].set(row_part)
        d_norm, stats_total = scatter_sum(partial, stats, tensors, width)
        row_mean = stats_total[0, :chunk_len][:, None] / model_width
        normed_own = lax.dynamic_slice(normed, (0, tensor_idx * width), (chunk_len, width))
        upstream_own = lax.dynamic_slice(full_chunk, (0, tensor_idx * width), (chunk_len, width))
        d_in = inv_rms * (d_norm * gain_own - normed_own * row_mean)
        grad_out = (upstream_own.astype(jnp.float32) + d_in).astype(jnp.bfloat16)
        gain_part = jnp.sum(d_norm * normed_own, axis=0)
        previous = lax.dynamic_slice(results, (batch_slot, half_now, 0, 0), (1, 1, chunk_len, width))
        updated = jnp.where(active, grad_out[None, None], previous)
        results = lax.dynamic_update_slice(results, updated, (batch_slot, half_now, 0, 0))
        gain_acc = gain_acc + jnp.where(active, gain_part, 0.0)
        conv_acc = conv_acc + jnp.where(active, conv_part, 0.0)
        tail_carry = jnp.where(active, new_tail, tail_carry)
        incoming = handed_down(grad_out, tensors, sections, width)
        return (incoming, results, gain_acc, conv_acc, tail_carry)

    initial = (
        jnp.zeros((chunk_len, model_width), jnp.bfloat16),
        jnp.zeros((batches, halves, chunk_len, width), jnp.bfloat16),
        jnp.zeros((width,), jnp.float32),
        jnp.zeros(weights.shape, jnp.float32),
        tail_init,
    )
    last_state = lax.fori_loop(0, total_steps, step_rows, initial)
    gathered = sent_to_all(last_state[1], "tensor")
    results = jnp.transpose(gathered, (1, 2, 3, 0, 4)).reshape(batches, seq_len, model_width)
    conv_acc = last_state[3]
    gain_total = sent_to_all(last_state[2], "tensor").reshape(model_width)
    return (results[None], gain_total[None], conv_acc[None])


def solution(mesh):
    placed = (
        P(),
        P(),
        P(),
        P("section", None, None, None),
        P("section", None, None, "tensor"),
        P("section", None),
        P("section", None, "tensor"),
        P("section", None, "tensor"),
        P("section", "tensor", None),
    )
    return jax.shard_map(
        local,
        mesh=mesh,
        in_specs=placed,
        out_specs=(
            P("section", None, None, None),
            P("section", None),
            P("section", None, "tensor"),
        ),
        check_vma=False,
    )
```

```python
import functools

import jax
import jax.numpy as jnp
from jax import lax
from jax.experimental import pallas as pl
from jax.experimental.pallas import tpu as pltpu
from jax.sharding import PartitionSpec as P

EPSILON = 1e-05
MESH = pl.DeviceIdType.MESH
CHUNKS_PER_BATCH = 2


def sent_to_all(x, axis):
    copies = jnp.broadcast_to(x, (lax.axis_size(axis), *x.shape))
    return lax.all_to_all(copies, axis, split_axis=0, concat_axis=0, tiled=True)


def matmul_nt_kernel(x_ref, w_ref, out_ref):
    product = lax.dot_general(
        x_ref[...], w_ref[...], (((1,), (1,)), ((), ())), preferred_element_type=jnp.float32
    )

    @pl.when(pl.program_id(1) == 0)
    def _():
        out_ref[...] = product.astype(out_ref.dtype)

    @pl.when(pl.program_id(1) > 0)
    def _():
        out_ref[...] += product.astype(out_ref.dtype)


def matmul_nt(x, w, block_n, block_k, out_dtype):
    rows, depth = x.shape
    cols = w.shape[0]
    grid = (cols // block_n, depth // block_k)
    return pl.pallas_call(
        matmul_nt_kernel,
        out_shape=jax.ShapeDtypeStruct((rows, cols), out_dtype),
        grid=grid,
        in_specs=[
            pl.BlockSpec((rows, block_k), lambda n, k: (0, k)),
            pl.BlockSpec((block_n, block_k), lambda n, k: (n, k)),
        ],
        out_specs=pl.BlockSpec((rows, block_n), lambda n, k: (0, n)),
        compiler_params=pltpu.CompilerParams(
            dimension_semantics=("arbitrary", "arbitrary"), vmem_limit_bytes=48 * 1024 * 1024
        ),
        cost_estimate=pl.CostEstimate(
            flops=2 * rows * cols * depth,
            bytes_accessed=2 * (rows * depth + cols * depth) + rows * cols * jnp.dtype(out_dtype).itemsize,
            transcendentals=0,
        ),
    )(x, w)


def layer_exchange_kernel(
    n, n_sec, width, x_ref, s_ref, normed_ref, inv_ref, gain_ref, up_ref,
    g_ref, next_ref, gain_out_ref,
    recv, srecv, gbuf, down, send_sem, recv_sem, ssend_sem, srecv_sem, dsend_sem, drecv_sem,
):
    me = lax.axis_index("tensor")
    sec = lax.axis_index("section")
    barrier = pltpu.get_barrier_semaphore()
    for k in range(1, n):
        pl.semaphore_signal(barrier, inc=1, device_id=(sec, lax.rem(me + k, n)), device_id_type=MESH)

    @pl.when(sec < n_sec - 1)
    def _():
        for t in range(n):
            pl.semaphore_signal(barrier, inc=1, device_id=(sec + 1, t), device_id_type=MESH)

    @pl.when(sec > 0)
    def _():
        pl.semaphore_wait(barrier, 2 * n - 1)

    @pl.when(sec == 0)
    def _():
        pl.semaphore_wait(barrier, n - 1)

    copies = []
    for k in range(1, n):
        peer = lax.rem(me + k, n)
        cols = pl.ds(pl.multiple_of(peer * width, 128), width)
        block = pltpu.make_async_remote_copy(
            src_ref=x_ref.at[:, cols],
            dst_ref=recv.at[me],
            send_sem=send_sem.at[k],
            recv_sem=recv_sem.at[k],
            device_id=(sec, peer),
            device_id_type=MESH,
        )
        block.start()
        stat = pltpu.make_async_remote_copy(
            src_ref=s_ref,
            dst_ref=srecv.at[me],
            send_sem=ssend_sem.at[k],
            recv_sem=srecv_sem.at[k],
            device_id=(sec, peer),
            device_id_type=MESH,
        )
        stat.start()
        copies.append((block, stat))
    for block, stat in copies:
        block.wait()
        stat.wait()
    mine = pl.ds(pl.multiple_of(me * width, 128), width)
    total = x_ref[:, mine].astype(jnp.float32)
    stat_total = s_ref[...]
    for k in range(1, n):
        src = lax.rem(me + n - k, n)
        total = total + recv[src].astype(jnp.float32)
        stat_total = stat_total + srecv[src]
    rows = total.shape[0]
    row_mean = stat_total[:, 0:1] * (1.0 / (n * width))
    normed = normed_ref[...]
    d_in = inv_ref[...] * (total * gain_ref[...] - normed * row_mean)
    result = (up_ref[...].astype(jnp.float32) + d_in).astype(g_ref.dtype)
    gbuf[...] = result
    g_ref[...] = result
    gain_out_ref[...] = jnp.sum(total * normed, axis=0, keepdims=True)

    @pl.when(sec > 0)
    def _():
        sends = []
        for t in range(n):
            copy = pltpu.make_async_remote_copy(
                src_ref=gbuf,
                dst_ref=down.at[:, mine],
                send_sem=dsend_sem.at[t],
                recv_sem=drecv_sem.at[me],
                device_id=(sec - 1, t),
                device_id_type=MESH,
            )
            copy.start()
            sends.append(copy)
        for copy in sends:
            copy.wait_send()

    @pl.when(sec < n_sec - 1)
    def _():
        for src in range(n):
            pltpu.make_async_remote_copy(
                src_ref=gbuf,
                dst_ref=down.at[:, pl.ds(src * width, width)],
                send_sem=dsend_sem.at[src],
                recv_sem=drecv_sem.at[src],
                device_id=(sec + 1, src),
                device_id_type=MESH,
            ).wait_recv()
        next_ref[...] = down[...]

    @pl.when(sec == n_sec - 1)
    def _():
        next_ref[...] = jnp.zeros_like(next_ref)


def layer_exchange(partial, stats, normed, inv_rms, gain_own, upstream, n, n_sec, width):
    rows = partial.shape[0]
    vmem = pl.BlockSpec(memory_space=pltpu.VMEM)
    return pl.pallas_call(
        functools.partial(layer_exchange_kernel, n, n_sec, width),
        out_shape=(
            jax.ShapeDtypeStruct((rows, width), jnp.bfloat16),
            jax.ShapeDtypeStruct((rows, n * width), jnp.bfloat16),
            jax.ShapeDtypeStruct((1, width), jnp.float32),
        ),
        in_specs=[vmem] * 6,
        out_specs=(vmem, vmem, vmem),
        scratch_shapes=[
            pltpu.VMEM((n, rows, width), partial.dtype),
            pltpu.VMEM((n, *stats.shape), jnp.float32),
            pltpu.VMEM((rows, width), jnp.bfloat16),
            pltpu.VMEM((rows, n * width), jnp.bfloat16),
            pltpu.SemaphoreType.DMA((n,)),
            pltpu.SemaphoreType.DMA((n,)),
            pltpu.SemaphoreType.DMA((n,)),
            pltpu.SemaphoreType.DMA((n,)),
            pltpu.SemaphoreType.DMA((n,)),
            pltpu.SemaphoreType.DMA((n,)),
        ],
        compiler_params=pltpu.CompilerParams(collective_id=2, has_side_effects=True),
    )(partial, stats, normed, inv_rms, gain_own, upstream)


def conv_block(weights, ext_vals, tail_rows, d_act):
    kernel_width = weights.shape[0]
    length = d_act.shape[0]
    pre_act = jnp.zeros_like(d_act)
    for lag_idx in range(kernel_width):
        start = kernel_width - 1 - lag_idx
        pre_act = pre_act + weights[lag_idx] * ext_vals[start : start + length]
    gate_sig = jax.nn.sigmoid(pre_act)
    d_pre = d_act * gate_sig * (1.0 + pre_act * (1.0 - gate_sig))
    padded_back = jnp.concatenate([d_pre, tail_rows], axis=0)
    d_vals = jnp.zeros_like(d_pre)
    for lag_idx in range(kernel_width):
        d_vals = d_vals + weights[lag_idx] * padded_back[lag_idx : lag_idx + length]
    lag_grads = jnp.stack(
        [
            jnp.sum(
                d_pre * ext_vals[kernel_width - 1 - lag_idx : kernel_width - 1 - lag_idx + length],
                axis=0,
            )
            for lag_idx in range(kernel_width)
        ]
    )
    return (d_vals.astype(jnp.bfloat16), lag_grads, d_pre[: kernel_width - 1])


def local(dy_top, loss_mask, counts, layer_in, conv_in, norm_gain, conv_weight, in_proj, out_proj):
    sections = lax.axis_size("section")
    tensors = lax.axis_size("tensor")
    section_idx = lax.axis_index("section")
    tensor_idx = lax.axis_index("tensor")
    batches, seq_len, model_width = dy_top.shape
    width = model_width // tensors
    gain_vec = norm_gain[0]
    weights = conv_weight[0]
    kernel_width = weights.shape[0]
    local_channels = weights.shape[1]
    w_in = in_proj[0]
    w_out = out_proj[0]
    conv_padded = jnp.pad(conv_in[0], ((0, 0), (kernel_width - 1, 0), (0, 0)))
    positions = jnp.arange(seq_len, dtype=jnp.int32)
    keep_mask = (loss_mask == 1) & (positions[None, :] < counts[:, None])
    top_grads = jnp.where(keep_mask[:, :, None], dy_top, jnp.zeros_like(dy_top))
    is_last = section_idx == sections - 1
    contract = (((1,), (1,)), ((), ()))

    values = layer_in[0].astype(jnp.float32)
    inv_rms_all = lax.rsqrt(jnp.mean(values * values, axis=-1, keepdims=True) + EPSILON)
    normed_all = values * inv_rms_all
    gain_own = lax.dynamic_slice(gain_vec, (tensor_idx * width,), (width,))

    halves = CHUNKS_PER_BATCH
    chunk_len = seq_len // halves
    n_chunks = batches * halves
    total_steps = sections + n_chunks - 1

    def pick_block(step_idx):
        block_raw = step_idx - (sections - 1 - section_idx)
        active = (block_raw >= 0) & (block_raw < n_chunks)
        block_now = jnp.clip(block_raw, 0, n_chunks - 1)
        within = lax.rem(block_now, halves)
        return (block_now // halves, halves - 1 - within, within > 0, active)

    def rows_of(array, batch_slot, first_row, row_count):
        return lax.dynamic_slice(array, (batch_slot, first_row, 0), (1, row_count, array.shape[2]))[0]

    tail_init = jnp.zeros((kernel_width - 1, local_channels), jnp.float32)

    def step_rows(step_idx, loop_state):
        incoming, results, gain_acc, conv_acc, tail_carry = loop_state
        batch_slot, half_now, join_now, active = pick_block(step_idx)
        row_start = half_now * chunk_len
        full_chunk = jnp.where(is_last, rows_of(top_grads, batch_slot, row_start, chunk_len), incoming)
        d_act = matmul_nt(full_chunk, w_out, w_out.shape[0], 2048, jnp.float32)
        ext_vals = lax.dynamic_slice(
            conv_padded, (batch_slot, row_start, 0), (1, chunk_len + kernel_width - 1, local_channels)
        )[0].astype(jnp.float32)
        tail_rows = jnp.where(join_now, tail_carry, 0.0)
        d_vals, conv_part, new_tail = conv_block(weights, ext_vals, tail_rows, d_act)
        partial = lax.dot_general(d_vals, w_in, contract, preferred_element_type=jnp.float32).astype(jnp.bfloat16)
        normed = rows_of(normed_all, batch_slot, row_start, chunk_len)
        inv_rms = rows_of(inv_rms_all, batch_slot, row_start, chunk_len)
        row_part = jnp.sum(partial.astype(jnp.float32) * gain_vec * normed, axis=-1)
        stats = jnp.zeros((chunk_len, 128), jnp.float32).at[:, 0].set(row_part)
        normed_own = lax.dynamic_slice(normed, (0, tensor_idx * width), (chunk_len, width))
        upstream_own = lax.dynamic_slice(full_chunk, (0, tensor_idx * width), (chunk_len, width))
        grad_out, incoming_next, gain_part = layer_exchange(
            partial, stats, normed_own, inv_rms, gain_own[None, :], upstream_own, tensors, sections, width
        )
        gain_part = gain_part[0]
        previous = lax.dynamic_slice(results, (batch_slot, half_now, 0, 0), (1, 1, chunk_len, width))
        updated = jnp.where(active, grad_out[None, None], previous)
        results = lax.dynamic_update_slice(results, updated, (batch_slot, half_now, 0, 0))
        gain_acc = gain_acc + jnp.where(active, gain_part, 0.0)
        conv_acc = conv_acc + jnp.where(active, conv_part, 0.0)
        tail_carry = jnp.where(active, new_tail, tail_carry)
        incoming = incoming_next
        return (incoming, results, gain_acc, conv_acc, tail_carry)

    initial = (
        jnp.zeros((chunk_len, model_width), jnp.bfloat16),
        jnp.zeros((batches, halves, chunk_len, width), jnp.bfloat16),
        jnp.zeros((width,), jnp.float32),
        jnp.zeros(weights.shape, jnp.float32),
        tail_init,
    )
    last_state = lax.fori_loop(0, total_steps, step_rows, initial)
    gathered = sent_to_all(last_state[1], "tensor")
    results = jnp.transpose(gathered, (1, 2, 3, 0, 4)).reshape(batches, seq_len, model_width)
    conv_acc = last_state[3]
    gain_total = sent_to_all(last_state[2], "tensor").reshape(model_width)
    return (results[None], gain_total[None], conv_acc[None])


def solution(mesh):
    placed = (
        P(),
        P(),
        P(),
        P("section", None, None, None),
        P("section", None, None, "tensor"),
        P("section", None),
        P("section", None, "tensor"),
        P("section", None, "tensor"),
        P("section", "tensor", None),
    )
    return jax.shard_map(
        local,
        mesh=mesh,
        in_specs=placed,
        out_specs=(
            P("section", None, None, None),
            P("section", None),
            P("section", None, "tensor"),
        ),
        check_vma=False,
    )
```

```python
import functools

import jax
import jax.numpy as jnp
from jax import lax
from jax.experimental import pallas as pl
from jax.experimental.pallas import tpu as pltpu
from jax.sharding import PartitionSpec as P

EPSILON = 1e-05
MESH = pl.DeviceIdType.MESH
CHUNKS_PER_BATCH = 2


def sent_to_all(x, axis):
    copies = jnp.broadcast_to(x, (lax.axis_size(axis), *x.shape))
    return lax.all_to_all(copies, axis, split_axis=0, concat_axis=0, tiled=True)


def matmul_nt_kernel(x_ref, w_ref, out_ref):
    product = lax.dot_general(
        x_ref[...], w_ref[...], (((1,), (1,)), ((), ())), preferred_element_type=jnp.float32
    )

    @pl.when(pl.program_id(1) == 0)
    def _():
        out_ref[...] = product.astype(out_ref.dtype)

    @pl.when(pl.program_id(1) > 0)
    def _():
        out_ref[...] += product.astype(out_ref.dtype)


def matmul_nt(x, w, block_n, block_k, out_dtype):
    rows, depth = x.shape
    cols = w.shape[0]
    grid = (cols // block_n, depth // block_k)
    return pl.pallas_call(
        matmul_nt_kernel,
        out_shape=jax.ShapeDtypeStruct((rows, cols), out_dtype),
        grid=grid,
        in_specs=[
            pl.BlockSpec((rows, block_k), lambda n, k: (0, k)),
            pl.BlockSpec((block_n, block_k), lambda n, k: (n, k)),
        ],
        out_specs=pl.BlockSpec((rows, block_n), lambda n, k: (0, n)),
        compiler_params=pltpu.CompilerParams(
            dimension_semantics=("arbitrary", "arbitrary"), vmem_limit_bytes=16 * 1024 * 1024
        ),
        cost_estimate=pl.CostEstimate(
            flops=2 * rows * cols * depth,
            bytes_accessed=2 * (rows * depth + cols * depth) + rows * cols * jnp.dtype(out_dtype).itemsize,
            transcendentals=0,
        ),
    )(x, w)


def layer_exchange_kernel(
    n, n_sec, width, x_ref, s_ref, normed_ref, inv_ref, gain_ref, up_ref,
    g_ref, next_ref, gain_out_ref,
    recv, srecv, gbuf, down, send_sem, recv_sem, ssend_sem, srecv_sem, dsend_sem, drecv_sem,
):
    me = lax.axis_index("tensor")
    sec = lax.axis_index("section")
    barrier = pltpu.get_barrier_semaphore()
    for k in range(1, n):
        pl.semaphore_signal(barrier, inc=1, device_id=(sec, lax.rem(me + k, n)), device_id_type=MESH)

    @pl.when(sec < n_sec - 1)
    def _():
        for t in range(n):
            pl.semaphore_signal(barrier, inc=1, device_id=(sec + 1, t), device_id_type=MESH)

    @pl.when(sec > 0)
    def _():
        pl.semaphore_wait(barrier, 2 * n - 1)

    @pl.when(sec == 0)
    def _():
        pl.semaphore_wait(barrier, n - 1)

    copies = []
    for k in range(1, n):
        peer = lax.rem(me + k, n)
        cols = pl.ds(pl.multiple_of(peer * width, 128), width)
        block = pltpu.make_async_remote_copy(
            src_ref=x_ref.at[:, cols],
            dst_ref=recv.at[me],
            send_sem=send_sem.at[k],
            recv_sem=recv_sem.at[k],
            device_id=(sec, peer),
            device_id_type=MESH,
        )
        block.start()
        stat = pltpu.make_async_remote_copy(
            src_ref=s_ref,
            dst_ref=srecv.at[me],
            send_sem=ssend_sem.at[k],
            recv_sem=srecv_sem.at[k],
            device_id=(sec, peer),
            device_id_type=MESH,
        )
        stat.start()
        copies.append((block, stat))
    for block, stat in copies:
        block.wait()
        stat.wait()
    mine = pl.ds(pl.multiple_of(me * width, 128), width)
    total = x_ref[:, mine].astype(jnp.float32)
    stat_total = s_ref[...]
    for k in range(1, n):
        src = lax.rem(me + n - k, n)
        total = total + recv[src].astype(jnp.float32)
        stat_total = stat_total + srecv[src]
    rows = total.shape[0]
    row_mean = stat_total[:, 0:1] * (1.0 / (n * width))
    normed = normed_ref[...]
    d_in = inv_ref[...] * (total * gain_ref[...] - normed * row_mean)
    result = (up_ref[:, mine].astype(jnp.float32) + d_in).astype(g_ref.dtype)
    gbuf[...] = result
    g_ref[...] = result
    gain_out_ref[...] = jnp.sum(total * normed, axis=0, keepdims=True)

    @pl.when(sec > 0)
    def _():
        sends = []
        for t in range(n):
            copy = pltpu.make_async_remote_copy(
                src_ref=gbuf,
                dst_ref=down.at[:, mine],
                send_sem=dsend_sem.at[t],
                recv_sem=drecv_sem.at[me],
                device_id=(sec - 1, t),
                device_id_type=MESH,
            )
            copy.start()
            sends.append(copy)
        for copy in sends:
            copy.wait_send()

    @pl.when(sec < n_sec - 1)
    def _():
        for src in range(n):
            pltpu.make_async_remote_copy(
                src_ref=gbuf,
                dst_ref=down.at[:, pl.ds(src * width, width)],
                send_sem=dsend_sem.at[src],
                recv_sem=drecv_sem.at[src],
                device_id=(sec + 1, src),
                device_id_type=MESH,
            ).wait_recv()
        next_ref[...] = down[...]

    @pl.when(sec == n_sec - 1)
    def _():
        next_ref[...] = jnp.zeros_like(next_ref)


def layer_exchange(partial, stats, normed, inv_rms, gain_own, upstream, n, n_sec, width):
    rows = partial.shape[0]
    vmem = pl.BlockSpec(memory_space=pltpu.VMEM)
    return pl.pallas_call(
        functools.partial(layer_exchange_kernel, n, n_sec, width),
        out_shape=(
            jax.ShapeDtypeStruct((rows, width), jnp.bfloat16),
            jax.ShapeDtypeStruct((rows, n * width), jnp.bfloat16),
            jax.ShapeDtypeStruct((1, width), jnp.float32),
        ),
        in_specs=[vmem] * 6,
        out_specs=(vmem, vmem, vmem),
        scratch_shapes=[
            pltpu.VMEM((n, rows, width), partial.dtype),
            pltpu.VMEM((n, *stats.shape), jnp.float32),
            pltpu.VMEM((rows, width), jnp.bfloat16),
            pltpu.VMEM((rows, n * width), jnp.bfloat16),
            pltpu.SemaphoreType.DMA((n,)),
            pltpu.SemaphoreType.DMA((n,)),
            pltpu.SemaphoreType.DMA((n,)),
            pltpu.SemaphoreType.DMA((n,)),
            pltpu.SemaphoreType.DMA((n,)),
            pltpu.SemaphoreType.DMA((n,)),
        ],
        compiler_params=pltpu.CompilerParams(
            collective_id=2, has_side_effects=True, vmem_limit_bytes=16 * 1024 * 1024
        ),
    )(partial, stats, normed, inv_rms, gain_own, upstream)


def conv_block(weights, ext_vals, tail_rows, d_act):
    kernel_width = weights.shape[0]
    length = d_act.shape[0]
    pre_act = jnp.zeros_like(d_act)
    for lag_idx in range(kernel_width):
        start = kernel_width - 1 - lag_idx
        pre_act = pre_act + weights[lag_idx] * ext_vals[start : start + length]
    gate_sig = jax.nn.sigmoid(pre_act)
    d_pre = d_act * gate_sig * (1.0 + pre_act * (1.0 - gate_sig))
    padded_back = jnp.concatenate([d_pre, tail_rows], axis=0)
    d_vals = jnp.zeros_like(d_pre)
    for lag_idx in range(kernel_width):
        d_vals = d_vals + weights[lag_idx] * padded_back[lag_idx : lag_idx + length]
    lag_grads = jnp.stack(
        [
            jnp.sum(
                d_pre * ext_vals[kernel_width - 1 - lag_idx : kernel_width - 1 - lag_idx + length],
                axis=0,
            )
            for lag_idx in range(kernel_width)
        ]
    )
    return (d_vals.astype(jnp.bfloat16), lag_grads, d_pre[: kernel_width - 1])


def local(dy_top, loss_mask, counts, layer_in, conv_in, norm_gain, conv_weight, in_proj, out_proj):
    sections = lax.axis_size("section")
    tensors = lax.axis_size("tensor")
    section_idx = lax.axis_index("section")
    tensor_idx = lax.axis_index("tensor")
    batches, seq_len, model_width = dy_top.shape
    width = model_width // tensors
    gain_vec = norm_gain[0]
    weights = conv_weight[0]
    kernel_width = weights.shape[0]
    local_channels = weights.shape[1]
    w_in = in_proj[0]
    w_out = out_proj[0]
    conv_padded = jnp.pad(conv_in[0], ((0, 0), (kernel_width - 1, 0), (0, 0)))
    positions = jnp.arange(seq_len, dtype=jnp.int32)
    keep_mask = (loss_mask == 1) & (positions[None, :] < counts[:, None])
    top_grads = jnp.where(keep_mask[:, :, None], dy_top, jnp.zeros_like(dy_top))
    is_last = section_idx == sections - 1
    contract = (((1,), (1,)), ((), ()))

    values = layer_in[0].astype(jnp.float32)
    inv_rms_all = lax.rsqrt(jnp.mean(values * values, axis=-1, keepdims=True) + EPSILON)
    normed_all = values * inv_rms_all
    gain_own = lax.dynamic_slice(gain_vec, (tensor_idx * width,), (width,))
    normed_own_all = lax.dynamic_slice(normed_all, (0, 0, tensor_idx * width), (batches, seq_len, width))

    halves = CHUNKS_PER_BATCH
    chunk_len = seq_len // halves
    n_chunks = batches * halves
    total_steps = sections + n_chunks - 1

    def pick_block(step_idx):
        block_raw = step_idx - (sections - 1 - section_idx)
        active = (block_raw >= 0) & (block_raw < n_chunks)
        block_now = jnp.clip(block_raw, 0, n_chunks - 1)
        within = lax.rem(block_now, halves)
        return (block_now // halves, halves - 1 - within, within > 0, active)

    def rows_of(array, batch_slot, first_row, row_count):
        return lax.dynamic_slice(array, (batch_slot, first_row, 0), (1, row_count, array.shape[2]))[0]

    tail_init = jnp.zeros((kernel_width - 1, local_channels), jnp.float32)

    def step_rows(step_idx, loop_state):
        incoming, results, gain_acc, conv_acc, tail_carry = loop_state
        batch_slot, half_now, join_now, active = pick_block(step_idx)
        row_start = half_now * chunk_len
        full_chunk = jnp.where(is_last, rows_of(top_grads, batch_slot, row_start, chunk_len), incoming)
        d_act = matmul_nt(full_chunk, w_out, w_out.shape[0], 2048, jnp.float32)
        ext_vals = lax.dynamic_slice(
            conv_padded, (batch_slot, row_start, 0), (1, chunk_len + kernel_width - 1, local_channels)
        )[0].astype(jnp.float32)
        tail_rows = jnp.where(join_now, tail_carry, 0.0)
        d_vals, conv_part, new_tail = conv_block(weights, ext_vals, tail_rows, d_act)
        partial = lax.dot_general(d_vals, w_in, contract, preferred_element_type=jnp.float32).astype(jnp.bfloat16)
        normed = rows_of(normed_all, batch_slot, row_start, chunk_len)
        inv_rms = rows_of(inv_rms_all, batch_slot, row_start, chunk_len)
        row_part = jnp.sum(partial.astype(jnp.float32) * gain_vec * normed, axis=-1)
        stats = jnp.zeros((chunk_len, 128), jnp.float32).at[:, 0].set(row_part)
        normed_own = rows_of(normed_own_all, batch_slot, row_start, chunk_len)
        grad_out, incoming_next, gain_part = layer_exchange(
            partial, stats, normed_own, inv_rms, gain_own[None, :], full_chunk, tensors, sections, width
        )
        gain_part = gain_part[0]
        previous = lax.dynamic_slice(results, (batch_slot, half_now, 0, 0), (1, 1, chunk_len, width))
        updated = jnp.where(active, grad_out[None, None], previous)
        results = lax.dynamic_update_slice(results, updated, (batch_slot, half_now, 0, 0))
        gain_acc = gain_acc + jnp.where(active, gain_part, 0.0)
        conv_acc = conv_acc + jnp.where(active, conv_part, 0.0)
        tail_carry = jnp.where(active, new_tail, tail_carry)
        incoming = incoming_next
        return (incoming, results, gain_acc, conv_acc, tail_carry)

    initial = (
        jnp.zeros((chunk_len, model_width), jnp.bfloat16),
        jnp.zeros((batches, halves, chunk_len, width), jnp.bfloat16),
        jnp.zeros((width,), jnp.float32),
        jnp.zeros(weights.shape, jnp.float32),
        tail_init,
    )
    last_state = lax.fori_loop(0, total_steps, step_rows, initial)
    gathered = sent_to_all(last_state[1], "tensor")
    results = jnp.transpose(gathered, (1, 2, 3, 0, 4)).reshape(batches, seq_len, model_width)
    conv_acc = last_state[3]
    gain_total = sent_to_all(last_state[2], "tensor").reshape(model_width)
    return (results[None], gain_total[None], conv_acc[None])


def solution(mesh):
    placed = (
        P(),
        P(),
        P(),
        P("section", None, None, None),
        P("section", None, None, "tensor"),
        P("section", None),
        P("section", None, "tensor"),
        P("section", None, "tensor"),
        P("section", "tensor", None),
    )
    return jax.shard_map(
        local,
        mesh=mesh,
        in_specs=placed,
        out_specs=(
            P("section", None, None, None),
            P("section", None),
            P("section", None, "tensor"),
        ),
        check_vma=False,
    )
```

```python
import functools

import jax
import jax.numpy as jnp
from jax import lax
from jax.experimental import pallas as pl
from jax.experimental.pallas import tpu as pltpu
from jax.sharding import PartitionSpec as P

EPSILON = 1e-05
MESH = pl.DeviceIdType.MESH
CHUNKS_PER_BATCH = 2


def sent_to_all(x, axis):
    copies = jnp.broadcast_to(x, (lax.axis_size(axis), *x.shape))
    return lax.all_to_all(copies, axis, split_axis=0, concat_axis=0, tiled=True)


def matmul_nt_kernel(x_ref, w_ref, out_ref):
    product = lax.dot_general(
        x_ref[...], w_ref[...], (((1,), (1,)), ((), ())), preferred_element_type=jnp.float32
    )

    @pl.when(pl.program_id(1) == 0)
    def _():
        out_ref[...] = product.astype(out_ref.dtype)

    @pl.when(pl.program_id(1) > 0)
    def _():
        out_ref[...] += product.astype(out_ref.dtype)


def matmul_nt(x, w, block_n, block_k, out_dtype):
    rows, depth = x.shape
    cols = w.shape[0]
    grid = (cols // block_n, depth // block_k)
    return pl.pallas_call(
        matmul_nt_kernel,
        out_shape=jax.ShapeDtypeStruct((rows, cols), out_dtype),
        grid=grid,
        in_specs=[
            pl.BlockSpec((rows, block_k), lambda n, k: (0, k)),
            pl.BlockSpec((block_n, block_k), lambda n, k: (n, k)),
        ],
        out_specs=pl.BlockSpec((rows, block_n), lambda n, k: (0, n)),
        compiler_params=pltpu.CompilerParams(
            dimension_semantics=("arbitrary", "arbitrary"), vmem_limit_bytes=16 * 1024 * 1024
        ),
        cost_estimate=pl.CostEstimate(
            flops=2 * rows * cols * depth,
            bytes_accessed=2 * (rows * depth + cols * depth) + rows * cols * jnp.dtype(out_dtype).itemsize,
            transcendentals=0,
        ),
    )(x, w)


def layer_exchange_kernel(
    n, n_sec, width, x_ref, s_ref, normed_ref, inv_ref, gain_ref, up_ref,
    g_ref, next_ref, gain_out_ref,
    recv, srecv, gbuf, down, send_sem, recv_sem, ssend_sem, srecv_sem, dsend_sem, drecv_sem,
):
    me = lax.axis_index("tensor")
    sec = lax.axis_index("section")
    barrier = pltpu.get_barrier_semaphore()
    for k in range(1, n):
        pl.semaphore_signal(barrier, inc=1, device_id=(sec, lax.rem(me + k, n)), device_id_type=MESH)

    @pl.when(sec < n_sec - 1)
    def _():
        for t in range(n):
            pl.semaphore_signal(barrier, inc=1, device_id=(sec + 1, t), device_id_type=MESH)

    @pl.when(sec > 0)
    def _():
        pl.semaphore_wait(barrier, 2 * n - 1)

    @pl.when(sec == 0)
    def _():
        pl.semaphore_wait(barrier, n - 1)

    copies = []
    for k in range(1, n):
        peer = lax.rem(me + k, n)
        cols = pl.ds(pl.multiple_of(peer * width, 128), width)
        block = pltpu.make_async_remote_copy(
            src_ref=x_ref.at[:, cols],
            dst_ref=recv.at[me],
            send_sem=send_sem.at[k],
            recv_sem=recv_sem.at[k],
            device_id=(sec, peer),
            device_id_type=MESH,
        )
        block.start()
        stat = pltpu.make_async_remote_copy(
            src_ref=s_ref,
            dst_ref=srecv.at[me],
            send_sem=ssend_sem.at[k],
            recv_sem=srecv_sem.at[k],
            device_id=(sec, peer),
            device_id_type=MESH,
        )
        stat.start()
        copies.append((block, stat))
    for block, stat in copies:
        block.wait()
        stat.wait()
    mine = pl.ds(pl.multiple_of(me * width, 128), width)
    total = x_ref[:, mine].astype(jnp.float32)
    stat_total = s_ref[...]
    for k in range(1, n):
        src = lax.rem(me + n - k, n)
        total = total + recv[src].astype(jnp.float32)
        stat_total = stat_total + srecv[src]
    rows = total.shape[0]
    row_mean = stat_total[:, 0:1] * (1.0 / (n * width))
    normed = normed_ref[...]
    d_in = inv_ref[...] * (total * gain_ref[...] - normed * row_mean)
    result = (up_ref[:, mine].astype(jnp.float32) + d_in).astype(g_ref.dtype)
    gbuf[...] = result
    g_ref[...] = result
    gain_out_ref[...] = jnp.sum(total * normed, axis=0, keepdims=True)

    @pl.when(sec > 0)
    def _():
        sends = []
        for t in range(n):
            copy = pltpu.make_async_remote_copy(
                src_ref=gbuf,
                dst_ref=down.at[:, mine],
                send_sem=dsend_sem.at[t],
                recv_sem=drecv_sem.at[me],
                device_id=(sec - 1, t),
                device_id_type=MESH,
            )
            copy.start()
            sends.append(copy)
        for copy in sends:
            copy.wait_send()

    @pl.when(sec < n_sec - 1)
    def _():
        for src in range(n):
            pltpu.make_async_remote_copy(
                src_ref=gbuf,
                dst_ref=down.at[:, pl.ds(src * width, width)],
                send_sem=dsend_sem.at[src],
                recv_sem=drecv_sem.at[src],
                device_id=(sec + 1, src),
                device_id_type=MESH,
            ).wait_recv()
        next_ref[...] = down[...]

    @pl.when(sec == n_sec - 1)
    def _():
        next_ref[...] = jnp.zeros_like(next_ref)


def layer_exchange(partial, stats, normed, inv_rms, gain_own, upstream, n, n_sec, width):
    rows = partial.shape[0]
    vmem = pl.BlockSpec(memory_space=pltpu.VMEM)
    return pl.pallas_call(
        functools.partial(layer_exchange_kernel, n, n_sec, width),
        out_shape=(
            jax.ShapeDtypeStruct((rows, width), jnp.bfloat16),
            jax.ShapeDtypeStruct((rows, n * width), jnp.bfloat16),
            jax.ShapeDtypeStruct((1, width), jnp.float32),
        ),
        in_specs=[vmem] * 6,
        out_specs=(vmem, vmem, vmem),
        scratch_shapes=[
            pltpu.VMEM((n, rows, width), partial.dtype),
            pltpu.VMEM((n, *stats.shape), jnp.float32),
            pltpu.VMEM((rows, width), jnp.bfloat16),
            pltpu.VMEM((rows, n * width), jnp.bfloat16),
            pltpu.SemaphoreType.DMA((n,)),
            pltpu.SemaphoreType.DMA((n,)),
            pltpu.SemaphoreType.DMA((n,)),
            pltpu.SemaphoreType.DMA((n,)),
            pltpu.SemaphoreType.DMA((n,)),
            pltpu.SemaphoreType.DMA((n,)),
        ],
        compiler_params=pltpu.CompilerParams(
            collective_id=2, has_side_effects=True, vmem_limit_bytes=16 * 1024 * 1024
        ),
    )(partial, stats, normed, inv_rms, gain_own, upstream)


def conv_block(weights, ext_vals, tail_rows, d_act):
    kernel_width = weights.shape[0]
    length = d_act.shape[0]
    pre_act = jnp.zeros_like(d_act)
    for lag_idx in range(kernel_width):
        start = kernel_width - 1 - lag_idx
        pre_act = pre_act + weights[lag_idx] * ext_vals[start : start + length]
    gate_sig = jax.nn.sigmoid(pre_act)
    d_pre = d_act * gate_sig * (1.0 + pre_act * (1.0 - gate_sig))
    padded_back = jnp.concatenate([d_pre, tail_rows], axis=0)
    d_vals = jnp.zeros_like(d_pre)
    for lag_idx in range(kernel_width):
        d_vals = d_vals + weights[lag_idx] * padded_back[lag_idx : lag_idx + length]
    lag_grads = jnp.stack(
        [
            jnp.sum(
                d_pre * ext_vals[kernel_width - 1 - lag_idx : kernel_width - 1 - lag_idx + length],
                axis=0,
            )
            for lag_idx in range(kernel_width)
        ]
    )
    return (d_vals.astype(jnp.bfloat16), lag_grads, d_pre[: kernel_width - 1])


def local(dy_top, loss_mask, counts, layer_in, conv_in, norm_gain, conv_weight, in_proj, out_proj):
    sections = lax.axis_size("section")
    tensors = lax.axis_size("tensor")
    section_idx = lax.axis_index("section")
    tensor_idx = lax.axis_index("tensor")
    batches, seq_len, model_width = dy_top.shape
    width = model_width // tensors
    gain_vec = norm_gain[0]
    weights = conv_weight[0]
    kernel_width = weights.shape[0]
    local_channels = weights.shape[1]
    w_in = in_proj[0]
    w_out = out_proj[0]
    conv_padded = jnp.pad(conv_in[0], ((0, 0), (kernel_width - 1, 0), (0, 0)))
    positions = jnp.arange(seq_len, dtype=jnp.int32)
    keep_mask = (loss_mask == 1) & (positions[None, :] < counts[:, None])
    top_grads = jnp.where(keep_mask[:, :, None], dy_top, jnp.zeros_like(dy_top))
    is_last = section_idx == sections - 1
    contract = (((1,), (1,)), ((), ()))

    values = layer_in[0].astype(jnp.float32)
    inv_rms_all = lax.rsqrt(jnp.mean(values * values, axis=-1, keepdims=True) + EPSILON)
    normed_all = values * inv_rms_all
    gain_own = lax.dynamic_slice(gain_vec, (tensor_idx * width,), (width,))
    normed_own_all = lax.dynamic_slice(normed_all, (0, 0, tensor_idx * width), (batches, seq_len, width))

    halves = CHUNKS_PER_BATCH
    chunk_len = seq_len // halves
    n_chunks = batches * halves
    total_steps = sections + n_chunks - 1

    def pick_block(step_idx):
        block_raw = step_idx - (sections - 1 - section_idx)
        active = (block_raw >= 0) & (block_raw < n_chunks)
        block_now = jnp.clip(block_raw, 0, n_chunks - 1)
        within = lax.rem(block_now, halves)
        return (block_now // halves, halves - 1 - within, within > 0, active)

    def rows_of(array, batch_slot, first_row, row_count):
        return lax.dynamic_slice(array, (batch_slot, first_row, 0), (1, row_count, array.shape[2]))[0]

    tail_init = jnp.zeros((kernel_width - 1, local_channels), jnp.float32)

    def step_rows(step_idx, loop_state):
        incoming, results, gain_acc, conv_acc, tail_carry = loop_state
        batch_slot, half_now, join_now, active = pick_block(step_idx)
        row_start = half_now * chunk_len
        full_chunk = jnp.where(is_last, rows_of(top_grads, batch_slot, row_start, chunk_len), incoming)
        d_act = matmul_nt(full_chunk, w_out, w_out.shape[0], 2048, jnp.float32)
        ext_vals = lax.dynamic_slice(
            conv_padded, (batch_slot, row_start, 0), (1, chunk_len + kernel_width - 1, local_channels)
        )[0].astype(jnp.float32)
        tail_rows = jnp.where(join_now, tail_carry, 0.0)
        d_vals, conv_part, new_tail = conv_block(weights, ext_vals, tail_rows, d_act)
        partial = lax.dot_general(d_vals, w_in, contract, preferred_element_type=jnp.float32).astype(jnp.bfloat16)
        normed = rows_of(normed_all, batch_slot, row_start, chunk_len)
        inv_rms = rows_of(inv_rms_all, batch_slot, row_start, chunk_len)
        row_part = jnp.sum(partial.astype(jnp.float32) * gain_vec * normed, axis=-1)
        stats = jnp.zeros((chunk_len, 128), jnp.float32).at[:, 0].set(row_part)
        normed_own = rows_of(normed_own_all, batch_slot, row_start, chunk_len)
        grad_out, incoming_next, gain_part = layer_exchange(
            partial, stats, normed_own, inv_rms, gain_own[None, :], full_chunk, tensors, sections, width
        )
        gain_part = gain_part[0]
        previous = lax.dynamic_slice(results, (batch_slot, half_now, 0, 0), (1, 1, chunk_len, width))
        updated = jnp.where(active, grad_out[None, None], previous)
        results = lax.dynamic_update_slice(results, updated, (batch_slot, half_now, 0, 0))
        gain_acc = gain_acc + jnp.where(active, gain_part, 0.0)
        conv_acc = conv_acc + jnp.where(active, conv_part, 0.0)
        tail_carry = jnp.where(active, new_tail, tail_carry)
        incoming = incoming_next
        return (incoming, results, gain_acc, conv_acc, tail_carry)

    initial = (
        jnp.zeros((chunk_len, model_width), jnp.bfloat16),
        jnp.zeros((batches, halves, chunk_len, width), jnp.bfloat16),
        jnp.zeros((width,), jnp.float32),
        jnp.zeros(weights.shape, jnp.float32),
        tail_init,
    )
    last_state = lax.fori_loop(0, total_steps, step_rows, initial)
    own = last_state[1].reshape(batches, seq_len, width)
    copies = jnp.broadcast_to(own, (tensors, batches, seq_len, width))
    results = lax.all_to_all(copies, "tensor", split_axis=0, concat_axis=3, tiled=True)[0]
    conv_acc = last_state[3]
    gain_total = sent_to_all(last_state[2], "tensor").reshape(model_width)
    return (results[None], gain_total[None], conv_acc[None])


def solution(mesh):
    placed = (
        P(),
        P(),
        P(),
        P("section", None, None, None),
        P("section", None, None, "tensor"),
        P("section", None),
        P("section", None, "tensor"),
        P("section", None, "tensor"),
        P("section", "tensor", None),
    )
    return jax.shard_map(
        local,
        mesh=mesh,
        in_specs=placed,
        out_specs=(
            P("section", None, None, None),
            P("section", None),
            P("section", None, "tensor"),
        ),
        check_vma=False,
    )
```

```python
import functools

import jax
import jax.numpy as jnp
from jax import lax
from jax.experimental import pallas as pl
from jax.experimental.pallas import tpu as pltpu
from jax.sharding import PartitionSpec as P

EPSILON = 1e-05
MESH = pl.DeviceIdType.MESH
CHUNKS_PER_BATCH = 2


def sent_to_all(x, axis):
    copies = jnp.broadcast_to(x, (lax.axis_size(axis), *x.shape))
    return lax.all_to_all(copies, axis, split_axis=0, concat_axis=0, tiled=True)


def matmul_nt_kernel(x_ref, w_ref, out_ref):
    product = lax.dot_general(
        x_ref[...], w_ref[...], (((1,), (1,)), ((), ())), preferred_element_type=jnp.float32
    )

    @pl.when(pl.program_id(1) == 0)
    def _():
        out_ref[...] = product.astype(out_ref.dtype)

    @pl.when(pl.program_id(1) > 0)
    def _():
        out_ref[...] += product.astype(out_ref.dtype)


def matmul_nt(x, w, block_n, block_k, out_dtype):
    rows, depth = x.shape
    cols = w.shape[0]
    grid = (cols // block_n, depth // block_k)
    return pl.pallas_call(
        matmul_nt_kernel,
        out_shape=jax.ShapeDtypeStruct((rows, cols), out_dtype),
        grid=grid,
        in_specs=[
            pl.BlockSpec((rows, block_k), lambda n, k: (0, k)),
            pl.BlockSpec((block_n, block_k), lambda n, k: (n, k)),
        ],
        out_specs=pl.BlockSpec((rows, block_n), lambda n, k: (0, n)),
        compiler_params=pltpu.CompilerParams(
            dimension_semantics=("arbitrary", "arbitrary"), vmem_limit_bytes=16 * 1024 * 1024
        ),
        cost_estimate=pl.CostEstimate(
            flops=2 * rows * cols * depth,
            bytes_accessed=2 * (rows * depth + cols * depth) + rows * cols * jnp.dtype(out_dtype).itemsize,
            transcendentals=0,
        ),
    )(x, w)


def layer_exchange_kernel(
    n, n_sec, width, x_ref, s_ref, normed_ref, inv_ref, gain_ref, up_ref,
    g_ref, next_ref, gain_out_ref,
    recv, srecv, gbuf, down, send_sem, recv_sem, ssend_sem, srecv_sem, dsend_sem, drecv_sem,
):
    me = lax.axis_index("tensor")
    sec = lax.axis_index("section")
    barrier = pltpu.get_barrier_semaphore()
    for k in range(1, n):
        pl.semaphore_signal(barrier, inc=1, device_id=(sec, lax.rem(me + k, n)), device_id_type=MESH)

    @pl.when(sec < n_sec - 1)
    def _():
        for t in range(n):
            pl.semaphore_signal(barrier, inc=1, device_id=(sec + 1, t), device_id_type=MESH)

    @pl.when(sec > 0)
    def _():
        pl.semaphore_wait(barrier, 2 * n - 1)

    @pl.when(sec == 0)
    def _():
        pl.semaphore_wait(barrier, n - 1)

    copies = []
    for k in range(1, n):
        peer = lax.rem(me + k, n)
        cols = pl.ds(pl.multiple_of(peer * width, 128), width)
        block = pltpu.make_async_remote_copy(
            src_ref=x_ref.at[:, cols],
            dst_ref=recv.at[me],
            send_sem=send_sem.at[k],
            recv_sem=recv_sem.at[k],
            device_id=(sec, peer),
            device_id_type=MESH,
        )
        block.start()
        stat = pltpu.make_async_remote_copy(
            src_ref=s_ref,
            dst_ref=srecv.at[me],
            send_sem=ssend_sem.at[k],
            recv_sem=srecv_sem.at[k],
            device_id=(sec, peer),
            device_id_type=MESH,
        )
        stat.start()
        copies.append((block, stat))
    for block, stat in copies:
        block.wait()
        stat.wait()
    mine = pl.ds(pl.multiple_of(me * width, 128), width)
    total = x_ref[:, mine].astype(jnp.float32)
    stat_total = s_ref[...]
    for k in range(1, n):
        src = lax.rem(me + n - k, n)
        total = total + recv[src].astype(jnp.float32)
        stat_total = stat_total + srecv[src]
    rows = total.shape[0]
    row_mean = stat_total[:, 0:1] * (1.0 / (n * width))
    normed = normed_ref[...]
    d_in = inv_ref[...] * (total * gain_ref[...] - normed * row_mean)
    result = (up_ref[:, mine].astype(jnp.float32) + d_in).astype(g_ref.dtype)
    gbuf[...] = result
    g_ref[...] = result
    gain_out_ref[...] = jnp.sum(total * normed, axis=0, keepdims=True)

    @pl.when(sec > 0)
    def _():
        sends = []
        for t in range(n):
            copy = pltpu.make_async_remote_copy(
                src_ref=gbuf,
                dst_ref=down.at[:, mine],
                send_sem=dsend_sem.at[t],
                recv_sem=drecv_sem.at[me],
                device_id=(sec - 1, t),
                device_id_type=MESH,
            )
            copy.start()
            sends.append(copy)
        for copy in sends:
            copy.wait_send()

    @pl.when(sec < n_sec - 1)
    def _():
        for src in range(n):
            pltpu.make_async_remote_copy(
                src_ref=gbuf,
                dst_ref=down.at[:, pl.ds(src * width, width)],
                send_sem=dsend_sem.at[src],
                recv_sem=drecv_sem.at[src],
                device_id=(sec + 1, src),
                device_id_type=MESH,
            ).wait_recv()
        next_ref[...] = down[...]

    @pl.when(sec == n_sec - 1)
    def _():
        next_ref[...] = jnp.zeros_like(next_ref)


def layer_exchange(partial, stats, normed, inv_rms, gain_own, upstream, n, n_sec, width):
    rows = partial.shape[0]
    vmem = pl.BlockSpec(memory_space=pltpu.VMEM)
    return pl.pallas_call(
        functools.partial(layer_exchange_kernel, n, n_sec, width),
        out_shape=(
            jax.ShapeDtypeStruct((rows, width), jnp.bfloat16),
            jax.ShapeDtypeStruct((rows, n * width), jnp.bfloat16),
            jax.ShapeDtypeStruct((1, width), jnp.float32),
        ),
        in_specs=[vmem] * 6,
        out_specs=(vmem, vmem, vmem),
        scratch_shapes=[
            pltpu.VMEM((n, rows, width), partial.dtype),
            pltpu.VMEM((n, *stats.shape), jnp.float32),
            pltpu.VMEM((rows, width), jnp.bfloat16),
            pltpu.VMEM((rows, n * width), jnp.bfloat16),
            pltpu.SemaphoreType.DMA((n,)),
            pltpu.SemaphoreType.DMA((n,)),
            pltpu.SemaphoreType.DMA((n,)),
            pltpu.SemaphoreType.DMA((n,)),
            pltpu.SemaphoreType.DMA((n,)),
            pltpu.SemaphoreType.DMA((n,)),
        ],
        compiler_params=pltpu.CompilerParams(
            collective_id=2, has_side_effects=True, vmem_limit_bytes=16 * 1024 * 1024
        ),
    )(partial, stats, normed, inv_rms, gain_own, upstream)


def conv_block(weights, ext_vals, tail_rows, d_act):
    kernel_width = weights.shape[0]
    length = d_act.shape[0]
    pre_act = jnp.zeros_like(d_act)
    for lag_idx in range(kernel_width):
        start = kernel_width - 1 - lag_idx
        pre_act = pre_act + weights[lag_idx] * ext_vals[start : start + length]
    gate_sig = jax.nn.sigmoid(pre_act)
    d_pre = d_act * gate_sig * (1.0 + pre_act * (1.0 - gate_sig))
    padded_back = jnp.concatenate([d_pre, tail_rows], axis=0)
    d_vals = jnp.zeros_like(d_pre)
    for lag_idx in range(kernel_width):
        d_vals = d_vals + weights[lag_idx] * padded_back[lag_idx : lag_idx + length]
    lag_grads = jnp.stack(
        [
            jnp.sum(
                d_pre * ext_vals[kernel_width - 1 - lag_idx : kernel_width - 1 - lag_idx + length],
                axis=0,
            )
            for lag_idx in range(kernel_width)
        ]
    )
    return (d_vals.astype(jnp.bfloat16), lag_grads, d_pre[: kernel_width - 1])


def local(dy_top, loss_mask, counts, layer_in, conv_in, norm_gain, conv_weight, in_proj, out_proj):
    sections = lax.axis_size("section")
    tensors = lax.axis_size("tensor")
    section_idx = lax.axis_index("section")
    tensor_idx = lax.axis_index("tensor")
    batches, seq_len, model_width = dy_top.shape
    width = model_width // tensors
    gain_vec = norm_gain[0]
    weights = conv_weight[0]
    kernel_width = weights.shape[0]
    local_channels = weights.shape[1]
    w_in = in_proj[0]
    w_out = out_proj[0]
    conv_padded = jnp.pad(conv_in[0], ((0, 0), (kernel_width - 1, 0), (0, 0)))
    positions = jnp.arange(seq_len, dtype=jnp.int32)
    keep_mask = (loss_mask == 1) & (positions[None, :] < counts[:, None])
    top_grads = jnp.where(keep_mask[:, :, None], dy_top, jnp.zeros_like(dy_top))
    is_last = section_idx == sections - 1
    contract = (((1,), (1,)), ((), ()))

    values = layer_in[0].astype(jnp.float32)
    inv_rms_all = lax.rsqrt(jnp.mean(values * values, axis=-1, keepdims=True) + EPSILON)
    normed_all = values * inv_rms_all
    gain_own = lax.dynamic_slice(gain_vec, (tensor_idx * width,), (width,))
    normed_own_all = lax.dynamic_slice(normed_all, (0, 0, tensor_idx * width), (batches, seq_len, width))

    halves = CHUNKS_PER_BATCH
    chunk_len = seq_len // halves
    n_chunks = batches * halves
    total_steps = sections + n_chunks - 1

    def pick_block(step_idx):
        block_raw = step_idx - (sections - 1 - section_idx)
        active = (block_raw >= 0) & (block_raw < n_chunks)
        block_now = jnp.clip(block_raw, 0, n_chunks - 1)
        within = lax.rem(block_now, halves)
        return (block_now // halves, halves - 1 - within, within > 0, active)

    def rows_of(array, batch_slot, first_row, row_count):
        return lax.dynamic_slice(array, (batch_slot, first_row, 0), (1, row_count, array.shape[2]))[0]

    tail_init = jnp.zeros((kernel_width - 1, local_channels), jnp.float32)

    def step_rows(step_idx, loop_state):
        incoming, results, gain_acc, conv_acc, tail_carry = loop_state
        batch_slot, half_now, join_now, active = pick_block(step_idx)
        row_start = half_now * chunk_len
        full_chunk = jnp.where(is_last, rows_of(top_grads, batch_slot, row_start, chunk_len), incoming)
        d_act = matmul_nt(full_chunk, w_out, w_out.shape[0], 2048, jnp.float32)
        ext_vals = lax.dynamic_slice(
            conv_padded, (batch_slot, row_start, 0), (1, chunk_len + kernel_width - 1, local_channels)
        )[0].astype(jnp.float32)
        tail_rows = jnp.where(join_now, tail_carry, 0.0)
        d_vals, conv_part, new_tail = conv_block(weights, ext_vals, tail_rows, d_act)
        partial = lax.dot_general(d_vals, w_in, contract, preferred_element_type=jnp.float32).astype(jnp.bfloat16)
        normed = rows_of(normed_all, batch_slot, row_start, chunk_len)
        inv_rms = rows_of(inv_rms_all, batch_slot, row_start, chunk_len)
        row_part = jnp.sum(partial.astype(jnp.float32) * gain_vec * normed, axis=-1)
        stats = jnp.zeros((chunk_len, 128), jnp.float32).at[:, 0].set(row_part)
        normed_own = rows_of(normed_own_all, batch_slot, row_start, chunk_len)
        grad_out, incoming_next, gain_part = layer_exchange(
            partial, stats, normed_own, inv_rms, gain_own[None, :], full_chunk, tensors, sections, width
        )
        gain_part = gain_part[0]
        previous = lax.dynamic_slice(results, (batch_slot, half_now, 0, 0), (1, 1, chunk_len, width))
        updated = jnp.where(active, grad_out[None, None], previous)
        results = lax.dynamic_update_slice(results, updated, (batch_slot, half_now, 0, 0))
        gain_acc = gain_acc + jnp.where(active, gain_part, 0.0)
        conv_acc = conv_acc + jnp.where(active, conv_part, 0.0)
        tail_carry = jnp.where(active, new_tail, tail_carry)
        incoming = incoming_next
        return (incoming, results, gain_acc, conv_acc, tail_carry)

    initial = (
        jnp.zeros((chunk_len, model_width), jnp.bfloat16),
        jnp.zeros((batches, halves, chunk_len, width), jnp.bfloat16),
        jnp.zeros((width,), jnp.float32),
        jnp.zeros(weights.shape, jnp.float32),
        tail_init,
    )
    last_state = lax.fori_loop(0, total_steps, step_rows, initial)
    own = last_state[1].reshape(batches * seq_len, width)
    gain_hi = last_state[2].astype(jnp.bfloat16)
    gain_lo = (last_state[2] - gain_hi.astype(jnp.float32)).astype(jnp.bfloat16)
    extra = jnp.zeros((16, width), jnp.bfloat16).at[0].set(gain_hi).at[1].set(gain_lo)
    own = jnp.concatenate([own, extra], axis=0)
    copies = jnp.broadcast_to(own, (tensors, *own.shape))
    gathered = lax.all_to_all(copies, "tensor", split_axis=0, concat_axis=2, tiled=True)[0]
    rows = batches * seq_len
    results = gathered[:rows].reshape(batches, seq_len, model_width)
    gain_total = gathered[rows].astype(jnp.float32) + gathered[rows + 1].astype(jnp.float32)
    conv_acc = last_state[3]
    return (results[None], gain_total[None], conv_acc[None])


def solution(mesh):
    placed = (
        P(),
        P(),
        P(),
        P("section", None, None, None),
        P("section", None, None, "tensor"),
        P("section", None),
        P("section", None, "tensor"),
        P("section", None, "tensor"),
        P("section", "tensor", None),
    )
    return jax.shard_map(
        local,
        mesh=mesh,
        in_specs=placed,
        out_specs=(
            P("section", None, None, None),
            P("section", None),
            P("section", None, "tensor"),
        ),
        check_vma=False,
    )
```

```python
import functools

import jax
import jax.numpy as jnp
from jax import lax
from jax.experimental import pallas as pl
from jax.experimental.pallas import tpu as pltpu
from jax.sharding import PartitionSpec as P

EPSILON = 1e-05
MESH = pl.DeviceIdType.MESH
CHUNKS_PER_BATCH = 2


def sent_to_all(x, axis):
    copies = jnp.broadcast_to(x, (lax.axis_size(axis), *x.shape))
    return lax.all_to_all(copies, axis, split_axis=0, concat_axis=0, tiled=True)


def matmul_nt_kernel(n_sec, top_ref, x_ref, w_ref, out_ref):
    lhs = jnp.where(lax.axis_index("section") == n_sec - 1, top_ref[...], x_ref[...])
    product = lax.dot_general(lhs, w_ref[...], (((1,), (1,)), ((), ())), preferred_element_type=jnp.float32)

    @pl.when(pl.program_id(1) == 0)
    def _():
        out_ref[...] = product.astype(out_ref.dtype)

    @pl.when(pl.program_id(1) > 0)
    def _():
        out_ref[...] += product.astype(out_ref.dtype)


def matmul_nt(top, x, w, block_n, block_k, out_dtype, n_sec):
    rows, depth = x.shape
    cols = w.shape[0]
    grid = (cols // block_n, depth // block_k)
    return pl.pallas_call(
        functools.partial(matmul_nt_kernel, n_sec),
        out_shape=jax.ShapeDtypeStruct((rows, cols), out_dtype),
        grid=grid,
        in_specs=[
            pl.BlockSpec((rows, block_k), lambda n, k: (0, k)),
            pl.BlockSpec((rows, block_k), lambda n, k: (0, k)),
            pl.BlockSpec((block_n, block_k), lambda n, k: (n, k)),
        ],
        out_specs=pl.BlockSpec((rows, block_n), lambda n, k: (0, n)),
        compiler_params=pltpu.CompilerParams(
            dimension_semantics=("arbitrary", "arbitrary"), vmem_limit_bytes=16 * 1024 * 1024
        ),
        cost_estimate=pl.CostEstimate(
            flops=2 * rows * cols * depth,
            bytes_accessed=2 * (2 * rows * depth + cols * depth) + rows * cols * jnp.dtype(out_dtype).itemsize,
            transcendentals=0,
        ),
    )(top, x, w)


def layer_exchange_kernel(
    n, n_sec, width, x_ref, s_ref, normed_ref, inv_ref, gain_ref, top_ref, up_ref,
    g_ref, next_ref, gain_out_ref,
    recv, srecv, gbuf, down, send_sem, recv_sem, ssend_sem, srecv_sem, dsend_sem, drecv_sem,
):
    me = lax.axis_index("tensor")
    sec = lax.axis_index("section")
    barrier = pltpu.get_barrier_semaphore()
    for k in range(1, n):
        pl.semaphore_signal(barrier, inc=1, device_id=(sec, lax.rem(me + k, n)), device_id_type=MESH)

    @pl.when(sec < n_sec - 1)
    def _():
        for t in range(n):
            pl.semaphore_signal(barrier, inc=1, device_id=(sec + 1, t), device_id_type=MESH)

    @pl.when(sec > 0)
    def _():
        pl.semaphore_wait(barrier, 2 * n - 1)

    @pl.when(sec == 0)
    def _():
        pl.semaphore_wait(barrier, n - 1)

    copies = []
    for k in range(1, n):
        peer = lax.rem(me + k, n)
        cols = pl.ds(pl.multiple_of(peer * width, 128), width)
        block = pltpu.make_async_remote_copy(
            src_ref=x_ref.at[:, cols],
            dst_ref=recv.at[me],
            send_sem=send_sem.at[k],
            recv_sem=recv_sem.at[k],
            device_id=(sec, peer),
            device_id_type=MESH,
        )
        block.start()
        stat = pltpu.make_async_remote_copy(
            src_ref=s_ref,
            dst_ref=srecv.at[me],
            send_sem=ssend_sem.at[k],
            recv_sem=srecv_sem.at[k],
            device_id=(sec, peer),
            device_id_type=MESH,
        )
        stat.start()
        copies.append((block, stat))
    for block, stat in copies:
        block.wait()
        stat.wait()
    mine = pl.ds(pl.multiple_of(me * width, 128), width)
    total = x_ref[:, mine].astype(jnp.float32)
    stat_total = s_ref[...]
    for k in range(1, n):
        src = lax.rem(me + n - k, n)
        total = total + recv[src].astype(jnp.float32)
        stat_total = stat_total + srecv[src]
    rows = total.shape[0]
    row_mean = stat_total[:, 0:1] * (1.0 / (n * width))
    normed = normed_ref[...]
    d_in = inv_ref[...] * (total * gain_ref[...] - normed * row_mean)
    upstream = jnp.where(sec == n_sec - 1, top_ref[:, mine], up_ref[:, mine])
    result = (upstream.astype(jnp.float32) + d_in).astype(g_ref.dtype)
    gbuf[...] = result
    g_ref[...] = result
    gain_out_ref[...] = jnp.sum(total * normed, axis=0, keepdims=True)

    @pl.when(sec > 0)
    def _():
        sends = []
        for t in range(n):
            copy = pltpu.make_async_remote_copy(
                src_ref=gbuf,
                dst_ref=down.at[:, mine],
                send_sem=dsend_sem.at[t],
                recv_sem=drecv_sem.at[me],
                device_id=(sec - 1, t),
                device_id_type=MESH,
            )
            copy.start()
            sends.append(copy)
        for copy in sends:
            copy.wait_send()

    @pl.when(sec < n_sec - 1)
    def _():
        for src in range(n):
            pltpu.make_async_remote_copy(
                src_ref=gbuf,
                dst_ref=down.at[:, pl.ds(src * width, width)],
                send_sem=dsend_sem.at[src],
                recv_sem=drecv_sem.at[src],
                device_id=(sec + 1, src),
                device_id_type=MESH,
            ).wait_recv()
        next_ref[...] = down[...]

    @pl.when(sec == n_sec - 1)
    def _():
        next_ref[...] = jnp.zeros_like(next_ref)


def layer_exchange(partial, stats, normed, inv_rms, gain_own, top, upstream, n, n_sec, width):
    rows = partial.shape[0]
    vmem = pl.BlockSpec(memory_space=pltpu.VMEM)
    return pl.pallas_call(
        functools.partial(layer_exchange_kernel, n, n_sec, width),
        out_shape=(
            jax.ShapeDtypeStruct((rows, width), jnp.bfloat16),
            jax.ShapeDtypeStruct((rows, n * width), jnp.bfloat16),
            jax.ShapeDtypeStruct((1, width), jnp.float32),
        ),
        in_specs=[vmem] * 7,
        out_specs=(vmem, vmem, vmem),
        scratch_shapes=[
            pltpu.VMEM((n, rows, width), partial.dtype),
            pltpu.VMEM((n, *stats.shape), jnp.float32),
            pltpu.VMEM((rows, width), jnp.bfloat16),
            pltpu.VMEM((rows, n * width), jnp.bfloat16),
            pltpu.SemaphoreType.DMA((n,)),
            pltpu.SemaphoreType.DMA((n,)),
            pltpu.SemaphoreType.DMA((n,)),
            pltpu.SemaphoreType.DMA((n,)),
            pltpu.SemaphoreType.DMA((n,)),
            pltpu.SemaphoreType.DMA((n,)),
        ],
        compiler_params=pltpu.CompilerParams(
            collective_id=2, has_side_effects=True, vmem_limit_bytes=16 * 1024 * 1024
        ),
    )(partial, stats, normed, inv_rms, gain_own, top, upstream)


def conv_block(weights, ext_vals, tail_rows, d_act):
    kernel_width = weights.shape[0]
    length = d_act.shape[0]
    pre_act = jnp.zeros_like(d_act)
    for lag_idx in range(kernel_width):
        start = kernel_width - 1 - lag_idx
        pre_act = pre_act + weights[lag_idx] * ext_vals[start : start + length]
    gate_sig = jax.nn.sigmoid(pre_act)
    d_pre = d_act * gate_sig * (1.0 + pre_act * (1.0 - gate_sig))
    padded_back = jnp.concatenate([d_pre, tail_rows], axis=0)
    d_vals = jnp.zeros_like(d_pre)
    for lag_idx in range(kernel_width):
        d_vals = d_vals + weights[lag_idx] * padded_back[lag_idx : lag_idx + length]
    lag_grads = jnp.stack(
        [
            jnp.sum(
                d_pre * ext_vals[kernel_width - 1 - lag_idx : kernel_width - 1 - lag_idx + length],
                axis=0,
            )
            for lag_idx in range(kernel_width)
        ]
    )
    return (d_vals.astype(jnp.bfloat16), lag_grads, d_pre[: kernel_width - 1])


def local(dy_top, loss_mask, counts, layer_in, conv_in, norm_gain, conv_weight, in_proj, out_proj):
    sections = lax.axis_size("section")
    tensors = lax.axis_size("tensor")
    section_idx = lax.axis_index("section")
    tensor_idx = lax.axis_index("tensor")
    batches, seq_len, model_width = dy_top.shape
    width = model_width // tensors
    gain_vec = norm_gain[0]
    weights = conv_weight[0]
    kernel_width = weights.shape[0]
    local_channels = weights.shape[1]
    w_in = in_proj[0]
    w_out = out_proj[0]
    conv_padded = jnp.pad(conv_in[0], ((0, 0), (kernel_width - 1, 0), (0, 0)))
    positions = jnp.arange(seq_len, dtype=jnp.int32)
    keep_mask = (loss_mask == 1) & (positions[None, :] < counts[:, None])
    top_grads = jnp.where(keep_mask[:, :, None], dy_top, jnp.zeros_like(dy_top))
    is_last = section_idx == sections - 1
    contract = (((1,), (1,)), ((), ()))

    values = layer_in[0].astype(jnp.float32)
    inv_rms_all = lax.rsqrt(jnp.mean(values * values, axis=-1, keepdims=True) + EPSILON)
    normed_all = values * inv_rms_all
    gain_own = lax.dynamic_slice(gain_vec, (tensor_idx * width,), (width,))
    normed_own_all = lax.dynamic_slice(normed_all, (0, 0, tensor_idx * width), (batches, seq_len, width))

    halves = CHUNKS_PER_BATCH
    chunk_len = seq_len // halves
    n_chunks = batches * halves
    total_steps = sections + n_chunks - 1

    def pick_block(step_idx):
        block_raw = step_idx - (sections - 1 - section_idx)
        active = (block_raw >= 0) & (block_raw < n_chunks)
        block_now = jnp.clip(block_raw, 0, n_chunks - 1)
        within = lax.rem(block_now, halves)
        return (block_now // halves, halves - 1 - within, within > 0, active)

    def rows_of(array, batch_slot, first_row, row_count):
        return lax.dynamic_slice(array, (batch_slot, first_row, 0), (1, row_count, array.shape[2]))[0]

    tail_init = jnp.zeros((kernel_width - 1, local_channels), jnp.float32)

    def step_rows(step_idx, loop_state):
        incoming, results, gain_acc, conv_acc, tail_carry = loop_state
        batch_slot, half_now, join_now, active = pick_block(step_idx)
        row_start = half_now * chunk_len
        top_chunk = rows_of(top_grads, batch_slot, row_start, chunk_len)
        d_act = matmul_nt(top_chunk, incoming, w_out, w_out.shape[0], 2048, jnp.float32, sections)
        ext_vals = lax.dynamic_slice(
            conv_padded, (batch_slot, row_start, 0), (1, chunk_len + kernel_width - 1, local_channels)
        )[0].astype(jnp.float32)
        tail_rows = jnp.where(join_now, tail_carry, 0.0)
        d_vals, conv_part, new_tail = conv_block(weights, ext_vals, tail_rows, d_act)
        partial = lax.dot_general(d_vals, w_in, contract, preferred_element_type=jnp.float32).astype(jnp.bfloat16)
        normed = rows_of(normed_all, batch_slot, row_start, chunk_len)
        inv_rms = rows_of(inv_rms_all, batch_slot, row_start, chunk_len)
        row_part = jnp.sum(partial.astype(jnp.float32) * gain_vec * normed, axis=-1)
        stats = jnp.zeros((chunk_len, 128), jnp.float32).at[:, 0].set(row_part)
        normed_own = rows_of(normed_own_all, batch_slot, row_start, chunk_len)
        grad_out, incoming_next, gain_part = layer_exchange(
            partial, stats, normed_own, inv_rms, gain_own[None, :], top_chunk, incoming, tensors, sections, width
        )
        gain_part = gain_part[0]
        previous = lax.dynamic_slice(results, (batch_slot, half_now, 0, 0), (1, 1, chunk_len, width))
        updated = jnp.where(active, grad_out[None, None], previous)
        results = lax.dynamic_update_slice(results, updated, (batch_slot, half_now, 0, 0))
        gain_acc = gain_acc + jnp.where(active, gain_part, 0.0)
        conv_acc = conv_acc + jnp.where(active, conv_part, 0.0)
        tail_carry = jnp.where(active, new_tail, tail_carry)
        incoming = incoming_next
        return (incoming, results, gain_acc, conv_acc, tail_carry)

    initial = (
        jnp.zeros((chunk_len, model_width), jnp.bfloat16),
        jnp.zeros((batches, halves, chunk_len, width), jnp.bfloat16),
        jnp.zeros((width,), jnp.float32),
        jnp.zeros(weights.shape, jnp.float32),
        tail_init,
    )
    last_state = lax.fori_loop(0, total_steps, step_rows, initial)
    own = last_state[1].reshape(batches * seq_len, width)
    gain_hi = last_state[2].astype(jnp.bfloat16)
    gain_lo = (last_state[2] - gain_hi.astype(jnp.float32)).astype(jnp.bfloat16)
    extra = jnp.zeros((16, width), jnp.bfloat16).at[0].set(gain_hi).at[1].set(gain_lo)
    own = jnp.concatenate([own, extra], axis=0)
    copies = jnp.broadcast_to(own, (tensors, *own.shape))
    gathered = lax.all_to_all(copies, "tensor", split_axis=0, concat_axis=2, tiled=True)[0]
    rows = batches * seq_len
    results = gathered[:rows].reshape(batches, seq_len, model_width)
    gain_total = gathered[rows].astype(jnp.float32) + gathered[rows + 1].astype(jnp.float32)
    conv_acc = last_state[3]
    return (results[None], gain_total[None], conv_acc[None])


def solution(mesh):
    placed = (
        P(),
        P(),
        P(),
        P("section", None, None, None),
        P("section", None, None, "tensor"),
        P("section", None),
        P("section", None, "tensor"),
        P("section", None, "tensor"),
        P("section", "tensor", None),
    )
    return jax.shard_map(
        local,
        mesh=mesh,
        in_specs=placed,
        out_specs=(
            P("section", None, None, None),
            P("section", None),
            P("section", None, "tensor"),
        ),
        check_vma=False,
    )
```

```python
import functools

import jax
import jax.numpy as jnp
from jax import lax
from jax.experimental import pallas as pl
from jax.experimental.pallas import tpu as pltpu
from jax.sharding import PartitionSpec as P

EPSILON = 1e-05
MESH = pl.DeviceIdType.MESH
CHUNKS_PER_BATCH = 2


def sent_to_all(x, axis):
    copies = jnp.broadcast_to(x, (lax.axis_size(axis), *x.shape))
    return lax.all_to_all(copies, axis, split_axis=0, concat_axis=0, tiled=True)


def matmul_nt_kernel(n_sec, top_ref, x_ref, w_ref, out_ref):
    lhs = jnp.where(lax.axis_index("section") == n_sec - 1, top_ref[...], x_ref[...])
    product = lax.dot_general(lhs, w_ref[...], (((1,), (1,)), ((), ())), preferred_element_type=jnp.float32)

    @pl.when(pl.program_id(1) == 0)
    def _():
        out_ref[...] = product.astype(out_ref.dtype)

    @pl.when(pl.program_id(1) > 0)
    def _():
        out_ref[...] += product.astype(out_ref.dtype)


def matmul_nt(top, x, w, block_n, block_k, out_dtype, n_sec):
    rows, depth = x.shape
    cols = w.shape[0]
    grid = (cols // block_n, depth // block_k)
    return pl.pallas_call(
        functools.partial(matmul_nt_kernel, n_sec),
        out_shape=jax.ShapeDtypeStruct((rows, cols), out_dtype),
        grid=grid,
        in_specs=[
            pl.BlockSpec((rows, block_k), lambda n, k: (0, k)),
            pl.BlockSpec((rows, block_k), lambda n, k: (0, k)),
            pl.BlockSpec((block_n, block_k), lambda n, k: (n, k)),
        ],
        out_specs=pl.BlockSpec((rows, block_n), lambda n, k: (0, n)),
        compiler_params=pltpu.CompilerParams(
            dimension_semantics=("arbitrary", "arbitrary"), vmem_limit_bytes=16 * 1024 * 1024
        ),
        cost_estimate=pl.CostEstimate(
            flops=2 * rows * cols * depth,
            bytes_accessed=2 * (2 * rows * depth + cols * depth) + rows * cols * jnp.dtype(out_dtype).itemsize,
            transcendentals=0,
        ),
    )(top, x, w)


def layer_exchange_kernel(
    n, n_sec, width, x_ref, s_ref, normed_ref, inv_ref, gain_ref, top_ref, up_ref,
    g_ref, next_ref, gain_out_ref,
    recv, srecv, gbuf, down, send_sem, recv_sem, ssend_sem, srecv_sem, dsend_sem, drecv_sem,
):
    me = lax.axis_index("tensor")
    sec = lax.axis_index("section")
    barrier = pltpu.get_barrier_semaphore()
    for k in range(1, n):
        pl.semaphore_signal(barrier, inc=1, device_id=(sec, lax.rem(me + k, n)), device_id_type=MESH)

    @pl.when(sec < n_sec - 1)
    def _():
        for t in range(n):
            pl.semaphore_signal(barrier, inc=1, device_id=(sec + 1, t), device_id_type=MESH)

    @pl.when(sec > 0)
    def _():
        pl.semaphore_wait(barrier, 2 * n - 1)

    @pl.when(sec == 0)
    def _():
        pl.semaphore_wait(barrier, n - 1)

    copies = []
    for k in range(1, n):
        peer = lax.rem(me + k, n)
        cols = pl.ds(pl.multiple_of(peer * width, 128), width)
        block = pltpu.make_async_remote_copy(
            src_ref=x_ref.at[:, cols],
            dst_ref=recv.at[me],
            send_sem=send_sem.at[k],
            recv_sem=recv_sem.at[k],
            device_id=(sec, peer),
            device_id_type=MESH,
        )
        block.start()
        stat = pltpu.make_async_remote_copy(
            src_ref=s_ref,
            dst_ref=srecv.at[me],
            send_sem=ssend_sem.at[k],
            recv_sem=srecv_sem.at[k],
            device_id=(sec, peer),
            device_id_type=MESH,
        )
        stat.start()
        copies.append((block, stat))
    for block, stat in copies:
        block.wait()
        stat.wait()
    mine = pl.ds(pl.multiple_of(me * width, 128), width)
    total = x_ref[:, mine].astype(jnp.float32)
    stat_total = s_ref[...]
    for k in range(1, n):
        src = lax.rem(me + n - k, n)
        total = total + recv[src].astype(jnp.float32)
        stat_total = stat_total + srecv[src]
    rows = total.shape[0]
    row_mean = jnp.transpose(stat_total)[:rows, 0:1] * (1.0 / (n * width))
    normed = normed_ref[...]
    d_in = inv_ref[...] * (total * gain_ref[...] - normed * row_mean)
    upstream = jnp.where(sec == n_sec - 1, top_ref[:, mine], up_ref[:, mine])
    result = (upstream.astype(jnp.float32) + d_in).astype(g_ref.dtype)
    gbuf[...] = result
    g_ref[...] = result
    gain_out_ref[...] = jnp.sum(total * normed, axis=0, keepdims=True)

    @pl.when(sec > 0)
    def _():
        sends = []
        for t in range(n):
            copy = pltpu.make_async_remote_copy(
                src_ref=gbuf,
                dst_ref=down.at[:, mine],
                send_sem=dsend_sem.at[t],
                recv_sem=drecv_sem.at[me],
                device_id=(sec - 1, t),
                device_id_type=MESH,
            )
            copy.start()
            sends.append(copy)
        for copy in sends:
            copy.wait_send()

    @pl.when(sec < n_sec - 1)
    def _():
        for src in range(n):
            pltpu.make_async_remote_copy(
                src_ref=gbuf,
                dst_ref=down.at[:, pl.ds(src * width, width)],
                send_sem=dsend_sem.at[src],
                recv_sem=drecv_sem.at[src],
                device_id=(sec + 1, src),
                device_id_type=MESH,
            ).wait_recv()
        next_ref[...] = down[...]

    @pl.when(sec == n_sec - 1)
    def _():
        next_ref[...] = jnp.zeros_like(next_ref)


def layer_exchange(partial, stats, normed, inv_rms, gain_own, top, upstream, n, n_sec, width):
    rows = partial.shape[0]
    vmem = pl.BlockSpec(memory_space=pltpu.VMEM)
    return pl.pallas_call(
        functools.partial(layer_exchange_kernel, n, n_sec, width),
        out_shape=(
            jax.ShapeDtypeStruct((rows, width), jnp.bfloat16),
            jax.ShapeDtypeStruct((rows, n * width), jnp.bfloat16),
            jax.ShapeDtypeStruct((1, width), jnp.float32),
        ),
        in_specs=[vmem] * 7,
        out_specs=(vmem, vmem, vmem),
        scratch_shapes=[
            pltpu.VMEM((n, rows, width), partial.dtype),
            pltpu.VMEM((n, *stats.shape), jnp.float32),
            pltpu.VMEM((rows, width), jnp.bfloat16),
            pltpu.VMEM((rows, n * width), jnp.bfloat16),
            pltpu.SemaphoreType.DMA((n,)),
            pltpu.SemaphoreType.DMA((n,)),
            pltpu.SemaphoreType.DMA((n,)),
            pltpu.SemaphoreType.DMA((n,)),
            pltpu.SemaphoreType.DMA((n,)),
            pltpu.SemaphoreType.DMA((n,)),
        ],
        compiler_params=pltpu.CompilerParams(
            collective_id=2, has_side_effects=True, vmem_limit_bytes=16 * 1024 * 1024
        ),
    )(partial, stats, normed, inv_rms, gain_own, top, upstream)


def conv_block(weights, ext_vals, tail_rows, d_act):
    kernel_width = weights.shape[0]
    length = d_act.shape[0]
    pre_act = jnp.zeros_like(d_act)
    for lag_idx in range(kernel_width):
        start = kernel_width - 1 - lag_idx
        pre_act = pre_act + weights[lag_idx] * ext_vals[start : start + length]
    gate_sig = jax.nn.sigmoid(pre_act)
    d_pre = d_act * gate_sig * (1.0 + pre_act * (1.0 - gate_sig))
    padded_back = jnp.concatenate([d_pre, tail_rows], axis=0)
    d_vals = jnp.zeros_like(d_pre)
    for lag_idx in range(kernel_width):
        d_vals = d_vals + weights[lag_idx] * padded_back[lag_idx : lag_idx + length]
    lag_grads = jnp.stack(
        [
            jnp.sum(
                d_pre * ext_vals[kernel_width - 1 - lag_idx : kernel_width - 1 - lag_idx + length],
                axis=0,
            )
            for lag_idx in range(kernel_width)
        ]
    )
    return (d_vals.astype(jnp.bfloat16), lag_grads, d_pre[: kernel_width - 1])


def local(dy_top, loss_mask, counts, layer_in, conv_in, norm_gain, conv_weight, in_proj, out_proj):
    sections = lax.axis_size("section")
    tensors = lax.axis_size("tensor")
    section_idx = lax.axis_index("section")
    tensor_idx = lax.axis_index("tensor")
    batches, seq_len, model_width = dy_top.shape
    width = model_width // tensors
    gain_vec = norm_gain[0]
    weights = conv_weight[0]
    kernel_width = weights.shape[0]
    local_channels = weights.shape[1]
    w_in = in_proj[0]
    w_out = out_proj[0]
    conv_padded = jnp.pad(conv_in[0], ((0, 0), (kernel_width - 1, 0), (0, 0)))
    positions = jnp.arange(seq_len, dtype=jnp.int32)
    keep_mask = (loss_mask == 1) & (positions[None, :] < counts[:, None])
    top_grads = jnp.where(keep_mask[:, :, None], dy_top, jnp.zeros_like(dy_top))
    is_last = section_idx == sections - 1
    contract = (((1,), (1,)), ((), ()))

    values = layer_in[0].astype(jnp.float32)
    inv_rms_all = lax.rsqrt(jnp.mean(values * values, axis=-1, keepdims=True) + EPSILON)
    normed_all = values * inv_rms_all
    gain_own = lax.dynamic_slice(gain_vec, (tensor_idx * width,), (width,))
    normed_own_all = lax.dynamic_slice(normed_all, (0, 0, tensor_idx * width), (batches, seq_len, width))

    halves = CHUNKS_PER_BATCH
    chunk_len = seq_len // halves
    n_chunks = batches * halves
    total_steps = sections + n_chunks - 1

    def pick_block(step_idx):
        block_raw = step_idx - (sections - 1 - section_idx)
        active = (block_raw >= 0) & (block_raw < n_chunks)
        block_now = jnp.clip(block_raw, 0, n_chunks - 1)
        within = lax.rem(block_now, halves)
        return (block_now // halves, halves - 1 - within, within > 0, active)

    def rows_of(array, batch_slot, first_row, row_count):
        return lax.dynamic_slice(array, (batch_slot, first_row, 0), (1, row_count, array.shape[2]))[0]

    tail_init = jnp.zeros((kernel_width - 1, local_channels), jnp.float32)

    def step_rows(step_idx, loop_state):
        incoming, results, gain_acc, conv_acc, tail_carry = loop_state
        batch_slot, half_now, join_now, active = pick_block(step_idx)
        row_start = half_now * chunk_len
        top_chunk = rows_of(top_grads, batch_slot, row_start, chunk_len)
        d_act = matmul_nt(top_chunk, incoming, w_out, w_out.shape[0], 2048, jnp.float32, sections)
        ext_vals = lax.dynamic_slice(
            conv_padded, (batch_slot, row_start, 0), (1, chunk_len + kernel_width - 1, local_channels)
        )[0].astype(jnp.float32)
        tail_rows = jnp.where(join_now, tail_carry, 0.0)
        d_vals, conv_part, new_tail = conv_block(weights, ext_vals, tail_rows, d_act)
        partial = lax.dot_general(d_vals, w_in, contract, preferred_element_type=jnp.float32).astype(jnp.bfloat16)
        normed = rows_of(normed_all, batch_slot, row_start, chunk_len)
        inv_rms = rows_of(inv_rms_all, batch_slot, row_start, chunk_len)
        row_part = jnp.sum(partial.astype(jnp.float32) * gain_vec * normed, axis=-1)
        stats = jnp.zeros((8, 128), jnp.float32).at[0, :chunk_len].set(row_part)
        normed_own = rows_of(normed_own_all, batch_slot, row_start, chunk_len)
        grad_out, incoming_next, gain_part = layer_exchange(
            partial, stats, normed_own, inv_rms, gain_own[None, :], top_chunk, incoming, tensors, sections, width
        )
        gain_part = gain_part[0]
        previous = lax.dynamic_slice(results, (batch_slot, half_now, 0, 0), (1, 1, chunk_len, width))
        updated = jnp.where(active, grad_out[None, None], previous)
        results = lax.dynamic_update_slice(results, updated, (batch_slot, half_now, 0, 0))
        gain_acc = gain_acc + jnp.where(active, gain_part, 0.0)
        conv_acc = conv_acc + jnp.where(active, conv_part, 0.0)
        tail_carry = jnp.where(active, new_tail, tail_carry)
        incoming = incoming_next
        return (incoming, results, gain_acc, conv_acc, tail_carry)

    initial = (
        jnp.zeros((chunk_len, model_width), jnp.bfloat16),
        jnp.zeros((batches, halves, chunk_len, width), jnp.bfloat16),
        jnp.zeros((width,), jnp.float32),
        jnp.zeros(weights.shape, jnp.float32),
        tail_init,
    )
    last_state = lax.fori_loop(0, total_steps, step_rows, initial)
    own = last_state[1].reshape(batches * seq_len, width)
    gain_hi = last_state[2].astype(jnp.bfloat16)
    gain_lo = (last_state[2] - gain_hi.astype(jnp.float32)).astype(jnp.bfloat16)
    extra = jnp.zeros((16, width), jnp.bfloat16).at[0].set(gain_hi).at[1].set(gain_lo)
    own = jnp.concatenate([own, extra], axis=0)
    copies = jnp.broadcast_to(own, (tensors, *own.shape))
    gathered = lax.all_to_all(copies, "tensor", split_axis=0, concat_axis=2, tiled=True)[0]
    rows = batches * seq_len
    results = gathered[:rows].reshape(batches, seq_len, model_width)
    gain_total = gathered[rows].astype(jnp.float32) + gathered[rows + 1].astype(jnp.float32)
    conv_acc = last_state[3]
    return (results[None], gain_total[None], conv_acc[None])


def solution(mesh):
    placed = (
        P(),
        P(),
        P(),
        P("section", None, None, None),
        P("section", None, None, "tensor"),
        P("section", None),
        P("section", None, "tensor"),
        P("section", None, "tensor"),
        P("section", "tensor", None),
    )
    return jax.shard_map(
        local,
        mesh=mesh,
        in_specs=placed,
        out_specs=(
            P("section", None, None, None),
            P("section", None),
            P("section", None, "tensor"),
        ),
        check_vma=False,
    )
```

```python
import functools

import jax
import jax.numpy as jnp
from jax import lax
from jax.experimental import pallas as pl
from jax.experimental.pallas import tpu as pltpu
from jax.sharding import PartitionSpec as P

EPSILON = 1e-05
MESH = pl.DeviceIdType.MESH
CHUNKS_PER_BATCH = 2


def sent_to_all(x, axis):
    copies = jnp.broadcast_to(x, (lax.axis_size(axis), *x.shape))
    return lax.all_to_all(copies, axis, split_axis=0, concat_axis=0, tiled=True)


def matmul_nt_kernel(n_sec, top_ref, x_ref, w_ref, out_ref):
    lhs = jnp.where(lax.axis_index("section") == n_sec - 1, top_ref[...], x_ref[...])
    product = lax.dot_general(lhs, w_ref[...], (((1,), (1,)), ((), ())), preferred_element_type=jnp.float32)

    @pl.when(pl.program_id(1) == 0)
    def _():
        out_ref[...] = product.astype(out_ref.dtype)

    @pl.when(pl.program_id(1) > 0)
    def _():
        out_ref[...] += product.astype(out_ref.dtype)


def matmul_nt(top, x, w, block_n, block_k, out_dtype, n_sec):
    rows, depth = x.shape
    cols = w.shape[0]
    grid = (cols // block_n, depth // block_k)
    return pl.pallas_call(
        functools.partial(matmul_nt_kernel, n_sec),
        out_shape=jax.ShapeDtypeStruct((rows, cols), out_dtype),
        grid=grid,
        in_specs=[
            pl.BlockSpec((rows, block_k), lambda n, k: (0, k)),
            pl.BlockSpec((rows, block_k), lambda n, k: (0, k)),
            pl.BlockSpec((block_n, block_k), lambda n, k: (n, k)),
        ],
        out_specs=pl.BlockSpec((rows, block_n), lambda n, k: (0, n)),
        compiler_params=pltpu.CompilerParams(
            dimension_semantics=("arbitrary", "arbitrary"), vmem_limit_bytes=16 * 1024 * 1024
        ),
        cost_estimate=pl.CostEstimate(
            flops=2 * rows * cols * depth,
            bytes_accessed=2 * (2 * rows * depth + cols * depth) + rows * cols * jnp.dtype(out_dtype).itemsize,
            transcendentals=0,
        ),
    )(top, x, w)


def layer_exchange_kernel(
    n, n_sec, width, x_ref, s_ref, aux_ref, gain_ref, top_ref, up_ref,
    g_ref, next_ref, gain_out_ref,
    recv, srecv, gbuf, down, send_sem, recv_sem, ssend_sem, srecv_sem, dsend_sem, drecv_sem,
):
    me = lax.axis_index("tensor")
    sec = lax.axis_index("section")
    barrier = pltpu.get_barrier_semaphore()
    for k in range(1, n):
        pl.semaphore_signal(barrier, inc=1, device_id=(sec, lax.rem(me + k, n)), device_id_type=MESH)

    @pl.when(sec < n_sec - 1)
    def _():
        for t in range(n):
            pl.semaphore_signal(barrier, inc=1, device_id=(sec + 1, t), device_id_type=MESH)

    @pl.when(sec > 0)
    def _():
        pl.semaphore_wait(barrier, 2 * n - 1)

    @pl.when(sec == 0)
    def _():
        pl.semaphore_wait(barrier, n - 1)

    copies = []
    for k in range(1, n):
        peer = lax.rem(me + k, n)
        cols = pl.ds(pl.multiple_of(peer * width, 128), width)
        block = pltpu.make_async_remote_copy(
            src_ref=x_ref.at[:, cols],
            dst_ref=recv.at[me],
            send_sem=send_sem.at[k],
            recv_sem=recv_sem.at[k],
            device_id=(sec, peer),
            device_id_type=MESH,
        )
        block.start()
        stat = pltpu.make_async_remote_copy(
            src_ref=s_ref,
            dst_ref=srecv.at[me],
            send_sem=ssend_sem.at[k],
            recv_sem=srecv_sem.at[k],
            device_id=(sec, peer),
            device_id_type=MESH,
        )
        stat.start()
        copies.append((block, stat))
    for block, stat in copies:
        block.wait()
        stat.wait()
    mine = pl.ds(pl.multiple_of(me * width, 128), width)
    total = x_ref[:, mine].astype(jnp.float32)
    stat_total = s_ref[...]
    for k in range(1, n):
        src = lax.rem(me + n - k, n)
        total = total + recv[src].astype(jnp.float32)
        stat_total = stat_total + srecv[src]
    rows = total.shape[0]
    row_mean = jnp.transpose(stat_total)[:rows, 0:1] * (1.0 / (n * width))
    normed = aux_ref[:, :width]
    inv_rms = aux_ref[:, width : width + 1]
    d_in = inv_rms * (total * gain_ref[...] - normed * row_mean)
    upstream = jnp.where(sec == n_sec - 1, top_ref[:, mine], up_ref[:, mine])
    result = (upstream.astype(jnp.float32) + d_in).astype(g_ref.dtype)
    gbuf[...] = result
    g_ref[...] = result
    gain_out_ref[...] = jnp.sum(total * normed, axis=0, keepdims=True)

    @pl.when(sec > 0)
    def _():
        sends = []
        for t in range(n):
            copy = pltpu.make_async_remote_copy(
                src_ref=gbuf,
                dst_ref=down.at[:, mine],
                send_sem=dsend_sem.at[t],
                recv_sem=drecv_sem.at[me],
                device_id=(sec - 1, t),
                device_id_type=MESH,
            )
            copy.start()
            sends.append(copy)
        for copy in sends:
            copy.wait_send()

    @pl.when(sec < n_sec - 1)
    def _():
        for src in range(n):
            pltpu.make_async_remote_copy(
                src_ref=gbuf,
                dst_ref=down.at[:, pl.ds(src * width, width)],
                send_sem=dsend_sem.at[src],
                recv_sem=drecv_sem.at[src],
                device_id=(sec + 1, src),
                device_id_type=MESH,
            ).wait_recv()
        next_ref[...] = down[...]

    @pl.when(sec == n_sec - 1)
    def _():
        next_ref[...] = jnp.zeros_like(next_ref)


def layer_exchange(partial, stats, aux, gain_own, top, upstream, n, n_sec, width):
    rows = partial.shape[0]
    vmem = pl.BlockSpec(memory_space=pltpu.VMEM)
    return pl.pallas_call(
        functools.partial(layer_exchange_kernel, n, n_sec, width),
        out_shape=(
            jax.ShapeDtypeStruct((rows, width), jnp.bfloat16),
            jax.ShapeDtypeStruct((rows, n * width), jnp.bfloat16),
            jax.ShapeDtypeStruct((1, width), jnp.float32),
        ),
        in_specs=[vmem] * 6,
        out_specs=(vmem, vmem, vmem),
        scratch_shapes=[
            pltpu.VMEM((n, rows, width), partial.dtype),
            pltpu.VMEM((n, *stats.shape), jnp.float32),
            pltpu.VMEM((rows, width), jnp.bfloat16),
            pltpu.VMEM((rows, n * width), jnp.bfloat16),
            pltpu.SemaphoreType.DMA((n,)),
            pltpu.SemaphoreType.DMA((n,)),
            pltpu.SemaphoreType.DMA((n,)),
            pltpu.SemaphoreType.DMA((n,)),
            pltpu.SemaphoreType.DMA((n,)),
            pltpu.SemaphoreType.DMA((n,)),
        ],
        compiler_params=pltpu.CompilerParams(
            collective_id=2, has_side_effects=True, vmem_limit_bytes=16 * 1024 * 1024
        ),
    )(partial, stats, aux, gain_own, top, upstream)


def conv_block(weights, ext_vals, tail_rows, d_act):
    kernel_width = weights.shape[0]
    length = d_act.shape[0]
    pre_act = jnp.zeros_like(d_act)
    for lag_idx in range(kernel_width):
        start = kernel_width - 1 - lag_idx
        pre_act = pre_act + weights[lag_idx] * ext_vals[start : start + length]
    gate_sig = jax.nn.sigmoid(pre_act)
    d_pre = d_act * gate_sig * (1.0 + pre_act * (1.0 - gate_sig))
    padded_back = jnp.concatenate([d_pre, tail_rows], axis=0)
    d_vals = jnp.zeros_like(d_pre)
    for lag_idx in range(kernel_width):
        d_vals = d_vals + weights[lag_idx] * padded_back[lag_idx : lag_idx + length]
    lag_grads = jnp.stack(
        [
            jnp.sum(
                d_pre * ext_vals[kernel_width - 1 - lag_idx : kernel_width - 1 - lag_idx + length],
                axis=0,
            )
            for lag_idx in range(kernel_width)
        ]
    )
    return (d_vals.astype(jnp.bfloat16), lag_grads, d_pre[: kernel_width - 1])


def local(dy_top, loss_mask, counts, layer_in, conv_in, norm_gain, conv_weight, in_proj, out_proj):
    sections = lax.axis_size("section")
    tensors = lax.axis_size("tensor")
    section_idx = lax.axis_index("section")
    tensor_idx = lax.axis_index("tensor")
    batches, seq_len, model_width = dy_top.shape
    width = model_width // tensors
    gain_vec = norm_gain[0]
    weights = conv_weight[0]
    kernel_width = weights.shape[0]
    local_channels = weights.shape[1]
    w_in = in_proj[0]
    w_out = out_proj[0]
    conv_padded = jnp.pad(conv_in[0], ((0, 0), (kernel_width - 1, 0), (0, 0)))
    positions = jnp.arange(seq_len, dtype=jnp.int32)
    keep_mask = (loss_mask == 1) & (positions[None, :] < counts[:, None])
    top_grads = jnp.where(keep_mask[:, :, None], dy_top, jnp.zeros_like(dy_top))
    is_last = section_idx == sections - 1
    contract = (((1,), (1,)), ((), ()))

    values = layer_in[0].astype(jnp.float32)
    inv_rms_all = lax.rsqrt(jnp.mean(values * values, axis=-1, keepdims=True) + EPSILON)
    normed_all = values * inv_rms_all
    gain_own = lax.dynamic_slice(gain_vec, (tensor_idx * width,), (width,))
    normed_own_all = lax.dynamic_slice(normed_all, (0, 0, tensor_idx * width), (batches, seq_len, width))
    aux_all = jnp.concatenate(
        [normed_own_all, jnp.broadcast_to(inv_rms_all, (batches, seq_len, 128))], axis=-1
    )

    halves = CHUNKS_PER_BATCH
    chunk_len = seq_len // halves
    n_chunks = batches * halves
    total_steps = sections + n_chunks - 1

    def pick_block(step_idx):
        block_raw = step_idx - (sections - 1 - section_idx)
        active = (block_raw >= 0) & (block_raw < n_chunks)
        block_now = jnp.clip(block_raw, 0, n_chunks - 1)
        within = lax.rem(block_now, halves)
        return (block_now // halves, halves - 1 - within, within > 0, active)

    def rows_of(array, batch_slot, first_row, row_count):
        return lax.dynamic_slice(array, (batch_slot, first_row, 0), (1, row_count, array.shape[2]))[0]

    tail_init = jnp.zeros((kernel_width - 1, local_channels), jnp.float32)

    def step_rows(step_idx, loop_state):
        incoming, results, gain_acc, conv_acc, tail_carry = loop_state
        batch_slot, half_now, join_now, active = pick_block(step_idx)
        row_start = half_now * chunk_len
        top_chunk = rows_of(top_grads, batch_slot, row_start, chunk_len)
        d_act = matmul_nt(top_chunk, incoming, w_out, w_out.shape[0], 2048, jnp.float32, sections)
        ext_vals = lax.dynamic_slice(
            conv_padded, (batch_slot, row_start, 0), (1, chunk_len + kernel_width - 1, local_channels)
        )[0].astype(jnp.float32)
        tail_rows = jnp.where(join_now, tail_carry, 0.0)
        d_vals, conv_part, new_tail = conv_block(weights, ext_vals, tail_rows, d_act)
        partial = lax.dot_general(d_vals, w_in, contract, preferred_element_type=jnp.float32).astype(jnp.bfloat16)
        normed = rows_of(normed_all, batch_slot, row_start, chunk_len)
        row_part = jnp.sum(partial.astype(jnp.float32) * gain_vec * normed, axis=-1)
        stats = jnp.zeros((8, 128), jnp.float32).at[0, :chunk_len].set(row_part)
        aux = rows_of(aux_all, batch_slot, row_start, chunk_len)
        grad_out, incoming_next, gain_part = layer_exchange(
            partial, stats, aux, gain_own[None, :], top_chunk, incoming, tensors, sections, width
        )
        gain_part = gain_part[0]
        previous = lax.dynamic_slice(results, (batch_slot, half_now, 0, 0), (1, 1, chunk_len, width))
        updated = jnp.where(active, grad_out[None, None], previous)
        results = lax.dynamic_update_slice(results, updated, (batch_slot, half_now, 0, 0))
        gain_acc = gain_acc + jnp.where(active, gain_part, 0.0)
        conv_acc = conv_acc + jnp.where(active, conv_part, 0.0)
        tail_carry = jnp.where(active, new_tail, tail_carry)
        incoming = incoming_next
        return (incoming, results, gain_acc, conv_acc, tail_carry)

    initial = (
        jnp.zeros((chunk_len, model_width), jnp.bfloat16),
        jnp.zeros((batches, halves, chunk_len, width), jnp.bfloat16),
        jnp.zeros((width,), jnp.float32),
        jnp.zeros(weights.shape, jnp.float32),
        tail_init,
    )
    last_state = lax.fori_loop(0, total_steps, step_rows, initial)
    own = last_state[1].reshape(batches * seq_len, width)
    gain_hi = last_state[2].astype(jnp.bfloat16)
    gain_lo = (last_state[2] - gain_hi.astype(jnp.float32)).astype(jnp.bfloat16)
    extra = jnp.zeros((16, width), jnp.bfloat16).at[0].set(gain_hi).at[1].set(gain_lo)
    own = jnp.concatenate([own, extra], axis=0)
    copies = jnp.broadcast_to(own, (tensors, *own.shape))
    gathered = lax.all_to_all(copies, "tensor", split_axis=0, concat_axis=2, tiled=True)[0]
    rows = batches * seq_len
    results = gathered[:rows].reshape(batches, seq_len, model_width)
    gain_total = gathered[rows].astype(jnp.float32) + gathered[rows + 1].astype(jnp.float32)
    conv_acc = last_state[3]
    return (results[None], gain_total[None], conv_acc[None])


def solution(mesh):
    placed = (
        P(),
        P(),
        P(),
        P("section", None, None, None),
        P("section", None, None, "tensor"),
        P("section", None),
        P("section", None, "tensor"),
        P("section", None, "tensor"),
        P("section", "tensor", None),
    )
    return jax.shard_map(
        local,
        mesh=mesh,
        in_specs=placed,
        out_specs=(
            P("section", None, None, None),
            P("section", None),
            P("section", None, "tensor"),
        ),
        check_vma=False,
    )
```

```python
import functools

import jax
import jax.numpy as jnp
from jax import lax
from jax.experimental import pallas as pl
from jax.experimental.pallas import tpu as pltpu
from jax.sharding import PartitionSpec as P

EPSILON = 1e-05
MESH = pl.DeviceIdType.MESH
CHUNKS_PER_BATCH = 2


def sent_to_all(x, axis):
    copies = jnp.broadcast_to(x, (lax.axis_size(axis), *x.shape))
    return lax.all_to_all(copies, axis, split_axis=0, concat_axis=0, tiled=True)


def matmul_nt_kernel(n_sec, top_ref, x_ref, w_ref, out_ref):
    lhs = jnp.where(lax.axis_index("section") == n_sec - 1, top_ref[...], x_ref[...])
    product = lax.dot_general(lhs, w_ref[...], (((1,), (1,)), ((), ())), preferred_element_type=jnp.float32)

    @pl.when(pl.program_id(1) == 0)
    def _():
        out_ref[...] = product.astype(out_ref.dtype)

    @pl.when(pl.program_id(1) > 0)
    def _():
        out_ref[...] += product.astype(out_ref.dtype)


def matmul_nt(top, x, w, block_n, block_k, out_dtype, n_sec):
    rows, depth = x.shape
    cols = w.shape[0]
    grid = (cols // block_n, depth // block_k)
    return pl.pallas_call(
        functools.partial(matmul_nt_kernel, n_sec),
        out_shape=jax.ShapeDtypeStruct((rows, cols), out_dtype),
        grid=grid,
        in_specs=[
            pl.BlockSpec((rows, block_k), lambda n, k: (0, k)),
            pl.BlockSpec((rows, block_k), lambda n, k: (0, k)),
            pl.BlockSpec((block_n, block_k), lambda n, k: (n, k)),
        ],
        out_specs=pl.BlockSpec((rows, block_n), lambda n, k: (0, n)),
        compiler_params=pltpu.CompilerParams(
            dimension_semantics=("arbitrary", "arbitrary"), vmem_limit_bytes=16 * 1024 * 1024
        ),
        cost_estimate=pl.CostEstimate(
            flops=2 * rows * cols * depth,
            bytes_accessed=2 * (2 * rows * depth + cols * depth) + rows * cols * jnp.dtype(out_dtype).itemsize,
            transcendentals=0,
        ),
    )(top, x, w)


def layer_exchange_kernel(
    n, n_sec, width, x_ref, s_ref, aux_ref, gain_ref, top_ref, up_ref,
    g_ref, next_ref, gain_out_ref,
    recv, srecv, gbuf, down, send_sem, recv_sem, ssend_sem, srecv_sem, dsend_sem, drecv_sem,
):
    me = lax.axis_index("tensor")
    sec = lax.axis_index("section")
    barrier = pltpu.get_barrier_semaphore()
    for k in range(1, n):
        pl.semaphore_signal(barrier, inc=1, device_id=(sec, lax.rem(me + k, n)), device_id_type=MESH)

    @pl.when(sec < n_sec - 1)
    def _():
        for t in range(n):
            pl.semaphore_signal(barrier, inc=1, device_id=(sec + 1, t), device_id_type=MESH)

    @pl.when(sec > 0)
    def _():
        pl.semaphore_wait(barrier, 2 * n - 1)

    @pl.when(sec == 0)
    def _():
        pl.semaphore_wait(barrier, n - 1)

    copies = []
    for k in range(1, n):
        peer = lax.rem(me + k, n)
        cols = pl.ds(pl.multiple_of(peer * width, 128), width)
        block = pltpu.make_async_remote_copy(
            src_ref=x_ref.at[:, cols],
            dst_ref=recv.at[me],
            send_sem=send_sem.at[k],
            recv_sem=recv_sem.at[k],
            device_id=(sec, peer),
            device_id_type=MESH,
        )
        block.start()
        stat = pltpu.make_async_remote_copy(
            src_ref=s_ref,
            dst_ref=srecv.at[me],
            send_sem=ssend_sem.at[k],
            recv_sem=srecv_sem.at[k],
            device_id=(sec, peer),
            device_id_type=MESH,
        )
        stat.start()
        copies.append((block, stat))
    for block, stat in copies:
        block.wait()
        stat.wait()
    mine = pl.ds(pl.multiple_of(me * width, 128), width)
    total = x_ref[:, mine].astype(jnp.float32)
    stat_total = s_ref[...]
    for k in range(1, n):
        src = lax.rem(me + n - k, n)
        total = total + recv[src].astype(jnp.float32)
        stat_total = stat_total + srecv[src]
    rows = total.shape[0]
    row_mean = jnp.transpose(stat_total)[:rows, 0:1] * (1.0 / (n * width))
    normed = aux_ref[:, :width]
    inv_rms = aux_ref[:, width : width + 1]
    d_in = inv_rms * (total * gain_ref[...] - normed * row_mean)
    upstream = jnp.where(sec == n_sec - 1, top_ref[:, mine], up_ref[:, mine])
    result = (upstream.astype(jnp.float32) + d_in).astype(g_ref.dtype)
    gbuf[...] = result
    g_ref[...] = result
    gain_out_ref[...] = jnp.sum(total * normed, axis=0, keepdims=True)

    @pl.when(sec > 0)
    def _():
        sends = []
        for t in range(n):
            copy = pltpu.make_async_remote_copy(
                src_ref=gbuf,
                dst_ref=down.at[:, mine],
                send_sem=dsend_sem.at[t],
                recv_sem=drecv_sem.at[me],
                device_id=(sec - 1, t),
                device_id_type=MESH,
            )
            copy.start()
            sends.append(copy)
        for copy in sends:
            copy.wait_send()

    @pl.when(sec < n_sec - 1)
    def _():
        for src in range(n):
            pltpu.make_async_remote_copy(
                src_ref=gbuf,
                dst_ref=down.at[:, pl.ds(src * width, width)],
                send_sem=dsend_sem.at[src],
                recv_sem=drecv_sem.at[src],
                device_id=(sec + 1, src),
                device_id_type=MESH,
            ).wait_recv()
        next_ref[...] = down[...]

    @pl.when(sec == n_sec - 1)
    def _():
        next_ref[...] = jnp.zeros_like(next_ref)


def layer_exchange(partial, stats, aux, gain_own, top, upstream, n, n_sec, width):
    rows = partial.shape[0]
    vmem = pl.BlockSpec(memory_space=pltpu.VMEM)
    return pl.pallas_call(
        functools.partial(layer_exchange_kernel, n, n_sec, width),
        out_shape=(
            jax.ShapeDtypeStruct((rows, width), jnp.bfloat16),
            jax.ShapeDtypeStruct((rows, n * width), jnp.bfloat16),
            jax.ShapeDtypeStruct((1, width), jnp.float32),
        ),
        in_specs=[vmem] * 6,
        out_specs=(vmem, vmem, vmem),
        scratch_shapes=[
            pltpu.VMEM((n, rows, width), partial.dtype),
            pltpu.VMEM((n, *stats.shape), jnp.float32),
            pltpu.VMEM((rows, width), jnp.bfloat16),
            pltpu.VMEM((rows, n * width), jnp.bfloat16),
            pltpu.SemaphoreType.DMA((n,)),
            pltpu.SemaphoreType.DMA((n,)),
            pltpu.SemaphoreType.DMA((n,)),
            pltpu.SemaphoreType.DMA((n,)),
            pltpu.SemaphoreType.DMA((n,)),
            pltpu.SemaphoreType.DMA((n,)),
        ],
        compiler_params=pltpu.CompilerParams(
            collective_id=2, has_side_effects=True, vmem_limit_bytes=16 * 1024 * 1024
        ),
    )(partial, stats, aux, gain_own, top, upstream)


def conv_block(weights, ext_vals, tail_rows, d_act):
    kernel_width = weights.shape[0]
    length = d_act.shape[0]
    pre_act = jnp.zeros_like(d_act)
    for lag_idx in range(kernel_width):
        start = kernel_width - 1 - lag_idx
        pre_act = pre_act + weights[lag_idx] * ext_vals[start : start + length]
    gate_sig = jax.nn.sigmoid(pre_act)
    d_pre = d_act * gate_sig * (1.0 + pre_act * (1.0 - gate_sig))
    padded_back = jnp.concatenate([d_pre, tail_rows], axis=0)
    d_vals = jnp.zeros_like(d_pre)
    for lag_idx in range(kernel_width):
        d_vals = d_vals + weights[lag_idx] * padded_back[lag_idx : lag_idx + length]
    lag_grads = jnp.stack(
        [
            jnp.sum(
                d_pre * ext_vals[kernel_width - 1 - lag_idx : kernel_width - 1 - lag_idx + length],
                axis=0,
            )
            for lag_idx in range(kernel_width)
        ]
    )
    return (d_vals.astype(jnp.bfloat16), lag_grads, d_pre[: kernel_width - 1])


def local(dy_top, loss_mask, counts, layer_in, conv_in, norm_gain, conv_weight, in_proj, out_proj):
    sections = lax.axis_size("section")
    tensors = lax.axis_size("tensor")
    section_idx = lax.axis_index("section")
    tensor_idx = lax.axis_index("tensor")
    batches, seq_len, model_width = dy_top.shape
    width = model_width // tensors
    gain_vec = norm_gain[0]
    weights = conv_weight[0]
    kernel_width = weights.shape[0]
    local_channels = weights.shape[1]
    w_in = in_proj[0]
    w_out = out_proj[0]
    conv_padded = jnp.pad(conv_in[0], ((0, 0), (kernel_width - 1, 0), (0, 0)))
    positions = jnp.arange(seq_len, dtype=jnp.int32)
    keep_mask = (loss_mask == 1) & (positions[None, :] < counts[:, None])
    top_grads = jnp.where(keep_mask[:, :, None], dy_top, jnp.zeros_like(dy_top))
    is_last = section_idx == sections - 1
    contract = (((1,), (1,)), ((), ()))

    values = layer_in[0].astype(jnp.float32)
    inv_rms_all = lax.rsqrt(jnp.mean(values * values, axis=-1, keepdims=True) + EPSILON)
    normed_all = values * inv_rms_all
    gain_own = lax.dynamic_slice(gain_vec, (tensor_idx * width,), (width,))
    normed_own_all = lax.dynamic_slice(normed_all, (0, 0, tensor_idx * width), (batches, seq_len, width))
    aux_all = jnp.concatenate(
        [normed_own_all, jnp.broadcast_to(inv_rms_all, (batches, seq_len, 128))], axis=-1
    )

    halves = CHUNKS_PER_BATCH
    chunk_len = seq_len // halves
    n_chunks = batches * halves
    total_steps = sections + n_chunks - 1

    def pick_block(step_idx):
        block_raw = step_idx - (sections - 1 - section_idx)
        active = (block_raw >= 0) & (block_raw < n_chunks)
        block_now = jnp.clip(block_raw, 0, n_chunks - 1)
        within = lax.rem(block_now, halves)
        return (block_now // halves, halves - 1 - within, within > 0, active)

    def rows_of(array, batch_slot, first_row, row_count):
        return lax.dynamic_slice(array, (batch_slot, first_row, 0), (1, row_count, array.shape[2]))[0]

    tail_init = jnp.zeros((kernel_width - 1, local_channels), jnp.float32)

    def step_rows(step_idx, loop_state):
        incoming, results, gain_acc, conv_acc, tail_carry = loop_state
        batch_slot, half_now, join_now, active = pick_block(step_idx)
        row_start = half_now * chunk_len
        top_chunk = rows_of(top_grads, batch_slot, row_start, chunk_len)
        d_act = matmul_nt(top_chunk, incoming, w_out, w_out.shape[0], 2048, jnp.float32, sections)
        ext_vals = lax.dynamic_slice(
            conv_padded, (batch_slot, row_start, 0), (1, chunk_len + kernel_width - 1, local_channels)
        )[0].astype(jnp.float32)
        tail_rows = jnp.where(join_now, tail_carry, 0.0)
        d_vals, conv_part, new_tail = conv_block(weights, ext_vals, tail_rows, d_act)
        partial = lax.dot_general(d_vals, w_in, contract, preferred_element_type=jnp.float32).astype(jnp.bfloat16)
        normed = rows_of(normed_all, batch_slot, row_start, chunk_len)
        row_part = jnp.sum(partial.astype(jnp.float32) * gain_vec * normed, axis=-1)
        stats = jnp.zeros((8, 128), jnp.float32).at[0, :chunk_len].set(row_part)
        aux = rows_of(aux_all, batch_slot, row_start, chunk_len)
        grad_out, incoming_next, gain_part = layer_exchange(
            partial, stats, aux, gain_own[None, :], top_chunk, incoming, tensors, sections, width
        )
        gain_part = gain_part[0]
        previous = lax.dynamic_slice(results, (batch_slot, half_now, 0, 0), (1, 1, chunk_len, width))
        updated = jnp.where(active, grad_out[None, None], previous)
        results = lax.dynamic_update_slice(results, updated, (batch_slot, half_now, 0, 0))
        gain_acc = gain_acc + jnp.where(active, gain_part, 0.0)
        conv_acc = conv_acc + jnp.where(active, conv_part, 0.0)
        tail_carry = jnp.where(active, new_tail, tail_carry)
        incoming = incoming_next
        return (incoming, results, gain_acc, conv_acc, tail_carry)

    initial = (
        jnp.zeros((chunk_len, model_width), jnp.bfloat16),
        jnp.zeros((batches, halves, chunk_len, width), jnp.bfloat16),
        jnp.zeros((width,), jnp.float32),
        jnp.zeros(weights.shape, jnp.float32),
        tail_init,
    )
    last_state = lax.fori_loop(0, total_steps, step_rows, initial)
    own = last_state[1].reshape(batches * seq_len, width)
    gain_hi = last_state[2].astype(jnp.bfloat16)
    gain_lo = (last_state[2] - gain_hi.astype(jnp.float32)).astype(jnp.bfloat16)
    extra = jnp.stack([gain_hi, gain_lo])
    own = jnp.concatenate([own, extra], axis=0)
    copies = jnp.broadcast_to(own, (tensors, *own.shape))
    gathered = lax.all_to_all(copies, "tensor", split_axis=0, concat_axis=2, tiled=True)[0]
    rows = batches * seq_len
    results = gathered[:rows].reshape(batches, seq_len, model_width)
    gain_total = gathered[rows].astype(jnp.float32) + gathered[rows + 1].astype(jnp.float32)
    conv_acc = last_state[3]
    return (results[None], gain_total[None], conv_acc[None])


def solution(mesh):
    placed = (
        P(),
        P(),
        P(),
        P("section", None, None, None),
        P("section", None, None, "tensor"),
        P("section", None),
        P("section", None, "tensor"),
        P("section", None, "tensor"),
        P("section", "tensor", None),
    )
    return jax.shard_map(
        local,
        mesh=mesh,
        in_specs=placed,
        out_specs=(
            P("section", None, None, None),
            P("section", None),
            P("section", None, "tensor"),
        ),
        check_vma=False,
    )
```

```python
import functools

import jax
import jax.numpy as jnp
from jax import lax
from jax.experimental import pallas as pl
from jax.experimental.pallas import tpu as pltpu
from jax.sharding import PartitionSpec as P

EPSILON = 1e-05
MESH = pl.DeviceIdType.MESH
CHUNKS_PER_BATCH = 2


def sent_to_all(x, axis):
    copies = jnp.broadcast_to(x, (lax.axis_size(axis), *x.shape))
    return lax.all_to_all(copies, axis, split_axis=0, concat_axis=0, tiled=True)


def matmul_nt_kernel(n_sec, top_ref, x_ref, w_ref, out_ref):
    lhs = jnp.where(lax.axis_index("section") == n_sec - 1, top_ref[...], x_ref[...])
    product = lax.dot_general(lhs, w_ref[...], (((1,), (1,)), ((), ())), preferred_element_type=jnp.float32)

    @pl.when(pl.program_id(1) == 0)
    def _():
        out_ref[...] = product.astype(out_ref.dtype)

    @pl.when(pl.program_id(1) > 0)
    def _():
        out_ref[...] += product.astype(out_ref.dtype)


def matmul_nt(top, x, w, block_n, block_k, out_dtype, n_sec):
    rows, depth = x.shape
    cols = w.shape[0]
    grid = (cols // block_n, depth // block_k)
    return pl.pallas_call(
        functools.partial(matmul_nt_kernel, n_sec),
        out_shape=jax.ShapeDtypeStruct((rows, cols), out_dtype),
        grid=grid,
        in_specs=[
            pl.BlockSpec((rows, block_k), lambda n, k: (0, k)),
            pl.BlockSpec((rows, block_k), lambda n, k: (0, k)),
            pl.BlockSpec((block_n, block_k), lambda n, k: (n, k)),
        ],
        out_specs=pl.BlockSpec((rows, block_n), lambda n, k: (0, n)),
        compiler_params=pltpu.CompilerParams(
            dimension_semantics=("arbitrary", "arbitrary"), vmem_limit_bytes=16 * 1024 * 1024
        ),
        cost_estimate=pl.CostEstimate(
            flops=2 * rows * cols * depth,
            bytes_accessed=2 * (2 * rows * depth + cols * depth) + rows * cols * jnp.dtype(out_dtype).itemsize,
            transcendentals=0,
        ),
    )(top, x, w)


def layer_exchange_kernel(
    n, n_sec, width, x_ref, s_ref, aux_ref, gain_ref, top_ref, up_ref,
    g_ref, next_ref, gain_out_ref,
    recv, srecv, gbuf, down, send_sem, recv_sem, ssend_sem, srecv_sem, dsend_sem, drecv_sem,
):
    me = lax.axis_index("tensor")
    sec = lax.axis_index("section")
    barrier = pltpu.get_barrier_semaphore()
    for k in range(1, n):
        pl.semaphore_signal(barrier, inc=1, device_id=(sec, lax.rem(me + k, n)), device_id_type=MESH)

    @pl.when(sec < n_sec - 1)
    def _():
        for t in range(n):
            pl.semaphore_signal(barrier, inc=1, device_id=(sec + 1, t), device_id_type=MESH)

    @pl.when(sec > 0)
    def _():
        pl.semaphore_wait(barrier, 2 * n - 1)

    @pl.when(sec == 0)
    def _():
        pl.semaphore_wait(barrier, n - 1)

    copies = []
    for k in range(1, n):
        peer = lax.rem(me + k, n)
        cols = pl.ds(pl.multiple_of(peer * width, 128), width)
        block = pltpu.make_async_remote_copy(
            src_ref=x_ref.at[:, cols],
            dst_ref=recv.at[me],
            send_sem=send_sem.at[k],
            recv_sem=recv_sem.at[k],
            device_id=(sec, peer),
            device_id_type=MESH,
        )
        block.start()
        stat = pltpu.make_async_remote_copy(
            src_ref=s_ref,
            dst_ref=srecv.at[me],
            send_sem=ssend_sem.at[k],
            recv_sem=srecv_sem.at[k],
            device_id=(sec, peer),
            device_id_type=MESH,
        )
        stat.start()
        copies.append((block, stat))
    for block, stat in copies:
        block.wait()
        stat.wait()
    mine = pl.ds(pl.multiple_of(me * width, 128), width)
    total = x_ref[:, mine].astype(jnp.float32)
    stat_total = s_ref[...]
    for k in range(1, n):
        src = lax.rem(me + n - k, n)
        total = total + recv[src].astype(jnp.float32)
        stat_total = stat_total + srecv[src]
    rows = total.shape[0]
    row_mean = jnp.transpose(stat_total)[:rows, 0:1] * (1.0 / (n * width))
    normed = aux_ref[:, :width]
    inv_rms = aux_ref[:, width : width + 1]
    d_in = inv_rms * (total * gain_ref[...] - normed * row_mean)
    upstream = jnp.where(sec == n_sec - 1, top_ref[:, mine], up_ref[:, mine])
    result = (upstream.astype(jnp.float32) + d_in).astype(g_ref.dtype)
    gbuf[...] = result
    g_ref[...] = result
    gain_out_ref[...] = jnp.sum(total * normed, axis=0, keepdims=True)

    @pl.when(sec > 0)
    def _():
        sends = []
        for t in range(n):
            copy = pltpu.make_async_remote_copy(
                src_ref=gbuf,
                dst_ref=down.at[:, mine],
                send_sem=dsend_sem.at[t],
                recv_sem=drecv_sem.at[me],
                device_id=(sec - 1, t),
                device_id_type=MESH,
            )
            copy.start()
            sends.append(copy)
        for copy in sends:
            copy.wait_send()

    @pl.when(sec < n_sec - 1)
    def _():
        for src in range(n):
            pltpu.make_async_remote_copy(
                src_ref=gbuf,
                dst_ref=down.at[:, pl.ds(src * width, width)],
                send_sem=dsend_sem.at[src],
                recv_sem=drecv_sem.at[src],
                device_id=(sec + 1, src),
                device_id_type=MESH,
            ).wait_recv()
        next_ref[...] = down[...]

    @pl.when(sec == n_sec - 1)
    def _():
        next_ref[...] = jnp.zeros_like(next_ref)


def layer_exchange(partial, stats, aux, gain_own, top, upstream, n, n_sec, width):
    rows = partial.shape[0]
    vmem = pl.BlockSpec(memory_space=pltpu.VMEM)
    return pl.pallas_call(
        functools.partial(layer_exchange_kernel, n, n_sec, width),
        out_shape=(
            jax.ShapeDtypeStruct((rows, width), jnp.bfloat16),
            jax.ShapeDtypeStruct((rows, n * width), jnp.bfloat16),
            jax.ShapeDtypeStruct((1, width), jnp.float32),
        ),
        in_specs=[vmem] * 6,
        out_specs=(vmem, vmem, vmem),
        scratch_shapes=[
            pltpu.VMEM((n, rows, width), partial.dtype),
            pltpu.VMEM((n, *stats.shape), jnp.float32),
            pltpu.VMEM((rows, width), jnp.bfloat16),
            pltpu.VMEM((rows, n * width), jnp.bfloat16),
            pltpu.SemaphoreType.DMA((n,)),
            pltpu.SemaphoreType.DMA((n,)),
            pltpu.SemaphoreType.DMA((n,)),
            pltpu.SemaphoreType.DMA((n,)),
            pltpu.SemaphoreType.DMA((n,)),
            pltpu.SemaphoreType.DMA((n,)),
        ],
        compiler_params=pltpu.CompilerParams(
            collective_id=2, has_side_effects=True, vmem_limit_bytes=16 * 1024 * 1024
        ),
    )(partial, stats, aux, gain_own, top, upstream)


def conv_block(weights, ext_vals, tail_rows, d_act):
    kernel_width = weights.shape[0]
    length = d_act.shape[0]
    pre_act = jnp.zeros_like(d_act)
    for lag_idx in range(kernel_width):
        start = kernel_width - 1 - lag_idx
        pre_act = pre_act + weights[lag_idx] * ext_vals[start : start + length]
    gate_sig = jax.nn.sigmoid(pre_act)
    d_pre = d_act * gate_sig * (1.0 + pre_act * (1.0 - gate_sig))
    padded_back = jnp.concatenate([d_pre, tail_rows], axis=0)
    d_vals = jnp.zeros_like(d_pre)
    for lag_idx in range(kernel_width):
        d_vals = d_vals + weights[lag_idx] * padded_back[lag_idx : lag_idx + length]
    lag_grads = jnp.stack(
        [
            jnp.sum(
                d_pre * ext_vals[kernel_width - 1 - lag_idx : kernel_width - 1 - lag_idx + length],
                axis=0,
            )
            for lag_idx in range(kernel_width)
        ]
    )
    return (d_vals.astype(jnp.bfloat16), lag_grads, d_pre[: kernel_width - 1])


def local(dy_top, loss_mask, counts, layer_in, conv_in, norm_gain, conv_weight, in_proj, out_proj):
    sections = lax.axis_size("section")
    tensors = lax.axis_size("tensor")
    section_idx = lax.axis_index("section")
    tensor_idx = lax.axis_index("tensor")
    batches, seq_len, model_width = dy_top.shape
    width = model_width // tensors
    gain_vec = norm_gain[0]
    weights = conv_weight[0]
    kernel_width = weights.shape[0]
    local_channels = weights.shape[1]
    w_in = in_proj[0]
    w_out = out_proj[0]
    conv_padded = jnp.pad(conv_in[0], ((0, 0), (kernel_width - 1, 0), (0, 0)))
    positions = jnp.arange(seq_len, dtype=jnp.int32)
    keep_mask = (loss_mask == 1) & (positions[None, :] < counts[:, None])
    top_grads = jnp.where(keep_mask[:, :, None], dy_top, jnp.zeros_like(dy_top))
    is_last = section_idx == sections - 1
    contract = (((1,), (1,)), ((), ()))

    values = layer_in[0].astype(jnp.float32)
    inv_rms_all = lax.rsqrt(jnp.mean(values * values, axis=-1, keepdims=True) + EPSILON)
    normed_all = values * inv_rms_all
    gain_own = lax.dynamic_slice(gain_vec, (tensor_idx * width,), (width,))
    normed_own_all = lax.dynamic_slice(normed_all, (0, 0, tensor_idx * width), (batches, seq_len, width))
    aux_all = jnp.concatenate(
        [normed_own_all, jnp.broadcast_to(inv_rms_all, (batches, seq_len, 128))], axis=-1
    )

    halves = CHUNKS_PER_BATCH
    chunk_len = seq_len // halves
    n_chunks = batches * halves
    total_steps = sections + n_chunks - 1

    def pick_block(step_idx):
        block_raw = step_idx - (sections - 1 - section_idx)
        active = (block_raw >= 0) & (block_raw < n_chunks)
        block_now = jnp.clip(block_raw, 0, n_chunks - 1)
        within = lax.rem(block_now, halves)
        return (block_now // halves, halves - 1 - within, within > 0, active)

    def rows_of(array, batch_slot, first_row, row_count):
        return lax.dynamic_slice(array, (batch_slot, first_row, 0), (1, row_count, array.shape[2]))[0]

    tail_init = jnp.zeros((kernel_width - 1, local_channels), jnp.float32)

    def step_rows(step_idx, loop_state):
        incoming, results, gain_acc, conv_acc, tail_carry = loop_state
        batch_slot, half_now, join_now, active = pick_block(step_idx)
        row_start = half_now * chunk_len
        top_chunk = rows_of(top_grads, batch_slot, row_start, chunk_len)
        d_act = matmul_nt(top_chunk, incoming, w_out, w_out.shape[0], 4096, jnp.float32, sections)
        ext_vals = lax.dynamic_slice(
            conv_padded, (batch_slot, row_start, 0), (1, chunk_len + kernel_width - 1, local_channels)
        )[0].astype(jnp.float32)
        tail_rows = jnp.where(join_now, tail_carry, 0.0)
        d_vals, conv_part, new_tail = conv_block(weights, ext_vals, tail_rows, d_act)
        partial = lax.dot_general(d_vals, w_in, contract, preferred_element_type=jnp.float32).astype(jnp.bfloat16)
        normed = rows_of(normed_all, batch_slot, row_start, chunk_len)
        row_part = jnp.sum(partial.astype(jnp.float32) * gain_vec * normed, axis=-1)
        stats = jnp.zeros((8, 128), jnp.float32).at[0, :chunk_len].set(row_part)
        aux = rows_of(aux_all, batch_slot, row_start, chunk_len)
        grad_out, incoming_next, gain_part = layer_exchange(
            partial, stats, aux, gain_own[None, :], top_chunk, incoming, tensors, sections, width
        )
        gain_part = gain_part[0]
        previous = lax.dynamic_slice(results, (batch_slot, half_now, 0, 0), (1, 1, chunk_len, width))
        updated = jnp.where(active, grad_out[None, None], previous)
        results = lax.dynamic_update_slice(results, updated, (batch_slot, half_now, 0, 0))
        gain_acc = gain_acc + jnp.where(active, gain_part, 0.0)
        conv_acc = conv_acc + jnp.where(active, conv_part, 0.0)
        tail_carry = jnp.where(active, new_tail, tail_carry)
        incoming = incoming_next
        return (incoming, results, gain_acc, conv_acc, tail_carry)

    initial = (
        jnp.zeros((chunk_len, model_width), jnp.bfloat16),
        jnp.zeros((batches, halves, chunk_len, width), jnp.bfloat16),
        jnp.zeros((width,), jnp.float32),
        jnp.zeros(weights.shape, jnp.float32),
        tail_init,
    )
    last_state = lax.fori_loop(0, total_steps, step_rows, initial)
    own = last_state[1].reshape(batches * seq_len, width)
    gain_hi = last_state[2].astype(jnp.bfloat16)
    gain_lo = (last_state[2] - gain_hi.astype(jnp.float32)).astype(jnp.bfloat16)
    extra = jnp.stack([gain_hi, gain_lo])
    own = jnp.concatenate([own, extra], axis=0)
    copies = jnp.broadcast_to(own, (tensors, *own.shape))
    gathered = lax.all_to_all(copies, "tensor", split_axis=0, concat_axis=2, tiled=True)[0]
    rows = batches * seq_len
    results = gathered[:rows].reshape(batches, seq_len, model_width)
    gain_total = gathered[rows].astype(jnp.float32) + gathered[rows + 1].astype(jnp.float32)
    conv_acc = last_state[3]
    return (results[None], gain_total[None], conv_acc[None])


def solution(mesh):
    placed = (
        P(),
        P(),
        P(),
        P("section", None, None, None),
        P("section", None, None, "tensor"),
        P("section", None),
        P("section", None, "tensor"),
        P("section", None, "tensor"),
        P("section", "tensor", None),
    )
    return jax.shard_map(
        local,
        mesh=mesh,
        in_specs=placed,
        out_specs=(
            P("section", None, None, None),
            P("section", None),
            P("section", None, "tensor"),
        ),
        check_vma=False,
    )
```

```python
import functools

import jax
import jax.numpy as jnp
from jax import lax
from jax.experimental import pallas as pl
from jax.experimental.pallas import tpu as pltpu
from jax.sharding import PartitionSpec as P

EPSILON = 1e-05
MESH = pl.DeviceIdType.MESH
CHUNKS_PER_BATCH = 2


def sent_to_all(x, axis):
    copies = jnp.broadcast_to(x, (lax.axis_size(axis), *x.shape))
    return lax.all_to_all(copies, axis, split_axis=0, concat_axis=0, tiled=True)


def matmul_nt_kernel(n_sec, top_ref, x_ref, w_ref, out_ref):
    lhs = jnp.where(lax.axis_index("section") == n_sec - 1, top_ref[...], x_ref[...])
    product = lax.dot_general(lhs, w_ref[...], (((1,), (1,)), ((), ())), preferred_element_type=jnp.float32)

    @pl.when(pl.program_id(1) == 0)
    def _():
        out_ref[...] = product.astype(out_ref.dtype)

    @pl.when(pl.program_id(1) > 0)
    def _():
        out_ref[...] += product.astype(out_ref.dtype)


def matmul_nt(top, x, w, block_n, block_k, out_dtype, n_sec):
    rows, depth = x.shape
    cols = w.shape[0]
    grid = (cols // block_n, depth // block_k)
    return pl.pallas_call(
        functools.partial(matmul_nt_kernel, n_sec),
        out_shape=jax.ShapeDtypeStruct((rows, cols), out_dtype),
        grid=grid,
        in_specs=[
            pl.BlockSpec((rows, block_k), lambda n, k: (0, k)),
            pl.BlockSpec((rows, block_k), lambda n, k: (0, k)),
            pl.BlockSpec((block_n, block_k), lambda n, k: (n, k)),
        ],
        out_specs=pl.BlockSpec((rows, block_n), lambda n, k: (0, n)),
        compiler_params=pltpu.CompilerParams(
            dimension_semantics=("arbitrary", "arbitrary"), vmem_limit_bytes=16 * 1024 * 1024
        ),
        cost_estimate=pl.CostEstimate(
            flops=2 * rows * cols * depth,
            bytes_accessed=2 * (2 * rows * depth + cols * depth) + rows * cols * jnp.dtype(out_dtype).itemsize,
            transcendentals=0,
        ),
    )(top, x, w)


def layer_exchange_kernel(
    n, n_sec, width, x_ref, s_ref, aux_ref, gain_ref, top_ref, up_ref,
    g_ref, next_ref, gain_out_ref,
    recv, srecv, gbuf, down, send_sem, recv_sem, ssend_sem, srecv_sem, dsend_sem, drecv_sem,
):
    me = lax.axis_index("tensor")
    sec = lax.axis_index("section")
    barrier = pltpu.get_barrier_semaphore()
    @pl.when(sec < n_sec - 1)
    def _():
        for t in range(n):
            pl.semaphore_signal(barrier, inc=1, device_id=(sec + 1, t), device_id_type=MESH)

    for k in range(1, n):
        pl.semaphore_signal(barrier, inc=1, device_id=(sec, lax.rem(me + k, n)), device_id_type=MESH)

    @pl.when(sec > 0)
    def _():
        pl.semaphore_wait(barrier, 2 * n - 1)

    @pl.when(sec == 0)
    def _():
        pl.semaphore_wait(barrier, n - 1)

    copies = []
    for k in range(1, n):
        peer = lax.rem(me + k, n)
        cols = pl.ds(pl.multiple_of(peer * width, 128), width)
        block = pltpu.make_async_remote_copy(
            src_ref=x_ref.at[:, cols],
            dst_ref=recv.at[me],
            send_sem=send_sem.at[k],
            recv_sem=recv_sem.at[k],
            device_id=(sec, peer),
            device_id_type=MESH,
        )
        block.start()
        stat = pltpu.make_async_remote_copy(
            src_ref=s_ref,
            dst_ref=srecv.at[me],
            send_sem=ssend_sem.at[k],
            recv_sem=srecv_sem.at[k],
            device_id=(sec, peer),
            device_id_type=MESH,
        )
        stat.start()
        copies.append((block, stat))
    for block, stat in copies:
        block.wait()
        stat.wait()
    mine = pl.ds(pl.multiple_of(me * width, 128), width)
    total = x_ref[:, mine].astype(jnp.float32)
    stat_total = s_ref[...]
    for k in range(1, n):
        src = lax.rem(me + n - k, n)
        total = total + recv[src].astype(jnp.float32)
        stat_total = stat_total + srecv[src]
    rows = total.shape[0]
    row_mean = jnp.transpose(stat_total)[:rows, 0:1] * (1.0 / (n * width))
    normed = aux_ref[:, :width]
    inv_rms = aux_ref[:, width : width + 1]
    d_in = inv_rms * (total * gain_ref[...] - normed * row_mean)
    upstream = jnp.where(sec == n_sec - 1, top_ref[:, mine], up_ref[:, mine])
    result = (upstream.astype(jnp.float32) + d_in).astype(g_ref.dtype)
    gbuf[...] = result
    g_ref[...] = result
    gain_out_ref[...] = jnp.sum(total * normed, axis=0, keepdims=True)

    @pl.when(sec > 0)
    def _():
        sends = []
        for t in range(n):
            copy = pltpu.make_async_remote_copy(
                src_ref=gbuf,
                dst_ref=down.at[:, mine],
                send_sem=dsend_sem.at[t],
                recv_sem=drecv_sem.at[me],
                device_id=(sec - 1, t),
                device_id_type=MESH,
            )
            copy.start()
            sends.append(copy)
        for copy in sends:
            copy.wait_send()

    @pl.when(sec < n_sec - 1)
    def _():
        for src in range(n):
            pltpu.make_async_remote_copy(
                src_ref=gbuf,
                dst_ref=down.at[:, pl.ds(src * width, width)],
                send_sem=dsend_sem.at[src],
                recv_sem=drecv_sem.at[src],
                device_id=(sec + 1, src),
                device_id_type=MESH,
            ).wait_recv()
        next_ref[...] = down[...]

    @pl.when(sec == n_sec - 1)
    def _():
        next_ref[...] = jnp.zeros_like(next_ref)


def layer_exchange(partial, stats, aux, gain_own, top, upstream, n, n_sec, width):
    rows = partial.shape[0]
    vmem = pl.BlockSpec(memory_space=pltpu.VMEM)
    return pl.pallas_call(
        functools.partial(layer_exchange_kernel, n, n_sec, width),
        out_shape=(
            jax.ShapeDtypeStruct((rows, width), jnp.bfloat16),
            jax.ShapeDtypeStruct((rows, n * width), jnp.bfloat16),
            jax.ShapeDtypeStruct((1, width), jnp.float32),
        ),
        in_specs=[vmem] * 6,
        out_specs=(vmem, vmem, vmem),
        scratch_shapes=[
            pltpu.VMEM((n, rows, width), partial.dtype),
            pltpu.VMEM((n, *stats.shape), jnp.float32),
            pltpu.VMEM((rows, width), jnp.bfloat16),
            pltpu.VMEM((rows, n * width), jnp.bfloat16),
            pltpu.SemaphoreType.DMA((n,)),
            pltpu.SemaphoreType.DMA((n,)),
            pltpu.SemaphoreType.DMA((n,)),
            pltpu.SemaphoreType.DMA((n,)),
            pltpu.SemaphoreType.DMA((n,)),
            pltpu.SemaphoreType.DMA((n,)),
        ],
        compiler_params=pltpu.CompilerParams(
            collective_id=2, has_side_effects=True, vmem_limit_bytes=16 * 1024 * 1024
        ),
    )(partial, stats, aux, gain_own, top, upstream)


def conv_block(weights, ext_vals, tail_rows, d_act):
    kernel_width = weights.shape[0]
    length = d_act.shape[0]
    pre_act = jnp.zeros_like(d_act)
    for lag_idx in range(kernel_width):
        start = kernel_width - 1 - lag_idx
        pre_act = pre_act + weights[lag_idx] * ext_vals[start : start + length]
    gate_sig = jax.nn.sigmoid(pre_act)
    d_pre = d_act * gate_sig * (1.0 + pre_act * (1.0 - gate_sig))
    padded_back = jnp.concatenate([d_pre, tail_rows], axis=0)
    d_vals = jnp.zeros_like(d_pre)
    for lag_idx in range(kernel_width):
        d_vals = d_vals + weights[lag_idx] * padded_back[lag_idx : lag_idx + length]
    lag_grads = jnp.stack(
        [
            jnp.sum(
                d_pre * ext_vals[kernel_width - 1 - lag_idx : kernel_width - 1 - lag_idx + length],
                axis=0,
            )
            for lag_idx in range(kernel_width)
        ]
    )
    return (d_vals.astype(jnp.bfloat16), lag_grads, d_pre[: kernel_width - 1])


def local(dy_top, loss_mask, counts, layer_in, conv_in, norm_gain, conv_weight, in_proj, out_proj):
    sections = lax.axis_size("section")
    tensors = lax.axis_size("tensor")
    section_idx = lax.axis_index("section")
    tensor_idx = lax.axis_index("tensor")
    batches, seq_len, model_width = dy_top.shape
    width = model_width // tensors
    gain_vec = norm_gain[0]
    weights = conv_weight[0]
    kernel_width = weights.shape[0]
    local_channels = weights.shape[1]
    w_in = in_proj[0]
    w_out = out_proj[0]
    conv_padded = jnp.pad(conv_in[0], ((0, 0), (kernel_width - 1, 0), (0, 0)))
    positions = jnp.arange(seq_len, dtype=jnp.int32)
    keep_mask = (loss_mask == 1) & (positions[None, :] < counts[:, None])
    top_grads = jnp.where(keep_mask[:, :, None], dy_top, jnp.zeros_like(dy_top))
    is_last = section_idx == sections - 1
    contract = (((1,), (1,)), ((), ()))

    values = layer_in[0].astype(jnp.float32)
    inv_rms_all = lax.rsqrt(jnp.mean(values * values, axis=-1, keepdims=True) + EPSILON)
    normed_all = values * inv_rms_all
    gain_own = lax.dynamic_slice(gain_vec, (tensor_idx * width,), (width,))
    normed_own_all = lax.dynamic_slice(normed_all, (0, 0, tensor_idx * width), (batches, seq_len, width))
    aux_all = jnp.concatenate(
        [normed_own_all, jnp.broadcast_to(inv_rms_all, (batches, seq_len, 128))], axis=-1
    )

    halves = CHUNKS_PER_BATCH
    chunk_len = seq_len // halves
    n_chunks = batches * halves
    total_steps = sections + n_chunks - 1

    def pick_block(step_idx):
        block_raw = step_idx - (sections - 1 - section_idx)
        active = (block_raw >= 0) & (block_raw < n_chunks)
        block_now = jnp.clip(block_raw, 0, n_chunks - 1)
        within = lax.rem(block_now, halves)
        return (block_now // halves, halves - 1 - within, within > 0, active)

    def rows_of(array, batch_slot, first_row, row_count):
        return lax.dynamic_slice(array, (batch_slot, first_row, 0), (1, row_count, array.shape[2]))[0]

    tail_init = jnp.zeros((kernel_width - 1, local_channels), jnp.float32)

    def step_rows(step_idx, loop_state):
        incoming, results, gain_acc, conv_acc, tail_carry = loop_state
        batch_slot, half_now, join_now, active = pick_block(step_idx)
        row_start = half_now * chunk_len
        top_chunk = rows_of(top_grads, batch_slot, row_start, chunk_len)
        d_act = matmul_nt(top_chunk, incoming, w_out, w_out.shape[0], 4096, jnp.float32, sections)
        ext_vals = lax.dynamic_slice(
            conv_padded, (batch_slot, row_start, 0), (1, chunk_len + kernel_width - 1, local_channels)
        )[0].astype(jnp.float32)
        tail_rows = jnp.where(join_now, tail_carry, 0.0)
        d_vals, conv_part, new_tail = conv_block(weights, ext_vals, tail_rows, d_act)
        partial = lax.dot_general(d_vals, w_in, contract, preferred_element_type=jnp.float32).astype(jnp.bfloat16)
        normed = rows_of(normed_all, batch_slot, row_start, chunk_len)
        row_part = jnp.sum(partial.astype(jnp.float32) * gain_vec * normed, axis=-1)
        stats = jnp.zeros((8, 128), jnp.float32).at[0, :chunk_len].set(row_part)
        aux = rows_of(aux_all, batch_slot, row_start, chunk_len)
        grad_out, incoming_next, gain_part = layer_exchange(
            partial, stats, aux, gain_own[None, :], top_chunk, incoming, tensors, sections, width
        )
        gain_part = gain_part[0]
        previous = lax.dynamic_slice(results, (batch_slot, half_now, 0, 0), (1, 1, chunk_len, width))
        updated = jnp.where(active, grad_out[None, None], previous)
        results = lax.dynamic_update_slice(results, updated, (batch_slot, half_now, 0, 0))
        gain_acc = gain_acc + jnp.where(active, gain_part, 0.0)
        conv_acc = conv_acc + jnp.where(active, conv_part, 0.0)
        tail_carry = jnp.where(active, new_tail, tail_carry)
        incoming = incoming_next
        return (incoming, results, gain_acc, conv_acc, tail_carry)

    initial = (
        jnp.zeros((chunk_len, model_width), jnp.bfloat16),
        jnp.zeros((batches, halves, chunk_len, width), jnp.bfloat16),
        jnp.zeros((width,), jnp.float32),
        jnp.zeros(weights.shape, jnp.float32),
        tail_init,
    )
    last_state = lax.fori_loop(0, total_steps, step_rows, initial)
    own = last_state[1].reshape(batches * seq_len, width)
    gain_hi = last_state[2].astype(jnp.bfloat16)
    gain_lo = (last_state[2] - gain_hi.astype(jnp.float32)).astype(jnp.bfloat16)
    extra = jnp.stack([gain_hi, gain_lo])
    own = jnp.concatenate([own, extra], axis=0)
    copies = jnp.broadcast_to(own, (tensors, *own.shape))
    gathered = lax.all_to_all(copies, "tensor", split_axis=0, concat_axis=2, tiled=True)[0]
    rows = batches * seq_len
    results = gathered[:rows].reshape(batches, seq_len, model_width)
    gain_total = gathered[rows].astype(jnp.float32) + gathered[rows + 1].astype(jnp.float32)
    conv_acc = last_state[3]
    return (results[None], gain_total[None], conv_acc[None])


def solution(mesh):
    placed = (
        P(),
        P(),
        P(),
        P("section", None, None, None),
        P("section", None, None, "tensor"),
        P("section", None),
        P("section", None, "tensor"),
        P("section", None, "tensor"),
        P("section", "tensor", None),
    )
    return jax.shard_map(
        local,
        mesh=mesh,
        in_specs=placed,
        out_specs=(
            P("section", None, None, None),
            P("section", None),
            P("section", None, "tensor"),
        ),
        check_vma=False,
    )
```

```python
import functools

import jax
import jax.numpy as jnp
from jax import lax
from jax.experimental import pallas as pl
from jax.experimental.pallas import tpu as pltpu
from jax.sharding import PartitionSpec as P

EPSILON = 1e-05
MESH = pl.DeviceIdType.MESH
CHUNKS_PER_BATCH = 4


def sent_to_all(x, axis):
    copies = jnp.broadcast_to(x, (lax.axis_size(axis), *x.shape))
    return lax.all_to_all(copies, axis, split_axis=0, concat_axis=0, tiled=True)


def matmul_nt_kernel(n_sec, top_ref, x_ref, w_ref, out_ref):
    lhs = jnp.where(lax.axis_index("section") == n_sec - 1, top_ref[...], x_ref[...])
    product = lax.dot_general(lhs, w_ref[...], (((1,), (1,)), ((), ())), preferred_element_type=jnp.float32)

    @pl.when(pl.program_id(1) == 0)
    def _():
        out_ref[...] = product.astype(out_ref.dtype)

    @pl.when(pl.program_id(1) > 0)
    def _():
        out_ref[...] += product.astype(out_ref.dtype)


def matmul_nt(top, x, w, block_n, block_k, out_dtype, n_sec):
    rows, depth = x.shape
    cols = w.shape[0]
    grid = (cols // block_n, depth // block_k)
    return pl.pallas_call(
        functools.partial(matmul_nt_kernel, n_sec),
        out_shape=jax.ShapeDtypeStruct((rows, cols), out_dtype),
        grid=grid,
        in_specs=[
            pl.BlockSpec((rows, block_k), lambda n, k: (0, k)),
            pl.BlockSpec((rows, block_k), lambda n, k: (0, k)),
            pl.BlockSpec((block_n, block_k), lambda n, k: (n, k)),
        ],
        out_specs=pl.BlockSpec((rows, block_n), lambda n, k: (0, n)),
        compiler_params=pltpu.CompilerParams(
            dimension_semantics=("arbitrary", "arbitrary"), vmem_limit_bytes=16 * 1024 * 1024
        ),
        cost_estimate=pl.CostEstimate(
            flops=2 * rows * cols * depth,
            bytes_accessed=2 * (2 * rows * depth + cols * depth) + rows * cols * jnp.dtype(out_dtype).itemsize,
            transcendentals=0,
        ),
    )(top, x, w)


def layer_exchange_kernel(
    n, n_sec, width, x_ref, s_ref, aux_ref, gain_ref, top_ref, up_ref,
    g_ref, next_ref, gain_out_ref,
    recv, srecv, gbuf, down, send_sem, recv_sem, ssend_sem, srecv_sem, dsend_sem, drecv_sem,
):
    me = lax.axis_index("tensor")
    sec = lax.axis_index("section")
    barrier = pltpu.get_barrier_semaphore()
    @pl.when(sec < n_sec - 1)
    def _():
        for t in range(n):
            pl.semaphore_signal(barrier, inc=1, device_id=(sec + 1, t), device_id_type=MESH)

    for k in range(1, n):
        pl.semaphore_signal(barrier, inc=1, device_id=(sec, lax.rem(me + k, n)), device_id_type=MESH)

    @pl.when(sec > 0)
    def _():
        pl.semaphore_wait(barrier, 2 * n - 1)

    @pl.when(sec == 0)
    def _():
        pl.semaphore_wait(barrier, n - 1)

    copies = []
    for k in range(1, n):
        peer = lax.rem(me + k, n)
        cols = pl.ds(pl.multiple_of(peer * width, 128), width)
        block = pltpu.make_async_remote_copy(
            src_ref=x_ref.at[:, cols],
            dst_ref=recv.at[me],
            send_sem=send_sem.at[k],
            recv_sem=recv_sem.at[k],
            device_id=(sec, peer),
            device_id_type=MESH,
        )
        block.start()
        stat = pltpu.make_async_remote_copy(
            src_ref=s_ref,
            dst_ref=srecv.at[me],
            send_sem=ssend_sem.at[k],
            recv_sem=srecv_sem.at[k],
            device_id=(sec, peer),
            device_id_type=MESH,
        )
        stat.start()
        copies.append((block, stat))
    for block, stat in copies:
        block.wait()
        stat.wait()
    mine = pl.ds(pl.multiple_of(me * width, 128), width)
    total = x_ref[:, mine].astype(jnp.float32)
    stat_total = s_ref[...]
    for k in range(1, n):
        src = lax.rem(me + n - k, n)
        total = total + recv[src].astype(jnp.float32)
        stat_total = stat_total + srecv[src]
    rows = total.shape[0]
    row_mean = jnp.transpose(stat_total)[:rows, 0:1] * (1.0 / (n * width))
    normed = aux_ref[:, :width]
    inv_rms = aux_ref[:, width : width + 1]
    d_in = inv_rms * (total * gain_ref[...] - normed * row_mean)
    upstream = jnp.where(sec == n_sec - 1, top_ref[:, mine], up_ref[:, mine])
    result = (upstream.astype(jnp.float32) + d_in).astype(g_ref.dtype)
    gbuf[...] = result
    g_ref[...] = result
    gain_out_ref[...] = jnp.sum(total * normed, axis=0, keepdims=True)

    @pl.when(sec > 0)
    def _():
        sends = []
        for t in range(n):
            copy = pltpu.make_async_remote_copy(
                src_ref=gbuf,
                dst_ref=down.at[:, mine],
                send_sem=dsend_sem.at[t],
                recv_sem=drecv_sem.at[me],
                device_id=(sec - 1, t),
                device_id_type=MESH,
            )
            copy.start()
            sends.append(copy)
        for copy in sends:
            copy.wait_send()

    @pl.when(sec < n_sec - 1)
    def _():
        for src in range(n):
            pltpu.make_async_remote_copy(
                src_ref=gbuf,
                dst_ref=down.at[:, pl.ds(src * width, width)],
                send_sem=dsend_sem.at[src],
                recv_sem=drecv_sem.at[src],
                device_id=(sec + 1, src),
                device_id_type=MESH,
            ).wait_recv()
        next_ref[...] = down[...]

    @pl.when(sec == n_sec - 1)
    def _():
        next_ref[...] = jnp.zeros_like(next_ref)


def layer_exchange(partial, stats, aux, gain_own, top, upstream, n, n_sec, width):
    rows = partial.shape[0]
    vmem = pl.BlockSpec(memory_space=pltpu.VMEM)
    return pl.pallas_call(
        functools.partial(layer_exchange_kernel, n, n_sec, width),
        out_shape=(
            jax.ShapeDtypeStruct((rows, width), jnp.bfloat16),
            jax.ShapeDtypeStruct((rows, n * width), jnp.bfloat16),
            jax.ShapeDtypeStruct((1, width), jnp.float32),
        ),
        in_specs=[vmem] * 6,
        out_specs=(vmem, vmem, vmem),
        scratch_shapes=[
            pltpu.VMEM((n, rows, width), partial.dtype),
            pltpu.VMEM((n, *stats.shape), jnp.float32),
            pltpu.VMEM((rows, width), jnp.bfloat16),
            pltpu.VMEM((rows, n * width), jnp.bfloat16),
            pltpu.SemaphoreType.DMA((n,)),
            pltpu.SemaphoreType.DMA((n,)),
            pltpu.SemaphoreType.DMA((n,)),
            pltpu.SemaphoreType.DMA((n,)),
            pltpu.SemaphoreType.DMA((n,)),
            pltpu.SemaphoreType.DMA((n,)),
        ],
        compiler_params=pltpu.CompilerParams(
            collective_id=2, has_side_effects=True, vmem_limit_bytes=16 * 1024 * 1024
        ),
    )(partial, stats, aux, gain_own, top, upstream)


def conv_block(weights, ext_vals, tail_rows, d_act):
    kernel_width = weights.shape[0]
    length = d_act.shape[0]
    pre_act = jnp.zeros_like(d_act)
    for lag_idx in range(kernel_width):
        start = kernel_width - 1 - lag_idx
        pre_act = pre_act + weights[lag_idx] * ext_vals[start : start + length]
    gate_sig = jax.nn.sigmoid(pre_act)
    d_pre = d_act * gate_sig * (1.0 + pre_act * (1.0 - gate_sig))
    padded_back = jnp.concatenate([d_pre, tail_rows], axis=0)
    d_vals = jnp.zeros_like(d_pre)
    for lag_idx in range(kernel_width):
        d_vals = d_vals + weights[lag_idx] * padded_back[lag_idx : lag_idx + length]
    lag_grads = jnp.stack(
        [
            jnp.sum(
                d_pre * ext_vals[kernel_width - 1 - lag_idx : kernel_width - 1 - lag_idx + length],
                axis=0,
            )
            for lag_idx in range(kernel_width)
        ]
    )
    return (d_vals.astype(jnp.bfloat16), lag_grads, d_pre[: kernel_width - 1])


def local(dy_top, loss_mask, counts, layer_in, conv_in, norm_gain, conv_weight, in_proj, out_proj):
    sections = lax.axis_size("section")
    tensors = lax.axis_size("tensor")
    section_idx = lax.axis_index("section")
    tensor_idx = lax.axis_index("tensor")
    batches, seq_len, model_width = dy_top.shape
    width = model_width // tensors
    gain_vec = norm_gain[0]
    weights = conv_weight[0]
    kernel_width = weights.shape[0]
    local_channels = weights.shape[1]
    w_in = in_proj[0]
    w_out = out_proj[0]
    conv_padded = jnp.pad(conv_in[0], ((0, 0), (kernel_width - 1, 0), (0, 0)))
    positions = jnp.arange(seq_len, dtype=jnp.int32)
    keep_mask = (loss_mask == 1) & (positions[None, :] < counts[:, None])
    top_grads = jnp.where(keep_mask[:, :, None], dy_top, jnp.zeros_like(dy_top))
    is_last = section_idx == sections - 1
    contract = (((1,), (1,)), ((), ()))

    values = layer_in[0].astype(jnp.float32)
    inv_rms_all = lax.rsqrt(jnp.mean(values * values, axis=-1, keepdims=True) + EPSILON)
    normed_all = values * inv_rms_all
    gain_own = lax.dynamic_slice(gain_vec, (tensor_idx * width,), (width,))
    normed_own_all = lax.dynamic_slice(normed_all, (0, 0, tensor_idx * width), (batches, seq_len, width))
    aux_all = jnp.concatenate(
        [normed_own_all, jnp.broadcast_to(inv_rms_all, (batches, seq_len, 128))], axis=-1
    )

    halves = CHUNKS_PER_BATCH
    chunk_len = seq_len // halves
    n_chunks = batches * halves
    total_steps = sections + n_chunks - 1

    def pick_block(step_idx):
        block_raw = step_idx - (sections - 1 - section_idx)
        active = (block_raw >= 0) & (block_raw < n_chunks)
        block_now = jnp.clip(block_raw, 0, n_chunks - 1)
        within = lax.rem(block_now, halves)
        return (block_now // halves, halves - 1 - within, within > 0, active)

    def rows_of(array, batch_slot, first_row, row_count):
        return lax.dynamic_slice(array, (batch_slot, first_row, 0), (1, row_count, array.shape[2]))[0]

    tail_init = jnp.zeros((kernel_width - 1, local_channels), jnp.float32)

    def step_rows(step_idx, loop_state):
        incoming, results, gain_acc, conv_acc, tail_carry = loop_state
        batch_slot, half_now, join_now, active = pick_block(step_idx)
        row_start = half_now * chunk_len
        top_chunk = rows_of(top_grads, batch_slot, row_start, chunk_len)
        d_act = matmul_nt(top_chunk, incoming, w_out, w_out.shape[0], 4096, jnp.float32, sections)
        ext_vals = lax.dynamic_slice(
            conv_padded, (batch_slot, row_start, 0), (1, chunk_len + kernel_width - 1, local_channels)
        )[0].astype(jnp.float32)
        tail_rows = jnp.where(join_now, tail_carry, 0.0)
        d_vals, conv_part, new_tail = conv_block(weights, ext_vals, tail_rows, d_act)
        partial = lax.dot_general(d_vals, w_in, contract, preferred_element_type=jnp.float32).astype(jnp.bfloat16)
        normed = rows_of(normed_all, batch_slot, row_start, chunk_len)
        row_part = jnp.sum(partial.astype(jnp.float32) * gain_vec * normed, axis=-1)
        stats = jnp.zeros((8, 128), jnp.float32).at[0, :chunk_len].set(row_part)
        aux = rows_of(aux_all, batch_slot, row_start, chunk_len)
        grad_out, incoming_next, gain_part = layer_exchange(
            partial, stats, aux, gain_own[None, :], top_chunk, incoming, tensors, sections, width
        )
        gain_part = gain_part[0]
        previous = lax.dynamic_slice(results, (batch_slot, half_now, 0, 0), (1, 1, chunk_len, width))
        updated = jnp.where(active, grad_out[None, None], previous)
        results = lax.dynamic_update_slice(results, updated, (batch_slot, half_now, 0, 0))
        gain_acc = gain_acc + jnp.where(active, gain_part, 0.0)
        conv_acc = conv_acc + jnp.where(active, conv_part, 0.0)
        tail_carry = jnp.where(active, new_tail, tail_carry)
        incoming = incoming_next
        return (incoming, results, gain_acc, conv_acc, tail_carry)

    initial = (
        jnp.zeros((chunk_len, model_width), jnp.bfloat16),
        jnp.zeros((batches, halves, chunk_len, width), jnp.bfloat16),
        jnp.zeros((width,), jnp.float32),
        jnp.zeros(weights.shape, jnp.float32),
        tail_init,
    )
    last_state = lax.fori_loop(0, total_steps, step_rows, initial)
    own = last_state[1].reshape(batches * seq_len, width)
    gain_hi = last_state[2].astype(jnp.bfloat16)
    gain_lo = (last_state[2] - gain_hi.astype(jnp.float32)).astype(jnp.bfloat16)
    extra = jnp.stack([gain_hi, gain_lo])
    own = jnp.concatenate([own, extra], axis=0)
    copies = jnp.broadcast_to(own, (tensors, *own.shape))
    gathered = lax.all_to_all(copies, "tensor", split_axis=0, concat_axis=2, tiled=True)[0]
    rows = batches * seq_len
    results = gathered[:rows].reshape(batches, seq_len, model_width)
    gain_total = gathered[rows].astype(jnp.float32) + gathered[rows + 1].astype(jnp.float32)
    conv_acc = last_state[3]
    return (results[None], gain_total[None], conv_acc[None])


def solution(mesh):
    placed = (
        P(),
        P(),
        P(),
        P("section", None, None, None),
        P("section", None, None, "tensor"),
        P("section", None),
        P("section", None, "tensor"),
        P("section", None, "tensor"),
        P("section", "tensor", None),
    )
    return jax.shard_map(
        local,
        mesh=mesh,
        in_specs=placed,
        out_specs=(
            P("section", None, None, None),
            P("section", None),
            P("section", None, "tensor"),
        ),
        check_vma=False,
    )
```

```python
import functools

import jax
import jax.numpy as jnp
from jax import lax
from jax.experimental import pallas as pl
from jax.experimental.pallas import tpu as pltpu
from jax.sharding import PartitionSpec as P

EPSILON = 1e-05
MESH = pl.DeviceIdType.MESH
CHUNKS_PER_BATCH = 2


def sent_to_all(x, axis):
    copies = jnp.broadcast_to(x, (lax.axis_size(axis), *x.shape))
    return lax.all_to_all(copies, axis, split_axis=0, concat_axis=0, tiled=True)


def matmul_nt_kernel(n_sec, top_ref, x_ref, w_ref, out_ref):
    lhs = jnp.where(lax.axis_index("section") == n_sec - 1, top_ref[...], x_ref[...])
    product = lax.dot_general(lhs, w_ref[...], (((1,), (1,)), ((), ())), preferred_element_type=jnp.float32)

    @pl.when(pl.program_id(1) == 0)
    def _():
        out_ref[...] = product.astype(out_ref.dtype)

    @pl.when(pl.program_id(1) > 0)
    def _():
        out_ref[...] += product.astype(out_ref.dtype)


def matmul_nt(top, x, w, block_n, block_k, out_dtype, n_sec):
    rows, depth = x.shape
    cols = w.shape[0]
    grid = (cols // block_n, depth // block_k)
    return pl.pallas_call(
        functools.partial(matmul_nt_kernel, n_sec),
        out_shape=jax.ShapeDtypeStruct((rows, cols), out_dtype),
        grid=grid,
        in_specs=[
            pl.BlockSpec((rows, block_k), lambda n, k: (0, k)),
            pl.BlockSpec((rows, block_k), lambda n, k: (0, k)),
            pl.BlockSpec((block_n, block_k), lambda n, k: (n, k)),
        ],
        out_specs=pl.BlockSpec((rows, block_n), lambda n, k: (0, n)),
        compiler_params=pltpu.CompilerParams(
            dimension_semantics=("arbitrary", "arbitrary"), vmem_limit_bytes=16 * 1024 * 1024
        ),
        cost_estimate=pl.CostEstimate(
            flops=2 * rows * cols * depth,
            bytes_accessed=2 * (2 * rows * depth + cols * depth) + rows * cols * jnp.dtype(out_dtype).itemsize,
            transcendentals=0,
        ),
    )(top, x, w)


def layer_exchange_kernel(
    n, n_sec, width, x_ref, s_ref, aux_ref, gain_ref, top_ref, up_ref,
    g_ref, next_ref, gain_out_ref,
    recv, srecv, down, send_sem, recv_sem, ssend_sem, srecv_sem, dsend_sem, drecv_sem,
):
    me = lax.axis_index("tensor")
    sec = lax.axis_index("section")
    barrier = pltpu.get_barrier_semaphore()
    @pl.when(sec < n_sec - 1)
    def _():
        for t in range(n):
            pl.semaphore_signal(barrier, inc=1, device_id=(sec + 1, t), device_id_type=MESH)

    for k in range(1, n):
        pl.semaphore_signal(barrier, inc=1, device_id=(sec, lax.rem(me + k, n)), device_id_type=MESH)

    @pl.when(sec > 0)
    def _():
        pl.semaphore_wait(barrier, 2 * n - 1)

    @pl.when(sec == 0)
    def _():
        pl.semaphore_wait(barrier, n - 1)

    copies = []
    for k in range(1, n):
        peer = lax.rem(me + k, n)
        cols = pl.ds(pl.multiple_of(peer * width, 128), width)
        block = pltpu.make_async_remote_copy(
            src_ref=x_ref.at[:, cols],
            dst_ref=recv.at[me],
            send_sem=send_sem.at[k],
            recv_sem=recv_sem.at[k],
            device_id=(sec, peer),
            device_id_type=MESH,
        )
        block.start()
        stat = pltpu.make_async_remote_copy(
            src_ref=s_ref,
            dst_ref=srecv.at[me],
            send_sem=ssend_sem.at[k],
            recv_sem=srecv_sem.at[k],
            device_id=(sec, peer),
            device_id_type=MESH,
        )
        stat.start()
        copies.append((block, stat))
    for block, stat in copies:
        block.wait()
        stat.wait()
    mine = pl.ds(pl.multiple_of(me * width, 128), width)
    total = x_ref[:, mine].astype(jnp.float32)
    stat_total = s_ref[...]
    for k in range(1, n):
        src = lax.rem(me + n - k, n)
        total = total + recv[src].astype(jnp.float32)
        stat_total = stat_total + srecv[src]
    rows = total.shape[0]
    row_mean = jnp.transpose(stat_total)[:rows, 0:1] * (1.0 / (n * width))
    normed = aux_ref[:, :width]
    inv_rms = aux_ref[:, width : width + 1]
    d_in = inv_rms * (total * gain_ref[...] - normed * row_mean)
    upstream = jnp.where(sec == n_sec - 1, top_ref[:, mine], up_ref[:, mine])
    result = (upstream.astype(jnp.float32) + d_in).astype(g_ref.dtype)
    g_ref[...] = result
    gain_out_ref[...] = jnp.sum(total * normed, axis=0, keepdims=True)

    @pl.when(sec > 0)
    def _():
        sends = []
        for t in range(n):
            copy = pltpu.make_async_remote_copy(
                src_ref=g_ref,
                dst_ref=down.at[:, mine],
                send_sem=dsend_sem.at[t],
                recv_sem=drecv_sem.at[me],
                device_id=(sec - 1, t),
                device_id_type=MESH,
            )
            copy.start()
            sends.append(copy)
        for copy in sends:
            copy.wait_send()

    @pl.when(sec < n_sec - 1)
    def _():
        for src in range(n):
            pltpu.make_async_remote_copy(
                src_ref=g_ref,
                dst_ref=down.at[:, pl.ds(src * width, width)],
                send_sem=dsend_sem.at[src],
                recv_sem=drecv_sem.at[src],
                device_id=(sec + 1, src),
                device_id_type=MESH,
            ).wait_recv()
        next_ref[...] = down[...]

    @pl.when(sec == n_sec - 1)
    def _():
        next_ref[...] = jnp.zeros_like(next_ref)


def layer_exchange(partial, stats, aux, gain_own, top, upstream, n, n_sec, width):
    rows = partial.shape[0]
    vmem = pl.BlockSpec(memory_space=pltpu.VMEM)
    return pl.pallas_call(
        functools.partial(layer_exchange_kernel, n, n_sec, width),
        out_shape=(
            jax.ShapeDtypeStruct((rows, width), jnp.bfloat16),
            jax.ShapeDtypeStruct((rows, n * width), jnp.bfloat16),
            jax.ShapeDtypeStruct((1, width), jnp.float32),
        ),
        in_specs=[vmem] * 6,
        out_specs=(vmem, vmem, vmem),
        scratch_shapes=[
            pltpu.VMEM((n, rows, width), partial.dtype),
            pltpu.VMEM((n, *stats.shape), jnp.float32),
            pltpu.VMEM((rows, n * width), jnp.bfloat16),
            pltpu.SemaphoreType.DMA((n,)),
            pltpu.SemaphoreType.DMA((n,)),
            pltpu.SemaphoreType.DMA((n,)),
            pltpu.SemaphoreType.DMA((n,)),
            pltpu.SemaphoreType.DMA((n,)),
            pltpu.SemaphoreType.DMA((n,)),
        ],
        compiler_params=pltpu.CompilerParams(
            collective_id=2, has_side_effects=True, vmem_limit_bytes=16 * 1024 * 1024
        ),
    )(partial, stats, aux, gain_own, top, upstream)


def conv_block(weights, ext_vals, tail_rows, d_act):
    kernel_width = weights.shape[0]
    length = d_act.shape[0]
    pre_act = jnp.zeros_like(d_act)
    for lag_idx in range(kernel_width):
        start = kernel_width - 1 - lag_idx
        pre_act = pre_act + weights[lag_idx] * ext_vals[start : start + length]
    gate_sig = jax.nn.sigmoid(pre_act)
    d_pre = d_act * gate_sig * (1.0 + pre_act * (1.0 - gate_sig))
    padded_back = jnp.concatenate([d_pre, tail_rows], axis=0)
    d_vals = jnp.zeros_like(d_pre)
    for lag_idx in range(kernel_width):
        d_vals = d_vals + weights[lag_idx] * padded_back[lag_idx : lag_idx + length]
    lag_grads = jnp.stack(
        [
            jnp.sum(
                d_pre * ext_vals[kernel_width - 1 - lag_idx : kernel_width - 1 - lag_idx + length],
                axis=0,
            )
            for lag_idx in range(kernel_width)
        ]
    )
    return (d_vals.astype(jnp.bfloat16), lag_grads, d_pre[: kernel_width - 1])


def local(dy_top, loss_mask, counts, layer_in, conv_in, norm_gain, conv_weight, in_proj, out_proj):
    sections = lax.axis_size("section")
    tensors = lax.axis_size("tensor")
    section_idx = lax.axis_index("section")
    tensor_idx = lax.axis_index("tensor")
    batches, seq_len, model_width = dy_top.shape
    width = model_width // tensors
    gain_vec = norm_gain[0]
    weights = conv_weight[0]
    kernel_width = weights.shape[0]
    local_channels = weights.shape[1]
    w_in = in_proj[0]
    w_out = out_proj[0]
    conv_padded = jnp.pad(conv_in[0], ((0, 0), (kernel_width - 1, 0), (0, 0)))
    positions = jnp.arange(seq_len, dtype=jnp.int32)
    keep_mask = (loss_mask == 1) & (positions[None, :] < counts[:, None])
    top_grads = jnp.where(keep_mask[:, :, None], dy_top, jnp.zeros_like(dy_top))
    is_last = section_idx == sections - 1
    contract = (((1,), (1,)), ((), ()))

    values = layer_in[0].astype(jnp.float32)
    inv_rms_all = lax.rsqrt(jnp.mean(values * values, axis=-1, keepdims=True) + EPSILON)
    normed_all = values * inv_rms_all
    gain_own = lax.dynamic_slice(gain_vec, (tensor_idx * width,), (width,))
    normed_own_all = lax.dynamic_slice(normed_all, (0, 0, tensor_idx * width), (batches, seq_len, width))
    aux_all = jnp.concatenate(
        [normed_own_all, jnp.broadcast_to(inv_rms_all, (batches, seq_len, 128))], axis=-1
    )

    halves = CHUNKS_PER_BATCH
    chunk_len = seq_len // halves
    n_chunks = batches * halves
    total_steps = sections + n_chunks - 1

    def pick_block(step_idx):
        block_raw = step_idx - (sections - 1 - section_idx)
        active = (block_raw >= 0) & (block_raw < n_chunks)
        block_now = jnp.clip(block_raw, 0, n_chunks - 1)
        within = lax.rem(block_now, halves)
        return (block_now // halves, halves - 1 - within, within > 0, active)

    def rows_of(array, batch_slot, first_row, row_count):
        return lax.dynamic_slice(array, (batch_slot, first_row, 0), (1, row_count, array.shape[2]))[0]

    tail_init = jnp.zeros((kernel_width - 1, local_channels), jnp.float32)

    def step_rows(step_idx, loop_state):
        incoming, results, gain_acc, conv_acc, tail_carry = loop_state
        batch_slot, half_now, join_now, active = pick_block(step_idx)
        row_start = half_now * chunk_len
        top_chunk = rows_of(top_grads, batch_slot, row_start, chunk_len)
        d_act = matmul_nt(top_chunk, incoming, w_out, w_out.shape[0], 4096, jnp.float32, sections)
        ext_vals = lax.dynamic_slice(
            conv_padded, (batch_slot, row_start, 0), (1, chunk_len + kernel_width - 1, local_channels)
        )[0].astype(jnp.float32)
        tail_rows = jnp.where(join_now, tail_carry, 0.0)
        d_vals, conv_part, new_tail = conv_block(weights, ext_vals, tail_rows, d_act)
        partial = lax.dot_general(d_vals, w_in, contract, preferred_element_type=jnp.float32).astype(jnp.bfloat16)
        normed = rows_of(normed_all, batch_slot, row_start, chunk_len)
        row_part = jnp.sum(partial.astype(jnp.float32) * gain_vec * normed, axis=-1)
        stats = jnp.zeros((8, 128), jnp.float32).at[0, :chunk_len].set(row_part)
        aux = rows_of(aux_all, batch_slot, row_start, chunk_len)
        grad_out, incoming_next, gain_part = layer_exchange(
            partial, stats, aux, gain_own[None, :], top_chunk, incoming, tensors, sections, width
        )
        gain_part = gain_part[0]
        previous = lax.dynamic_slice(results, (batch_slot, half_now, 0, 0), (1, 1, chunk_len, width))
        updated = jnp.where(active, grad_out[None, None], previous)
        results = lax.dynamic_update_slice(results, updated, (batch_slot, half_now, 0, 0))
        gain_acc = gain_acc + jnp.where(active, gain_part, 0.0)
        conv_acc = conv_acc + jnp.where(active, conv_part, 0.0)
        tail_carry = jnp.where(active, new_tail, tail_carry)
        incoming = incoming_next
        return (incoming, results, gain_acc, conv_acc, tail_carry)

    initial = (
        jnp.zeros((chunk_len, model_width), jnp.bfloat16),
        jnp.zeros((batches, halves, chunk_len, width), jnp.bfloat16),
        jnp.zeros((width,), jnp.float32),
        jnp.zeros(weights.shape, jnp.float32),
        tail_init,
    )
    last_state = lax.fori_loop(0, total_steps, step_rows, initial)
    own = last_state[1].reshape(batches * seq_len, width)
    gain_hi = last_state[2].astype(jnp.bfloat16)
    gain_lo = (last_state[2] - gain_hi.astype(jnp.float32)).astype(jnp.bfloat16)
    extra = jnp.stack([gain_hi, gain_lo])
    own = jnp.concatenate([own, extra], axis=0)
    copies = jnp.broadcast_to(own, (tensors, *own.shape))
    gathered = lax.all_to_all(copies, "tensor", split_axis=0, concat_axis=2, tiled=True)[0]
    rows = batches * seq_len
    results = gathered[:rows].reshape(batches, seq_len, model_width)
    gain_total = gathered[rows].astype(jnp.float32) + gathered[rows + 1].astype(jnp.float32)
    conv_acc = last_state[3]
    return (results[None], gain_total[None], conv_acc[None])


def solution(mesh):
    placed = (
        P(),
        P(),
        P(),
        P("section", None, None, None),
        P("section", None, None, "tensor"),
        P("section", None),
        P("section", None, "tensor"),
        P("section", None, "tensor"),
        P("section", "tensor", None),
    )
    return jax.shard_map(
        local,
        mesh=mesh,
        in_specs=placed,
        out_specs=(
            P("section", None, None, None),
            P("section", None),
            P("section", None, "tensor"),
        ),
        check_vma=False,
    )
```
